512 devices in a mesh: req: 64 (over z, y), hid: 8 (over x, core).
Axes of the slice: x: 4, y: 4, z: 16, core: 2. Of those that a mesh axis runs over, the one named last changes fastest.
Arguments:
- resid: bfloat16 [8192, 1024], P('req'), may hold values from -6 to 6
- attn_gain: float32 [1024], replicated, may hold values from 0.25 to 1.75
- w_query: bfloat16 [1024, 1024], P(None, 'hid'), may hold values from -4 to 4
- w_key: bfloat16 [1024, 1024], P(None, 'hid'), may hold values from -1 to 1
- w_value: bfloat16 [1024, 1024], P(None, 'hid'), may hold values from -0.1875 to 0.1875
- w_attn_out: bfloat16 [1024, 1024], P('hid'), may hold values from -0.1875 to 0.1875
- cache: bfloat16 [2048, 2, 16, 1024], P('req', None, None, 'hid'), may hold values from -48 to 48
- cache_lens: int32 [2048], P('req'), may hold values from 1 to 16
- seg_ids: int32 [64, 96], P('req'), may hold values from 0 to 3, never falling along the last dimension, each value on 1 to 48 neighbouring positions
- ffn_gain: float32 [1024], replicated, may hold values from 0.25 to 1.75
- router: bfloat16 [1024, 16], replicated, may hold values from -0.078125 to 0.078125
- routes: int32 [8192, 2], P('req'), may hold values from 0 to 15, all different within a row; in each aligned block of 16 rows (0 to 15, 16 to 31, ...) at most 3 rows name the same one
- w_in: bfloat16 [2, 1024, 45056], P(None, None, ('req', 'hid')), may hold values from -0.1875 to 0.1875
- w_out: bfloat16 [45056, 1024], P('req'), may hold values from -0.109375 to 0.109375
Outputs:
- layer_out: bfloat16 [8192, 1024], P(('req', 'hid'))
The draws below stay inside these ranges and needn't reach their ends.
Inputs may be any that keep to these rules, and one draw needn't show every extreme that they name: `routes`: in every aligned block of 16 rows no expert is named more than 3 times, so no assignment is dropped.
All inputs are finite; a program needn't handle non-finite values.
Results may differ from the reference program's by a relative error of at most 0.012.
The reference program's roundings to bfloat16 on the way (of `normed`, `weights`, `context`, `ffn_in`, `hidden` and `part`) count: a program that leaves them out, or rounds other values in their place, can miss the bound.
Values may be sent and summed in bfloat16 or wider, within the bound.
No kernel may reach another device: no remote copies, remote signals or barrier semaphores. Data moves between devices by JAX's collectives and lax.ppermute only.
A program may use at most 64 MiB of HBM per device.

```python
import math
import jax
import jax.numpy as jnp
import numpy as np
from jax import lax

D = 1024
HEADS = 16
HDIM = 64
EXPERTS = 16
FF = 2816
PACK = 96
DEC = 32
CACHE = 16
PROMPTS = 4
GROUPS = 64
TOK_DEV = 128
TOKENS = 8192
DECODES = 2048
BLOCK = 16
CAP = 3
REPL = 4


def query_key_pair(key):
    shape = (D, HEADS * HDIM)
    base = jnp.clip(jax.random.normal(jax.random.fold_in(key, 11), shape, jnp.float32), -6.0, 6.0) * D ** (-0.5)
    other = jnp.clip(jax.random.normal(jax.random.fold_in(key, 12), shape, jnp.float32), -6.0, 6.0) * D ** (-0.5)
    return (base, other)


def draw_w_query(key, part):
    base, other = query_key_pair(key)
    return other.astype(jnp.bfloat16)


def draw_w_key(key, part):
    base, other = query_key_pair(key)
    return base.astype(jnp.bfloat16)


def draw_cache(key, part):
    shape = (DECODES, 2, CACHE, HEADS * HDIM)
    values = jnp.clip(jax.random.normal(jax.random.fold_in(key, 21), shape, jnp.float32), -6.0, 6.0)
    return values.astype(jnp.bfloat16)


def set_ends(drawn, key, smallest, top_value):
    index_at = [jax.random.randint(jax.random.fold_in(key, axis), (), 0, length) for axis, length in enumerate(drawn.shape)]
    main_axis = drawn.shape.index(max(drawn.shape))
    neighbour = index_at[:main_axis] + [(index_at[main_axis] + 1) % drawn.shape[main_axis]] + index_at[main_axis + 1:]
    return drawn.at[tuple(index_at)].set(smallest).at[tuple(neighbour)].set(top_value)


def block_scale(stream_key, shape, shards, low, largest):
    factor_of = 1.0
    for dim, parts in shards:
        steps = jax.random.uniform(jax.random.fold_in(jax.random.fold_in(stream_key, 6), dim), (parts,), jnp.float32, low / len(shards), largest / len(shards))
        factor_of = factor_of * jnp.repeat(jnp.exp(steps), shape[dim] // parts).reshape((-1,) + (1,) * (len(shape) - 1 - dim))
    return factor_of


def profile(number_of, total, limit, slope):
    portions = [(1 << 20) // math.isqrt(grade ** slope) + 1 for grade in range(2, number_of + 1)]
    spare, given = total - limit - (number_of - 1), [1] * (number_of - 1)
    while spare > 0:
        free = [i for i in range(number_of - 1) if given[i] < limit]
        mass, left = sum([portions[i] for i in free]), spare
        for i in free:
            extra = min(limit - given[i], max(1, left * portions[i] // mass), spare)
            given[i] = given[i] + extra
            spare = spare - extra
    return np.array([limit] + given)


def uneven(stream_key, count, total, most, skew):
    if count == 2:
        one = jax.random.randint(stream_key, (), max(1, total - most), min(most, total - 1) + 1)
        return jnp.stack([one, total - one])
    sizes = jnp.asarray(profile(count, total, most, skew), jnp.int32)
    twos = (count - 1) // 2
    source_of, taker = sizes[1:1 + 2 * twos:2], sizes[2:2 + 2 * twos:2]
    room = jnp.minimum(source_of - 1, most - taker)
    shifted = jax.random.randint(jax.random.fold_in(stream_key, 1), (twos,), 0, 1 << 20) % (room + 1)
    sizes = sizes.at[1:1 + 2 * twos:2].set(source_of - shifted).at[2:2 + 2 * twos:2].set(taker + shifted)
    return sizes[jax.random.permutation(jax.random.fold_in(stream_key, 2), count)]


def deal_out(key, own, number, rows, count, top, bound, slope):
    order = jax.random.permutation(key, count)
    heavy_load, ordinary = shares(count, rows * top, bound, slope, True), shares(count, rows * top, bound, slope, False)
    places = jnp.arange(count)

    def named(sizes, turn):
        used = int((sizes > 0).sum())
        fixed = max(1, used // 4)
        passed = fixed + (places - fixed + turn * (used - fixed)) % max(1, count - fixed)
        return jnp.zeros((count,), jnp.int32).at[order[jnp.where(places < fixed, places, passed)]].set(jnp.asarray(sizes, jnp.int32))

    sizes = jnp.where(number % 4 == 0, named(heavy_load, number // 4), named(ordinary, number - number // 4 - 1))
    mixed = jax.random.permutation(jax.random.fold_in(own, 3), count)
    donor, receiver = mixed[0:count // 2 * 2:2], mixed[1:count // 2 * 2:2]
    room = jnp.minimum(sizes[donor] - 1, bound - sizes[receiver]) // 2
    room = jnp.where((donor == order[0]) | (receiver == order[0]) | (sizes[receiver] == 0), 0, jnp.maximum(room, 0))
    passed = jax.random.randint(jax.random.fold_in(own, 4), (count // 2,), 0, 1 << 20) % (room + 1)
    sizes = sizes.at[donor].add(-passed).at[receiver].add(passed)
    items = jnp.searchsorted(jnp.cumsum(sizes), jnp.arange(rows * top), side="right").astype(jnp.int32)
    table = items.reshape(top, rows).T
    table = table[jax.random.permutation(jax.random.fold_in(own, 1), rows)]
    turn = jax.random.randint(jax.random.fold_in(own, 2), (rows, 1), 0, top)
    return jnp.take_along_axis(table, (jnp.arange(top)[None, :] + turn) % top, axis=1)


def shares(count, total, bound, skew, full):
    weights = [(1 << 20) // math.isqrt(grade ** skew) + 1 for grade in range(1, count + 1)]
    largest = bound if full else min(bound, max(-(-total // count), total * weights[0] // sum(weights)))
    least = 1 if total - largest >= count - 1 else 0
    counts, rest = [largest] + [least] * (count - 1), total - largest - least * (count - 1)
    while rest > 0:
        movable = [i for i in range(1, count) if counts[i] < largest] or [i for i in range(1, count) if counts[i] < bound]
        whole, budget = sum([weights[i] for i in movable]), rest
        for i in movable:
            addition = min(bound - counts[i], max(1, budget * weights[i] // whole), rest)
            counts[i] = counts[i] + addition
            rest = rest - addition
    return np.array(counts)


def centred(rng, dims, spread, most, cuts=(), held_as=jnp.bfloat16):
    values = jax.random.normal(rng, dims, jnp.float32) * spread
    if len(cuts) > 0:
        values = block_scale(rng, dims, cuts, -0.22, 0.18) * values
    return jnp.clip(values, min=-most, max=most).astype(held_as)


def setup_inputs(seed: int = 0) -> dict:
    splits = jax.random.split(jax.random.key(seed), 15)
    resid = centred(splits[0], (TOKENS, D), 1.0, 6.0, ((0, 64),))
    attn_gain = jnp.clip(1.0 + 0.15 * jax.random.normal(splits[1], (D,), jnp.float32), 0.25, 1.75)
    w_query = draw_w_query(jax.random.fold_in(splits[14], 71), 0)
    w_key = draw_w_key(jax.random.fold_in(splits[14], 71), 0)
    w_value = centred(splits[4], (D, HEADS * HDIM), D ** -0.5, 0.1875, ((1, 8),))
    w_attn_out = centred(splits[5], (HEADS * HDIM, D), (HEADS * HDIM) ** -0.5, 0.1875, ((0, 8),))
    cache = draw_cache(jax.random.fold_in(splits[14], 71), 0)
    cache_lens = set_ends(jax.random.randint(splits[7], (DECODES,), 1, CACHE + 1), jax.random.fold_in(splits[7], 1), 1, CACHE).astype(jnp.int32)
    seg_ids = jax.vmap(lambda own: jnp.searchsorted(jnp.cumsum(uneven(own, PROMPTS, PACK, PACK // 2, 2)), jnp.arange(PACK), side="right"))(jax.random.split(splits[8], GROUPS)).reshape((GROUPS, PACK)).astype(jnp.int32)
    ffn_gain = jnp.clip(1.0 + 0.15 * jax.random.normal(splits[9], (D,), jnp.float32), 0.25, 1.75)
    router = centred(splits[10], (D, EXPERTS), (6 * D) ** -0.5, 0.078125)
    routes_keys = jax.random.split(jax.random.fold_in(splits[11], 1), TOKENS // BLOCK)
    routes_turns = jax.random.permutation(jax.random.fold_in(splits[11], 3), TOKENS // BLOCK)
    routes = jax.vmap(lambda own, number: deal_out(jax.random.fold_in(splits[11], 2), own, number, BLOCK, EXPERTS, 2, CAP, 2))(routes_keys, routes_turns).reshape((TOKENS, 2))
    w_in = centred(splits[12], (2, D, EXPERTS * FF), D ** -0.5, 0.1875, ((2, 512),))
    w_out = centred(splits[13], (EXPERTS * FF, D), FF ** -0.5, 0.109375, ((0, 64),))
    return dict(resid=resid, attn_gain=attn_gain, w_query=w_query, w_key=w_key, w_value=w_value, w_attn_out=w_attn_out, cache=cache, cache_lens=cache_lens, seg_ids=seg_ids, ffn_gain=ffn_gain, router=router, routes=routes, w_in=w_in, w_out=w_out)


EPS = 1e-06

def rms_scale(values, gain):
    values = values.astype(jnp.float32)
    inverse = lax.rsqrt(lax.optimization_barrier(jnp.mean(values * values, axis=-1, keepdims=True)) + EPS)
    return (values * inverse * gain.astype(jnp.float32)).astype(jnp.bfloat16)

def softmax_bf16(scores, allowed):
    scores = jnp.where(allowed, scores, -jnp.inf)
    highest = lax.optimization_barrier(jnp.max(scores, axis=-1, keepdims=True))
    weights = jnp.exp(scores - highest)
    return (weights / lax.optimization_barrier(jnp.sum(weights, axis=-1, keepdims=True))).astype(jnp.bfloat16)

def attend(normed, w_query, w_key, w_value, segments, cached, lengths):
    heads = w_query.shape[1] // HDIM
    scale = HDIM ** (-0.5)
    total = normed.shape[0]
    packed = segments.shape[0]
    decoded = total - packed
    slots = cached.shape[2]
    query = jnp.dot(normed, w_query, preferred_element_type=jnp.float32).astype(jnp.bfloat16)
    keys = jnp.dot(normed, w_key, preferred_element_type=jnp.float32).astype(jnp.bfloat16)
    values = jnp.dot(normed, w_value, preferred_element_type=jnp.float32).astype(jnp.bfloat16)
    query = query.reshape(total, heads, HDIM).astype(jnp.float32)
    keys = keys.reshape(total, heads, HDIM).astype(jnp.float32)
    values = values.reshape(total, heads, HDIM).astype(jnp.float32)
    positions = jnp.arange(packed)
    allowed = (positions[None, :] <= positions[:, None]) & (segments[None, :] == segments[:, None])
    scores = jnp.einsum('qhd,khd->hqk', query[:packed], keys[:packed]) * scale
    weights = softmax_bf16(scores, allowed[None])
    prompt_ctx = jnp.einsum('hqk,khd->qhd', weights.astype(jnp.float32), values[:packed])
    stored = cached.astype(jnp.float32).reshape(decoded, 2, slots, heads, HDIM)
    cached_scores = jnp.einsum('uhd,uchd->uhc', query[packed:], stored[:, 0]) * scale
    own_scores = lax.optimization_barrier(jnp.sum(query[packed:] * keys[packed:], axis=-1, keepdims=True)) * scale
    valid = jnp.arange(slots)[None, None, :] < lengths[:, None, None]
    allowed_all = jnp.concatenate([jnp.broadcast_to(valid, cached_scores.shape), jnp.ones(own_scores.shape, dtype=bool)], axis=-1)
    joined = jnp.concatenate([cached_scores, own_scores], axis=-1)
    weights_dec = softmax_bf16(joined, allowed_all).astype(jnp.float32)
    decode_ctx = jnp.einsum('uhc,uchd->uhd', weights_dec[..., :slots], stored[:, 1]) + weights_dec[..., slots:] * values[packed:]
    context = jnp.concatenate([prompt_ctx, decode_ctx], axis=0)
    return context.reshape(total, heads * HDIM).astype(jnp.bfloat16)

def reference(resid, attn_gain, w_query, w_key, w_value, w_attn_out, cache, cache_lens, seg_ids, ffn_gain, router, routes, w_in, w_out):

    def one_group(operands):
        group_rows, segments, cached, lengths = operands
        normed = rms_scale(group_rows, attn_gain)
        context = attend(normed, w_query, w_key, w_value, segments, cached, lengths)
        mixed = jnp.dot(context, w_attn_out, preferred_element_type=jnp.float32)
        return group_rows.astype(jnp.float32) + mixed
    after = lax.map(one_group, (resid.reshape(GROUPS, TOK_DEV, D), seg_ids, cache.reshape(GROUPS, DEC, 2, CACHE, HEADS * HDIM), cache_lens.reshape(GROUPS, DEC)))
    after = after.reshape(TOKENS, D)
    ffn_in = rms_scale(after, ffn_gain)
    logits = jnp.dot(ffn_in, router, preferred_element_type=jnp.float32)
    gates = jax.nn.sigmoid(jnp.take_along_axis(logits, routes, axis=1))
    blocks = TOKENS // BLOCK
    chosen = routes.reshape(blocks, BLOCK * 2)
    onehot = (chosen[:, :, None] == jnp.arange(EXPERTS, dtype=jnp.int32)[None, None, :]).astype(jnp.int32)
    earlier = jnp.cumsum(onehot, axis=1) - onehot
    slot = lax.optimization_barrier(jnp.sum(earlier * onehot, axis=2)).astype(jnp.int32)
    token_row = (jnp.arange(blocks, dtype=jnp.int32)[:, None] * BLOCK + jnp.arange(BLOCK * 2, dtype=jnp.int32)[None, :] // 2).astype(jnp.int32)
    block_index = jnp.broadcast_to(jnp.arange(blocks, dtype=jnp.int32)[:, None], chosen.shape)
    table = jnp.zeros((blocks, EXPERTS, CAP), jnp.int32).at[block_index, chosen, slot].set(token_row)
    weight_table = jnp.zeros((blocks, EXPERTS, CAP), jnp.float32).at[block_index, chosen, slot].set(gates.reshape(blocks, BLOCK * 2))
    quarter = FF // REPL

    def one_expert(total, expert):
        picked = table[:, expert, :].reshape(-1)
        weight = weight_table[:, expert, :].reshape(-1)
        chosen_rows = ffn_in[picked]
        start = (expert * FF).astype(jnp.int32)
        gate_w = lax.dynamic_slice_in_dim(w_in[0], start, FF, 1)
        up_w = lax.dynamic_slice_in_dim(w_in[1], start, FF, 1)
        down_w = lax.dynamic_slice_in_dim(w_out, start, FF, 0)
        gate_val = jnp.dot(chosen_rows, gate_w, preferred_element_type=jnp.float32)
        up_val = jnp.dot(chosen_rows, up_w, preferred_element_type=jnp.float32)
        hidden = (jax.nn.gelu(gate_val, approximate=True) * up_val).astype(jnp.bfloat16)
        result = jnp.zeros((picked.shape[0], D), jnp.float32)
        for index in range(REPL):
            partial_sum = jnp.dot(hidden[:, index * quarter:(index + 1) * quarter], down_w[index * quarter:(index + 1) * quarter], preferred_element_type=jnp.float32).astype(jnp.bfloat16)
            partial_sum = lax.optimization_barrier(partial_sum)
            result = result + partial_sum.astype(jnp.float32)
        total = total.at[picked].add(weight[:, None] * result)
        return (total, None)
    ffn_total, _ = lax.scan(one_expert, jnp.zeros((TOKENS, D), jnp.float32), jnp.arange(EXPERTS, dtype=jnp.int32))
    return (after + ffn_total).astype(jnp.bfloat16)
```

```python
import jax
import jax.numpy as jnp
from jax import lax
from jax.experimental import pallas as pl
from jax.experimental.pallas import tpu as pltpu
from jax.sharding import Mesh
from jax.sharding import PartitionSpec as P

HDIM = 64
EPS = 1e-06
BF = jnp.bfloat16
F32 = jnp.float32
LANES = 128


def dot(a, b):
    return jnp.dot(a, b, preferred_element_type=F32)


def dot_nt(a, b):
    return lax.dot_general(a, b, (((1,), (1,)), ((), ())), preferred_element_type=F32)


def dot_tn(a, b):
    return lax.dot_general(a, b, (((0,), (0,)), ((), ())), preferred_element_type=F32)


def iota(shape, dim):
    return lax.broadcasted_iota(jnp.int32, shape, dim)


def to_column(row, size):
    diagonal = iota((size, size), 0) == iota((size, size), 1)
    return jnp.sum(jnp.where(diagonal, jnp.broadcast_to(row, (size, size)), 0), axis=1, keepdims=True)


def attention_kernel(
    resid_ref, gain_ref, wq_ref, wk_ref, wv_ref, wo_ref, cache_ref, lens_ref, seg_ref, out_ref, seg_row
):
    total = resid_ref.shape[0]
    packed = seg_ref.shape[1]
    decoded, _, slots, width = cache_ref.shape
    heads = width // HDIM
    scale = HDIM ** (-0.5)
    x = resid_ref[...].astype(F32)
    inverse = lax.rsqrt(jnp.mean(x * x, axis=-1, keepdims=True) + EPS)
    normed = (x * inverse * gain_ref[...]).astype(BF)
    query = dot(normed, wq_ref[...]).astype(BF)
    keys = dot(normed, wk_ref[...]).astype(BF)
    values = dot(normed, wv_ref[...]).astype(BF)

    seg_row[...] = iota((1, total), 1) + (1 << 20)
    seg_row[:, :packed] = seg_ref[...]
    segments = seg_row[...]
    allowed = (iota((total, total), 1) <= iota((total, total), 0)) & (to_column(segments, total) == segments)
    lengths = to_column(lens_ref[...], decoded)
    slot_at = iota((decoded, decoded * slots), 1)
    own_cache = (slot_at // slots == iota((decoded, decoded * slots), 0)) & (slot_at % slots < lengths)

    cached_keys = cache_ref[:, 0].reshape(decoded * slots, width)
    cached_values = cache_ref[:, 1].reshape(decoded * slots, width)
    lane_head = iota((total, width), 1) // HDIM
    context = jnp.zeros((total, width), F32)
    for head in range(heads):
        mine = lane_head == head
        head_query = jnp.where(mine, query, jnp.zeros_like(query))
        scores = jnp.where(allowed, dot_nt(head_query, keys) * scale, -jnp.inf)
        highest = jnp.max(scores, axis=-1, keepdims=True)
        cached = jnp.where(own_cache, dot_nt(head_query[packed:], cached_keys) * scale, -jnp.inf)
        top_dec = jnp.maximum(highest[packed:], jnp.max(cached, axis=-1, keepdims=True))
        highest = jnp.concatenate([highest[:packed], top_dec], axis=0)
        weights = jnp.exp(scores - highest)
        weights_cache = jnp.exp(cached - top_dec)
        norm = jnp.sum(weights, axis=-1, keepdims=True)
        norm_dec = norm[packed:] + jnp.sum(weights_cache, axis=-1, keepdims=True)
        norm = jnp.concatenate([norm[:packed], norm_dec], axis=0)
        part = dot((weights / norm).astype(BF), values)
        part_cache = dot((weights_cache / norm_dec).astype(BF), cached_values)
        part = jnp.concatenate([part[:packed], part[packed:] + part_cache], axis=0)
        context = jnp.where(mine, part, context)
    out_ref[...] = dot(context.astype(BF), wo_ref[...]).astype(out_ref.dtype)


def own_routes(routes_ref, which, index, block):
    lane = iota((1, LANES), 1)
    row = pltpu.roll(routes_ref[pl.ds(which, 1), :], (LANES - index * block) % LANES, 1)
    size = block
    while size < LANES:
        row = jnp.where(lane < size, row, pltpu.roll(row, size, 1))
        size *= 2
    return row


def placement(row, columns, block, capacity, chunks):
    token = iota((block, LANES), 1) % block
    before = iota((block, LANES), 0) < token
    slot = jnp.zeros((1, LANES), jnp.int32)
    for column in columns:
        slot = slot + jnp.sum(((column == row) & before).astype(jnp.int32), axis=0, keepdims=True)
    target = row * capacity + slot
    return target


def slot_rows(rows, capacity, chunks):
    at = iota((rows, LANES), 0)
    expert = at // (chunks * capacity)
    rest = at - expert * (chunks * capacity)
    chunk = rest // capacity
    return expert * capacity + rest - chunk * capacity, chunk


def route_columns(rows, block):
    size = (block, LANES)
    diagonal = iota(size, 0) == iota(size, 1)
    return [
        jnp.sum(jnp.where(diagonal, jnp.broadcast_to(row, size), 0), axis=1, keepdims=True) for row in rows
    ]


def dispatch_kernel(
    index_ref, parts_ref, resid_ref, gain_ref, router_ref, routes_ref, out_ref, after_ref, gates_ref, target_ref
):
    sources, block, width = parts_ref.shape
    experts = router_ref.shape[0]
    chunks = width // LANES
    capacity = out_ref.shape[0] // (experts * chunks)
    index = index_ref[0]
    start = pl.multiple_of(index * block, block)
    mixed = parts_ref[0].astype(F32)
    for source in range(1, sources):
        mixed = mixed + parts_ref[source].astype(F32)
    after = resid_ref[pl.ds(start, block), :].astype(F32) + mixed
    after_ref[...] = after
    inverse = lax.rsqrt(jnp.mean(after * after, axis=-1, keepdims=True) + EPS)
    ffn_in = (after * inverse * gain_ref[...]).astype(BF)
    rows = [own_routes(routes_ref, which, index, block) for which in range(2)]
    columns = route_columns(rows, block)
    targets = [placement(row, columns, block, capacity, chunks) for row in rows]
    wanted, chunk = slot_rows(out_ref.shape[0], capacity, chunks)
    same = chunk == iota(chunk.shape, 1) // block
    chosen = same & ((wanted == targets[0]) | (wanted == targets[1]))
    stacked = jnp.concatenate([ffn_in[:, at * LANES : (at + 1) * LANES] for at in range(chunks)], axis=0)
    out_ref[...] = dot(jnp.where(chosen, 1.0, 0.0).astype(BF), stacked).astype(BF)
    logits = dot_nt(ffn_in, router_ref[...])
    expert_at = iota((block, experts), 1)
    for which in range(2):
        picked = jnp.sum(jnp.where(expert_at == columns[which], logits, 0.0), axis=1, keepdims=True)
        gates_ref[which] = jnp.broadcast_to(jax.nn.sigmoid(picked), (block, LANES))
        target_ref[pl.ds(which, 1), :] = targets[which]


def ffn_kernel(tokens_ref, gate_ref, up_ref, down_ref, out_ref, rows_ref):
    groups, chunk_rows, _ = tokens_ref.shape
    width = rows_ref.shape[1]
    chunks = width // LANES
    each = chunk_rows // chunks
    capacity = 3
    at = iota((chunk_rows, chunk_rows), 0)
    chunk = at // each
    rest = at - chunk * each
    source = rest // capacity
    wanted = source * (chunks * capacity) + chunk * capacity + rest - source * capacity
    order = jnp.where(wanted == iota((chunk_rows, chunk_rows), 1), 1.0, 0.0).astype(BF)
    for group in range(groups):
        unpacked = dot(order, tokens_ref[group]).astype(BF)
        for at in range(chunks):
            rows_ref[group * each : (group + 1) * each, at * LANES : (at + 1) * LANES] = unpacked[
                at * each : (at + 1) * each
            ]
    rows = rows_ref[...]
    gate_val = dot_nt(rows, gate_ref[...])
    up_val = dot_nt(rows, up_ref[...])
    hidden = (jax.nn.gelu(gate_val, approximate=True) * up_val).astype(BF)
    parts = dot(hidden, down_ref[...]).astype(BF)
    for group in range(groups):
        mine = parts[group * each : (group + 1) * each]
        stacked = jnp.concatenate([mine[:, at * LANES : (at + 1) * LANES] for at in range(chunks)], axis=0)
        out_ref[group] = dot_tn(order, stacked).astype(BF)


def combine_kernel(experts_ref, after_ref, gates_ref, target_ref, out_ref):
    rows = experts_ref.shape[0]
    block, width = after_ref.shape
    chunks = width // LANES
    capacity = 3
    wanted, chunk = slot_rows(rows, capacity, chunks)
    same = chunk == iota(chunk.shape, 1) // block
    outputs = experts_ref[...]
    picked = []
    for which in range(2):
        chosen = same & (wanted == target_ref[pl.ds(which, 1), :])
        picked.append(dot_tn(jnp.where(chosen, 1.0, 0.0).astype(BF), outputs))
    for at in range(chunks):
        lanes = slice(at * LANES, (at + 1) * LANES)
        mine = slice(at * block, (at + 1) * block)
        total = gates_ref[0] * picked[0][mine] + gates_ref[1] * picked[1][mine]
        out_ref[:, lanes] = (after_ref[:, lanes] + total).astype(BF)


VMEM = pl.BlockSpec(memory_space=pltpu.VMEM)
SMEM = pl.BlockSpec(memory_space=pltpu.SMEM)
PARAMS = pltpu.CompilerParams(vmem_limit_bytes=40 * 1024 * 1024)


def body(
    resid, attn_gain, w_query, w_key, w_value, w_attn_out, cache, cache_lens, seg_ids, ffn_gain, router, routes, w_in, w_out
):
    hid = ("x", "c")
    hid_count = lax.axis_size(hid)
    hid_index = lax.axis_index(hid).astype(jnp.int32).reshape(1)
    group_rows, width = resid.shape
    experts = router.shape[1]
    block = group_rows // hid_count
    capacity = 3
    chunks = width // LANES
    slot_count = experts * chunks * capacity
    split = lax.axis_size("y")
    w_cols = jnp.transpose(w_in, (0, 2, 1))
    w_gate = lax.all_gather(w_cols[0], hid, axis=0, tiled=True)
    w_up = lax.all_gather(w_cols[1], hid, axis=0, tiled=True)

    partial_mix = pl.pallas_call(
        attention_kernel,
        out_shape=jax.ShapeDtypeStruct((group_rows, width), BF),
        in_specs=[VMEM] * 9,
        out_specs=VMEM,
        scratch_shapes=[pltpu.VMEM((1, group_rows), jnp.int32)],
        compiler_params=PARAMS,
        name="attention",
    )(
        resid,
        attn_gain.reshape(1, width),
        w_query,
        w_key,
        w_value,
        w_attn_out,
        cache,
        cache_lens.reshape(1, -1),
        seg_ids,
    )
    parts = lax.all_to_all(partial_mix.reshape(hid_count, block, width), hid, 0, 0, tiled=True)
    outgoing, after, gates, target = pl.pallas_call(
        dispatch_kernel,
        out_shape=(
            jax.ShapeDtypeStruct((slot_count, LANES), BF),
            jax.ShapeDtypeStruct((block, width), F32),
            jax.ShapeDtypeStruct((2, block, LANES), F32),
            jax.ShapeDtypeStruct((2, LANES), jnp.int32),
        ),
        in_specs=[SMEM] + [VMEM] * 5,
        out_specs=(VMEM,) * 4,
        compiler_params=PARAMS,
        name="dispatch",
    )(hid_index, parts, resid, ffn_gain.reshape(1, width), router.T, routes.T)
    arrived = lax.all_to_all(outgoing.reshape(experts, chunks * capacity, LANES), "z", 0, 0, tiled=True)
    tokens = lax.all_gather(arrived.reshape(slot_count, LANES), "y", axis=0)
    projected = pl.pallas_call(
        ffn_kernel,
        out_shape=jax.ShapeDtypeStruct((split, slot_count, LANES), BF),
        in_specs=[VMEM] * 4,
        out_specs=VMEM,
        scratch_shapes=[pltpu.VMEM((split * experts * capacity, width), BF)],
        compiler_params=PARAMS,
        name="ffn",
    )(tokens, w_gate, w_up, w_out)
    quarters = lax.all_to_all(projected, "y", 0, 0, tiled=True)
    summed = jnp.sum(quarters.astype(F32), axis=0).astype(BF)
    returned = lax.all_to_all(summed.reshape(experts, chunks * capacity, LANES), "z", 0, 0, tiled=True)
    return pl.pallas_call(
        combine_kernel,
        out_shape=jax.ShapeDtypeStruct((block, width), BF),
        in_specs=[VMEM] * 4,
        out_specs=VMEM,
        compiler_params=PARAMS,
        name="combine",
    )(returned.reshape(slot_count, LANES), after, gates, target)


def solution(mesh):
    fine = Mesh(mesh.devices.reshape(16, 4, 4, 2), ("z", "y", "x", "c"))
    req = ("z", "y")
    hid = ("x", "c")
    in_specs = (
        P(req, None),
        P(),
        P(None, hid),
        P(None, hid),
        P(None, hid),
        P(hid, None),
        P(req, None, None, hid),
        P(req),
        P(req, None),
        P(),
        P(),
        P(req, None),
        P(None, None, req + hid),
        P(req, None),
    )
    out_specs = P(req + hid, None)
    return jax.shard_map(body, mesh=fine, in_specs=in_specs, out_specs=out_specs, check_vma=False)
```

```python
import functools

import jax
import jax.numpy as jnp
from jax import lax
from jax.experimental import pallas as pl
from jax.experimental.pallas import tpu as pltpu
from jax.sharding import Mesh
from jax.sharding import PartitionSpec as P

HDIM = 64
EPS = 1e-06
BF = jnp.bfloat16
F32 = jnp.float32
LANES = 128
CAPACITY = 3


def dot(a, b):
    return jnp.dot(a, b, preferred_element_type=F32)


def dot_nt(a, b):
    return lax.dot_general(a, b, (((1,), (1,)), ((), ())), preferred_element_type=F32)


def dot_tn(a, b):
    return lax.dot_general(a, b, (((0,), (0,)), ((), ())), preferred_element_type=F32)


def iota(shape, dim):
    return lax.broadcasted_iota(jnp.int32, shape, dim)


def to_column(row, size):
    diagonal = iota((size, size), 0) == iota((size, size), 1)
    return jnp.sum(jnp.where(diagonal, jnp.broadcast_to(row, (size, size)), 0), axis=1, keepdims=True)


def attention_kernel(
    index_ref, resid_hbm, gain_hbm, wq_hbm, wk_hbm, wv_hbm, wo_hbm, cache_hbm, lens_hbm, seg_hbm,
    ffn_gain_hbm, router_hbm, out_ref, own_ref, ffn_gain_ref, router_ref,
    resid_ref, gain_ref, wq_ref, wk_ref, wv_ref, wo_ref, cache_ref, lens_ref, seg_ref, seg_row, sems
):
    sources = (
        resid_hbm, gain_hbm, wq_hbm, wk_hbm, wv_hbm, seg_hbm, lens_hbm, cache_hbm, wo_hbm, ffn_gain_hbm, router_hbm
    )
    targets = (
        resid_ref, gain_ref, wq_ref, wk_ref, wv_ref, seg_ref, lens_ref, cache_ref, wo_ref, ffn_gain_ref, router_ref
    )
    copies = [pltpu.make_async_copy(a, b, sems.at[i]) for i, (a, b) in enumerate(zip(sources, targets))]
    for copy in copies:
        copy.start()
    total = resid_ref.shape[0]
    packed = seg_ref.shape[1]
    decoded, _, slots, width = cache_ref.shape
    heads = width // HDIM
    scale = HDIM ** (-0.5)
    copies[0].wait()
    copies[1].wait()
    x = resid_ref[...].astype(F32)
    inverse = lax.rsqrt(jnp.mean(x * x, axis=-1, keepdims=True) + EPS)
    normed = (x * inverse * gain_ref[...]).astype(BF)
    copies[2].wait()
    query = dot(normed, wq_ref[...]).astype(BF)
    copies[3].wait()
    keys = dot(normed, wk_ref[...]).astype(BF)
    copies[4].wait()
    values = dot(normed, wv_ref[...]).astype(BF)
    copies[5].wait()
    copies[6].wait()
    copies[7].wait()

    seg_row[...] = iota((1, total), 1) + (1 << 20)
    seg_row[:, :packed] = seg_ref[...]
    segments = seg_row[...]
    allowed = (iota((total, total), 1) <= iota((total, total), 0)) & (to_column(segments, total) == segments)
    lengths = to_column(lens_ref[...], decoded)
    slot_at = iota((decoded, decoded * slots), 1)
    own_cache = (slot_at // slots == iota((decoded, decoded * slots), 0)) & (slot_at % slots < lengths)

    cached_keys = cache_ref[:, 0].reshape(decoded * slots, width)
    cached_values = cache_ref[:, 1].reshape(decoded * slots, width)
    lane_head = iota((total, width), 1) // HDIM
    context = jnp.zeros((total, width), F32)
    for head in range(heads):
        mine = lane_head == head
        head_query = jnp.where(mine, query, jnp.zeros_like(query))
        scores = jnp.where(allowed, dot_nt(head_query, keys) * scale, -jnp.inf)
        highest = jnp.max(scores, axis=-1, keepdims=True)
        cached = jnp.where(own_cache, dot_nt(head_query[packed:], cached_keys) * scale, -jnp.inf)
        top_dec = jnp.maximum(highest[packed:], jnp.max(cached, axis=-1, keepdims=True))
        highest = jnp.concatenate([highest[:packed], top_dec], axis=0)
        weights = jnp.exp(scores - highest)
        weights_cache = jnp.exp(cached - top_dec)
        norm = jnp.sum(weights, axis=-1, keepdims=True)
        norm_dec = norm[packed:] + jnp.sum(weights_cache, axis=-1, keepdims=True)
        norm = jnp.concatenate([norm[:packed], norm_dec], axis=0)
        part = dot((weights / norm).astype(BF), values)
        part_cache = dot((weights_cache / norm_dec).astype(BF), cached_values)
        part = jnp.concatenate([part[:packed], part[packed:] + part_cache], axis=0)
        context = jnp.where(mine, part, context)
    copies[8].wait()
    out_ref[...] = dot(context.astype(BF), wo_ref[...]).astype(out_ref.dtype)

    block = own_ref.shape[0]
    index = index_ref[0]
    own_ref[...] = resid_ref[pl.ds(pl.multiple_of(index * block, block), block), :].astype(F32)
    copies[9].wait()
    copies[10].wait()


def own_routes(routes_ref, which, index, block):
    lane = iota((1, LANES), 1)
    row = pltpu.roll(routes_ref[pl.ds(which, 1), :], (LANES - index * block) % LANES, 1)
    size = block
    while size < LANES:
        row = jnp.where(lane < size, row, pltpu.roll(row, size, 1))
        size *= 2
    return row


def placement(row, columns, block, capacity):
    token = iota((block, LANES), 1) % block
    before = iota((block, LANES), 0) < token
    slot = jnp.zeros((1, LANES), jnp.int32)
    for column in columns:
        slot = slot + jnp.sum(((column == row) & before).astype(jnp.int32), axis=0, keepdims=True)
    return row * capacity + slot


def slot_rows(rows, capacity, chunks):
    at = iota((rows, LANES), 0)
    expert = at // (chunks * capacity)
    rest = at - expert * (chunks * capacity)
    chunk = rest // capacity
    return expert * capacity + rest - chunk * capacity, chunk


def route_columns(rows, block):
    size = (block, LANES)
    diagonal = iota(size, 0) == iota(size, 1)
    return [
        jnp.sum(jnp.where(diagonal, jnp.broadcast_to(row, size), 0), axis=1, keepdims=True) for row in rows
    ]


def routing_kernel(index_ref, routes_ref, gain_ref, chosen_ref, select_ref, column_ref):
    block = column_ref.shape[1]
    chunks = gain_ref.shape[1] // LANES
    rows = [own_routes(routes_ref, which, index_ref[0], block) for which in range(2)]
    columns = route_columns(rows, block)
    wanted, chunk = slot_rows(chosen_ref.shape[0], CAPACITY, chunks)
    same = chunk == iota(chunk.shape, 1) // block
    both = None
    for which in range(2):
        target = placement(rows[which], columns, block, CAPACITY)
        here = jnp.where(same & (wanted == target), 1.0, 0.0)
        select_ref[which] = here.astype(BF)
        both = here if both is None else both + here
        column_ref[which] = jnp.broadcast_to(columns[which], (block, LANES))
    chosen_ref[...] = both.astype(BF)


def dispatch_kernel(parts_ref, own_ref, gain_ref, chosen_ref, out_ref, after_ref, ffn_in_ref):
    sources, block, width = parts_ref.shape
    chunks = width // LANES
    mixed = parts_ref[0].astype(F32)
    for source in range(1, sources):
        mixed = mixed + parts_ref[source].astype(F32)
    after = own_ref[...] + mixed
    after_ref[...] = after
    inverse = lax.rsqrt(jnp.mean(after * after, axis=-1, keepdims=True) + EPS)
    ffn_in = (after * inverse * gain_ref[...]).astype(BF)
    ffn_in_ref[...] = ffn_in
    stacked = jnp.concatenate([ffn_in[:, at * LANES : (at + 1) * LANES] for at in range(chunks)], axis=0)
    out_ref[...] = dot(chosen_ref[...], stacked).astype(BF)


def gates_kernel(ffn_in_ref, router_ref, column_ref, gates_ref):
    block = ffn_in_ref.shape[0]
    experts = router_ref.shape[0]
    logits = dot_nt(ffn_in_ref[...], router_ref[...])
    expert_at = iota((block, experts), 1)
    for which in range(2):
        mine = expert_at == column_ref[which][:, :experts]
        picked = jnp.sum(jnp.where(mine, logits, 0.0), axis=1, keepdims=True)
        gates_ref[which] = jnp.broadcast_to(jax.nn.sigmoid(picked), (block, LANES))


def order_kernel(chunks, tokens_ref, order_ref):
    chunk_rows = order_ref.shape[0]
    each = chunk_rows // chunks
    at = iota((chunk_rows, chunk_rows), 0)
    chunk = at // each
    rest = at - chunk * each
    source = rest // CAPACITY
    wanted = source * (chunks * CAPACITY) + chunk * CAPACITY + rest - source * CAPACITY
    order_ref[...] = jnp.where(wanted == iota((chunk_rows, chunk_rows), 1), 1.0, 0.0).astype(BF)


def unpack_kernel(tokens_ref, order_ref, rows_ref):
    groups, chunk_rows, _ = tokens_ref.shape
    chunks = rows_ref.shape[1] // LANES
    each = chunk_rows // chunks
    for group in range(groups):
        unpacked = dot(order_ref[...], tokens_ref[group]).astype(BF)
        for at in range(chunks):
            rows_ref[group * each : (group + 1) * each, at * LANES : (at + 1) * LANES] = unpacked[
                at * each : (at + 1) * each
            ]


def ffn_kernel(index_ref, rows_ref, order_ref, down_ref, *refs):
    *pieces, out_ref, total_ref = refs
    groups, chunk_rows, _ = out_ref.shape
    width = rows_ref.shape[1]
    chunks = width // LANES
    each = chunk_rows // chunks
    chips = len(pieces) // 2
    both = pieces[0].shape[0]
    columns = both // 2
    core = index_ref[0] % 2
    chip = index_ref[0] // 2

    def experts_part(first, second):
        total = None
        for shift in range(chips):
            came = (chip - shift + chips) % chips
            hidden = []
            for piece in (first[shift], second[shift]):
                projected = dot_nt(rows_ref[...], piece[...])
                gate_val, up_val = projected[:, :columns], projected[:, columns:]
                hidden.append(jax.nn.gelu(gate_val, approximate=True) * up_val)
            hidden = jnp.concatenate(hidden, axis=1).astype(BF)
            part = dot(hidden, down_ref[pl.ds(pl.multiple_of(came * both, 16), both), :])
            total = part if total is None else total + part
        total_ref[...] = total.astype(BF)

    @pl.when(core == 0)
    def _():
        experts_part(pieces[:chips], pieces[chips:])

    @pl.when(core != 0)
    def _():
        experts_part(pieces[chips:], pieces[:chips])

    for group in range(groups):
        mine = total_ref[group * each : (group + 1) * each]
        stacked = jnp.concatenate([mine[:, at * LANES : (at + 1) * LANES] for at in range(chunks)], axis=0)
        out_ref[group] = dot_tn(order_ref[...], stacked).astype(BF)


def sum_kernel(parts_ref, out_ref):
    total = parts_ref[0].astype(F32)
    for at in range(1, parts_ref.shape[0]):
        total = total + parts_ref[at].astype(F32)
    out_ref[...] = total.astype(BF)


def combine_kernel(experts_ref, after_ref, gates_ref, select_ref, out_ref):
    block, width = after_ref.shape
    chunks = width // LANES
    picked = [dot_tn(select_ref[which], experts_ref[...]) for which in range(2)]
    for at in range(chunks):
        lanes = slice(at * LANES, (at + 1) * LANES)
        mine = slice(at * block, (at + 1) * block)
        total = gates_ref[0] * picked[0][mine] + gates_ref[1] * picked[1][mine]
        out_ref[:, lanes] = (after_ref[:, lanes] + total).astype(BF)


VMEM = pl.BlockSpec(memory_space=pltpu.VMEM)
HBM = pl.BlockSpec(memory_space=pltpu.HBM)
SMEM = pl.BlockSpec(memory_space=pltpu.SMEM)


def in_hbm(array):
    return pltpu.with_memory_space_constraint(array, pltpu.HBM)


PARAMS = pltpu.CompilerParams(vmem_limit_bytes=16 * 1024 * 1024)


def body(
    resid, attn_gain, w_query, w_key, w_value, w_attn_out, cache, cache_lens, seg_ids, ffn_gain, router, routes, w_in, w_out
):
    hid = ("x", "c")
    hid_count = lax.axis_size(hid)
    hid_index = lax.axis_index(hid).astype(jnp.int32).reshape(1)
    group_rows, width = resid.shape
    experts = router.shape[1]
    block = group_rows // hid_count
    capacity = CAPACITY
    chunks = width // LANES
    slot_count = experts * chunks * capacity
    split = lax.axis_size("y")
    w_cols = jnp.transpose(w_in, (0, 2, 1))
    row = lax.axis_size("x")

    operands = (
        resid,
        attn_gain.reshape(1, width),
        w_query,
        w_key,
        w_value,
        w_attn_out,
        cache,
        cache_lens.reshape(1, -1),
        seg_ids,
        ffn_gain.reshape(1, width),
        router.T,
    )
    partial_mix, own, gain, router_rows = pl.pallas_call(
        attention_kernel,
        out_shape=(
            jax.ShapeDtypeStruct((group_rows, width), BF),
            jax.ShapeDtypeStruct((block, width), F32),
            jax.ShapeDtypeStruct((1, width), F32),
            jax.ShapeDtypeStruct((experts, width), BF),
        ),
        in_specs=[SMEM] + [HBM] * len(operands),
        out_specs=(VMEM,) * 4,
        scratch_shapes=[pltpu.VMEM(each.shape, each.dtype) for each in operands[:9]]
        + [pltpu.VMEM((1, group_rows), jnp.int32), pltpu.SemaphoreType.DMA((len(operands),))],
        compiler_params=PARAMS,
        name="attention",
    )(hid_index, *map(in_hbm, operands))
    chosen, select, column = pl.pallas_call(
        routing_kernel,
        out_shape=(
            jax.ShapeDtypeStruct((slot_count, LANES), BF),
            jax.ShapeDtypeStruct((2, slot_count, LANES), BF),
            jax.ShapeDtypeStruct((2, block, LANES), jnp.int32),
        ),
        in_specs=[SMEM, VMEM, VMEM],
        out_specs=(VMEM,) * 3,
        compiler_params=PARAMS,
        name="routing",
    )(hid_index, routes.T, gain)
    parts = lax.all_to_all(partial_mix.reshape(hid_count, block, width), hid, 0, 0, tiled=True)
    outgoing, after, ffn_in = pl.pallas_call(
        dispatch_kernel,
        out_shape=(
            jax.ShapeDtypeStruct((slot_count, LANES), BF),
            jax.ShapeDtypeStruct((block, width), F32),
            jax.ShapeDtypeStruct((block, width), BF),
        ),
        in_specs=[VMEM] * 4,
        out_specs=(VMEM,) * 3,
        compiler_params=PARAMS,
        name="dispatch",
    )(parts, own, gain, chosen)
    gates = pl.pallas_call(
        gates_kernel,
        out_shape=jax.ShapeDtypeStruct((2, block, LANES), F32),
        in_specs=[VMEM] * 3,
        out_specs=VMEM,
        compiler_params=PARAMS,
        name="gates",
    )(ffn_in, router_rows, column)
    gates, w_cols = lax.optimization_barrier((gates, w_cols))
    exchanged = (experts, chunks * CAPACITY, LANES)
    arrived = lax.all_to_all(outgoing.reshape(exchanged), "z", 0, 0, tiled=True)
    own_core = [w_cols]
    for shift in range(1, row):
        own_core.append(lax.ppermute(w_cols, "x", [(at, (at + shift) % row) for at in range(row)]))
    spread = jnp.broadcast_to(arrived.reshape(1, slot_count, LANES), (split, slot_count, LANES))
    order = pl.pallas_call(
        functools.partial(order_kernel, chunks),
        out_shape=jax.ShapeDtypeStruct((slot_count, slot_count), BF),
        in_specs=[VMEM],
        out_specs=VMEM,
        compiler_params=PARAMS,
        name="order",
    )(spread)
    order, *own_core = lax.optimization_barrier((order, *own_core))
    other_core = [lax.ppermute(cols, "c", [(0, 1), (1, 0)]) for cols in own_core]
    tokens = lax.all_to_all(spread, "y", 0, 0, tiled=True)
    rows = pl.pallas_call(
        unpack_kernel,
        out_shape=jax.ShapeDtypeStruct((split * experts * CAPACITY, width), BF),
        in_specs=[VMEM] * 2,
        out_specs=VMEM,
        compiler_params=PARAMS,
        cost_estimate=pl.CostEstimate(flops=10**10, transcendentals=0, bytes_accessed=1 << 21),
        name="unpack",
    )(tokens, order)
    pieces = [cols.reshape(-1, width) for cols in (*own_core, *other_core)]
    projected = pl.pallas_call(
        ffn_kernel,
        out_shape=jax.ShapeDtypeStruct((split, slot_count, LANES), BF),
        in_specs=[SMEM] + [VMEM] * (3 + len(pieces)),
        out_specs=VMEM,
        scratch_shapes=[pltpu.VMEM((split * experts * CAPACITY, width), BF)],
        compiler_params=PARAMS,
        name="ffn",
    )(hid_index, rows, order, w_out, *pieces)
    quarters = lax.all_to_all(projected, "y", 0, 0, tiled=True)
    summed = pl.pallas_call(
        sum_kernel,
        out_shape=jax.ShapeDtypeStruct((slot_count, LANES), BF),
        in_specs=[VMEM],
        out_specs=VMEM,
        compiler_params=PARAMS,
        name="sum_quarters",
    )(quarters)
    returned = lax.all_to_all(summed.reshape(exchanged), "z", 0, 0, tiled=True)
    return pl.pallas_call(
        combine_kernel,
        out_shape=jax.ShapeDtypeStruct((block, width), BF),
        in_specs=[VMEM] * 4,
        out_specs=VMEM,
        compiler_params=PARAMS,
        name="combine",
    )(returned.reshape(slot_count, LANES), after, gates, select)


def solution(mesh):
    fine = Mesh(mesh.devices.reshape(16, 4, 4, 2), ("z", "y", "x", "c"))
    req = ("z", "y")
    hid = ("x", "c")
    in_specs = (
        P(req, None),
        P(),
        P(None, hid),
        P(None, hid),
        P(None, hid),
        P(hid, None),
        P(req, None, None, hid),
        P(req),
        P(req, None),
        P(),
        P(),
        P(req, None),
        P(None, None, req + hid),
        P(req, None),
    )
    out_specs = P(req + hid, None)
    return jax.shard_map(body, mesh=fine, in_specs=in_specs, out_specs=out_specs, check_vma=False)
```

```python
import functools

import jax
import jax.numpy as jnp
from jax import lax
from jax.experimental import pallas as pl
from jax.experimental.pallas import tpu as pltpu
from jax.sharding import Mesh
from jax.sharding import PartitionSpec as P

HDIM = 64
EPS = 1e-06
BF = jnp.bfloat16
F32 = jnp.float32
LANES = 128
CAPACITY = 3


def dot(a, b):
    return jnp.dot(a, b, preferred_element_type=F32)


def dot_nt(a, b):
    return lax.dot_general(a, b, (((1,), (1,)), ((), ())), preferred_element_type=F32)


def dot_tn(a, b):
    return lax.dot_general(a, b, (((0,), (0,)), ((), ())), preferred_element_type=F32)


def iota(shape, dim):
    return lax.broadcasted_iota(jnp.int32, shape, dim)


def to_column(row, size):
    diagonal = iota((size, size), 0) == iota((size, size), 1)
    return jnp.sum(jnp.where(diagonal, jnp.broadcast_to(row, (size, size)), 0), axis=1, keepdims=True)


def attention_kernel(
    index_ref, resid_hbm, gain_hbm, wq_hbm, wk_hbm, wv_hbm, wo_hbm, cache_hbm, lens_hbm, seg_hbm,
    ffn_gain_hbm, router_hbm, out_ref, own_ref, ffn_gain_ref, router_ref,
    resid_ref, gain_ref, wq_ref, wk_ref, wv_ref, wo_ref, cache_ref, lens_ref, seg_ref, seg_row, sems
):
    sources = (
        resid_hbm, gain_hbm, wq_hbm, wk_hbm, wv_hbm, seg_hbm, lens_hbm, cache_hbm, wo_hbm, ffn_gain_hbm, router_hbm
    )
    targets = (
        resid_ref, gain_ref, wq_ref, wk_ref, wv_ref, seg_ref, lens_ref, cache_ref, wo_ref, ffn_gain_ref, router_ref
    )
    copies = [pltpu.make_async_copy(a, b, sems.at[i]) for i, (a, b) in enumerate(zip(sources, targets))]
    for copy in copies:
        copy.start()
    total = resid_ref.shape[0]
    packed = seg_ref.shape[1]
    decoded, _, slots, width = cache_ref.shape
    heads = width // HDIM
    scale = HDIM ** (-0.5)
    copies[0].wait()
    copies[1].wait()
    x = resid_ref[...].astype(F32)
    inverse = lax.rsqrt(jnp.mean(x * x, axis=-1, keepdims=True) + EPS)
    normed = (x * inverse * gain_ref[...]).astype(BF)
    copies[2].wait()
    query = dot(normed, wq_ref[...]).astype(BF)
    copies[3].wait()
    keys = dot(normed, wk_ref[...]).astype(BF)
    copies[4].wait()
    values = dot(normed, wv_ref[...]).astype(BF)
    copies[5].wait()
    copies[6].wait()
    copies[7].wait()

    seg_row[...] = iota((1, total), 1) + (1 << 20)
    seg_row[:, :packed] = seg_ref[...]
    segments = seg_row[...]
    allowed = (iota((total, total), 1) <= iota((total, total), 0)) & (to_column(segments, total) == segments)
    lengths = to_column(lens_ref[...], decoded)
    slot_at = iota((decoded, decoded * slots), 1)
    own_cache = (slot_at // slots == iota((decoded, decoded * slots), 0)) & (slot_at % slots < lengths)

    cached_keys = cache_ref[:, 0].reshape(decoded * slots, width)
    cached_values = cache_ref[:, 1].reshape(decoded * slots, width)
    lane_head = iota((total, width), 1) // HDIM
    context = jnp.zeros((total, width), F32)
    for head in range(heads):
        mine = lane_head == head
        head_query = jnp.where(mine, query, jnp.zeros_like(query))
        scores = jnp.where(allowed, dot_nt(head_query, keys) * scale, -jnp.inf)
        highest = jnp.max(scores, axis=-1, keepdims=True)
        cached = jnp.where(own_cache, dot_nt(head_query[packed:], cached_keys) * scale, -jnp.inf)
        top_dec = jnp.maximum(highest[packed:], jnp.max(cached, axis=-1, keepdims=True))
        highest = jnp.concatenate([highest[:packed], top_dec], axis=0)
        weights = jnp.exp(scores - highest)
        weights_cache = jnp.exp(cached - top_dec)
        norm = jnp.sum(weights, axis=-1, keepdims=True)
        norm_dec = norm[packed:] + jnp.sum(weights_cache, axis=-1, keepdims=True)
        norm = jnp.concatenate([norm[:packed], norm_dec], axis=0)
        part = dot((weights / norm).astype(BF), values)
        part_cache = dot((weights_cache / norm_dec).astype(BF), cached_values)
        part = jnp.concatenate([part[:packed], part[packed:] + part_cache], axis=0)
        context = jnp.where(mine, part, context)
    copies[8].wait()
    out_ref[...] = dot(context.astype(BF), wo_ref[...]).astype(out_ref.dtype)

    block = own_ref.shape[0]
    index = index_ref[0]
    own_ref[...] = resid_ref[pl.ds(pl.multiple_of(index * block, block), block), :].astype(F32)
    copies[9].wait()
    copies[10].wait()


def own_routes(routes_ref, which, index, block):
    lane = iota((1, LANES), 1)
    row = pltpu.roll(routes_ref[pl.ds(which, 1), :], (LANES - index * block) % LANES, 1)
    size = block
    while size < LANES:
        row = jnp.where(lane < size, row, pltpu.roll(row, size, 1))
        size *= 2
    return row


def placement(row, columns, block, capacity):
    token = iota((block, LANES), 1) % block
    before = iota((block, LANES), 0) < token
    slot = jnp.zeros((1, LANES), jnp.int32)
    for column in columns:
        slot = slot + jnp.sum(((column == row) & before).astype(jnp.int32), axis=0, keepdims=True)
    return row * capacity + slot


def slot_rows(rows, capacity, chunks):
    at = iota((rows, LANES), 0)
    expert = at // (chunks * capacity)
    rest = at - expert * (chunks * capacity)
    chunk = rest // capacity
    return expert * capacity + rest - chunk * capacity, chunk


def route_columns(rows, block):
    size = (block, LANES)
    diagonal = iota(size, 0) == iota(size, 1)
    return [
        jnp.sum(jnp.where(diagonal, jnp.broadcast_to(row, size), 0), axis=1, keepdims=True) for row in rows
    ]


def routing_kernel(index_ref, routes_ref, gain_ref, chosen_ref, select_ref, column_ref):
    block = column_ref.shape[1]
    chunks = gain_ref.shape[1] // LANES
    rows = [own_routes(routes_ref, which, index_ref[0], block) for which in range(2)]
    columns = route_columns(rows, block)
    wanted, chunk = slot_rows(chosen_ref.shape[0], CAPACITY, chunks)
    same = chunk == iota(chunk.shape, 1) // block
    both = None
    for which in range(2):
        target = placement(rows[which], columns, block, CAPACITY)
        here = jnp.where(same & (wanted == target), 1.0, 0.0)
        select_ref[which] = here.astype(BF)
        both = here if both is None else both + here
        column_ref[which] = jnp.broadcast_to(columns[which], (block, LANES))
    chosen_ref[...] = both.astype(BF)


def mix_kernel(parts_ref, own_ref, gain_ref, after_ref, ffn_in_ref):
    mixed = parts_ref[0].astype(F32)
    for source in range(1, parts_ref.shape[0]):
        mixed = mixed + parts_ref[source].astype(F32)
    after = own_ref[...] + mixed
    after_ref[...] = after
    inverse = lax.rsqrt(jnp.mean(after * after, axis=-1, keepdims=True) + EPS)
    ffn_in_ref[...] = (after * inverse * gain_ref[...]).astype(BF)


def dispatch_kernel(ffn_in_ref, chosen_ref, out_ref):
    chunks = ffn_in_ref.shape[1] // LANES
    stacked = jnp.concatenate([ffn_in_ref[:, at * LANES : (at + 1) * LANES] for at in range(chunks)], axis=0)
    out_ref[...] = dot(chosen_ref[...], stacked).astype(BF)


def gates_kernel(ffn_in_ref, router_ref, column_ref, gates_ref):
    block = ffn_in_ref.shape[0]
    experts = router_ref.shape[0]
    logits = dot_nt(ffn_in_ref[...], router_ref[...])
    expert_at = iota((block, experts), 1)
    for which in range(2):
        mine = expert_at == column_ref[which][:, :experts]
        picked = jnp.sum(jnp.where(mine, logits, 0.0), axis=1, keepdims=True)
        gates_ref[which] = jnp.broadcast_to(jax.nn.sigmoid(picked), (block, LANES))


def order_kernel(chunks, tokens_ref, order_ref):
    chunk_rows = order_ref.shape[0]
    each = chunk_rows // chunks
    at = iota((chunk_rows, chunk_rows), 0)
    chunk = at // each
    rest = at - chunk * each
    source = rest // CAPACITY
    wanted = source * (chunks * CAPACITY) + chunk * CAPACITY + rest - source * CAPACITY
    order_ref[...] = jnp.where(wanted == iota((chunk_rows, chunk_rows), 1), 1.0, 0.0).astype(BF)


def unpack_kernel(tokens_ref, order_ref, rows_ref):
    groups, chunk_rows, _ = tokens_ref.shape
    chunks = rows_ref.shape[1] // LANES
    each = chunk_rows // chunks
    for group in range(groups):
        unpacked = dot(order_ref[...], tokens_ref[group]).astype(BF)
        for at in range(chunks):
            rows_ref[group * each : (group + 1) * each, at * LANES : (at + 1) * LANES] = unpacked[
                at * each : (at + 1) * each
            ]


def ffn_kernel(index_ref, rows_ref, order_ref, down_ref, *refs):
    *pieces, out_ref, total_ref = refs
    groups, chunk_rows, _ = out_ref.shape
    width = rows_ref.shape[1]
    chunks = width // LANES
    each = chunk_rows // chunks
    chips = len(pieces) // 2
    both = pieces[0].shape[0]
    columns = both // 2
    core = index_ref[0] % 2
    chip = index_ref[0] // 2

    def experts_part(first, second):
        total = None
        for shift in range(chips):
            came = (chip - shift + chips) % chips
            hidden = []
            for piece in (first[shift], second[shift]):
                projected = dot_nt(rows_ref[...], piece[...])
                gate_val, up_val = projected[:, :columns], projected[:, columns:]
                hidden.append(jax.nn.gelu(gate_val, approximate=True) * up_val)
            hidden = jnp.concatenate(hidden, axis=1).astype(BF)
            part = dot(hidden, down_ref[pl.ds(pl.multiple_of(came * both, 16), both), :])
            total = part if total is None else total + part
        total_ref[...] = total.astype(BF)

    @pl.when(core == 0)
    def _():
        experts_part(pieces[:chips], pieces[chips:])

    @pl.when(core != 0)
    def _():
        experts_part(pieces[chips:], pieces[:chips])

    for group in range(groups):
        mine = total_ref[group * each : (group + 1) * each]
        stacked = jnp.concatenate([mine[:, at * LANES : (at + 1) * LANES] for at in range(chunks)], axis=0)
        out_ref[group] = dot_tn(order_ref[...], stacked).astype(BF)


def sum_kernel(parts_ref, out_ref):
    total = parts_ref[0].astype(F32)
    for at in range(1, parts_ref.shape[0]):
        total = total + parts_ref[at].astype(F32)
    out_ref[...] = total.astype(BF)


def combine_kernel(experts_ref, after_ref, gates_ref, select_ref, out_ref):
    block, width = after_ref.shape
    chunks = width // LANES
    picked = [dot_tn(select_ref[which], experts_ref[...]) for which in range(2)]
    for at in range(chunks):
        lanes = slice(at * LANES, (at + 1) * LANES)
        mine = slice(at * block, (at + 1) * block)
        total = gates_ref[0] * picked[0][mine] + gates_ref[1] * picked[1][mine]
        out_ref[:, lanes] = (after_ref[:, lanes] + total).astype(BF)


VMEM = pl.BlockSpec(memory_space=pltpu.VMEM)
HBM = pl.BlockSpec(memory_space=pltpu.HBM)
SMEM = pl.BlockSpec(memory_space=pltpu.SMEM)


def in_hbm(array):
    return pltpu.with_memory_space_constraint(array, pltpu.HBM)


LONG = pl.CostEstimate(flops=10**10, transcendentals=0, bytes_accessed=1 << 21)
PARAMS = pltpu.CompilerParams(vmem_limit_bytes=16 * 1024 * 1024)


def body(
    resid, attn_gain, w_query, w_key, w_value, w_attn_out, cache, cache_lens, seg_ids, ffn_gain, router, routes, w_in, w_out
):
    hid = ("x", "c")
    hid_count = lax.axis_size(hid)
    hid_index = lax.axis_index(hid).astype(jnp.int32).reshape(1)
    group_rows, width = resid.shape
    experts = router.shape[1]
    block = group_rows // hid_count
    capacity = CAPACITY
    chunks = width // LANES
    slot_count = experts * chunks * capacity
    split = lax.axis_size("y")
    w_cols = jnp.transpose(w_in, (0, 2, 1))
    row = lax.axis_size("x")

    operands = (
        resid,
        attn_gain.reshape(1, width),
        w_query,
        w_key,
        w_value,
        w_attn_out,
        cache,
        cache_lens.reshape(1, -1),
        seg_ids,
        ffn_gain.reshape(1, width),
        router.T,
    )
    partial_mix, own, gain, router_rows = pl.pallas_call(
        attention_kernel,
        out_shape=(
            jax.ShapeDtypeStruct((group_rows, width), BF),
            jax.ShapeDtypeStruct((block, width), F32),
            jax.ShapeDtypeStruct((1, width), F32),
            jax.ShapeDtypeStruct((experts, width), BF),
        ),
        in_specs=[SMEM] + [HBM] * len(operands),
        out_specs=(VMEM,) * 4,
        scratch_shapes=[pltpu.VMEM(each.shape, each.dtype) for each in operands[:9]]
        + [pltpu.VMEM((1, group_rows), jnp.int32), pltpu.SemaphoreType.DMA((len(operands),))],
        compiler_params=PARAMS,
        name="attention",
    )(hid_index, *map(in_hbm, operands))
    chosen, select, column = pl.pallas_call(
        routing_kernel,
        out_shape=(
            jax.ShapeDtypeStruct((slot_count, LANES), BF),
            jax.ShapeDtypeStruct((2, slot_count, LANES), BF),
            jax.ShapeDtypeStruct((2, block, LANES), jnp.int32),
        ),
        in_specs=[SMEM, VMEM, VMEM],
        out_specs=(VMEM,) * 3,
        compiler_params=PARAMS,
        name="routing",
    )(hid_index, routes.T, gain)
    column, w_cols = lax.optimization_barrier((column, w_cols))
    before = lax.ppermute(w_cols, "x", [(at, (at + 1) % row) for at in range(row)])
    after_it = lax.ppermute(w_cols, "x", [(at, (at - 1) % row) for at in range(row)])
    parts = lax.all_to_all(partial_mix.reshape(hid_count, block, width), hid, 0, 0, tiled=True)
    after, ffn_in = pl.pallas_call(
        mix_kernel,
        out_shape=(jax.ShapeDtypeStruct((block, width), F32), jax.ShapeDtypeStruct((block, width), BF)),
        in_specs=[VMEM] * 3,
        out_specs=(VMEM,) * 2,
        compiler_params=PARAMS,
        cost_estimate=LONG,
        name="mix",
    )(parts, own, gain)
    ffn_in, before, after_it = lax.optimization_barrier((ffn_in, before, after_it))
    outgoing = pl.pallas_call(
        dispatch_kernel,
        out_shape=jax.ShapeDtypeStruct((slot_count, LANES), BF),
        in_specs=[VMEM] * 2,
        out_specs=VMEM,
        compiler_params=PARAMS,
        name="dispatch",
    )(ffn_in, chosen)
    gates = pl.pallas_call(
        gates_kernel,
        out_shape=jax.ShapeDtypeStruct((2, block, LANES), F32),
        in_specs=[VMEM] * 3,
        out_specs=VMEM,
        compiler_params=PARAMS,
        name="gates",
    )(ffn_in, router_rows, column)
    exchanged = (experts, chunks * CAPACITY, LANES)
    arrived = lax.all_to_all(outgoing.reshape(exchanged), "z", 0, 0, tiled=True)
    order = pl.pallas_call(
        functools.partial(order_kernel, chunks),
        out_shape=jax.ShapeDtypeStruct((slot_count, slot_count), BF),
        in_specs=[VMEM],
        out_specs=VMEM,
        compiler_params=PARAMS,
        name="order",
    )(gates)
    order, w_cols, before, after_it = lax.optimization_barrier((order, w_cols, before, after_it))
    across = lax.ppermute(w_cols, "x", [(at, (at + 2) % row) for at in range(row)])
    own_core = (w_cols, before, across, after_it)
    other_core = [lax.ppermute(cols, "c", [(0, 1), (1, 0)]) for cols in own_core]
    tokens = lax.all_gather(arrived.reshape(slot_count, LANES), "y", axis=0)
    rows = pl.pallas_call(
        unpack_kernel,
        out_shape=jax.ShapeDtypeStruct((split * experts * CAPACITY, width), BF),
        in_specs=[VMEM] * 2,
        out_specs=VMEM,
        compiler_params=PARAMS,
        cost_estimate=LONG,
        name="unpack",
    )(tokens, order)
    pieces = [cols.reshape(-1, width) for cols in (*own_core, *other_core)]
    projected = pl.pallas_call(
        ffn_kernel,
        out_shape=jax.ShapeDtypeStruct((split, slot_count, LANES), BF),
        in_specs=[SMEM] + [VMEM] * (3 + len(pieces)),
        out_specs=VMEM,
        scratch_shapes=[pltpu.VMEM((split * experts * CAPACITY, width), BF)],
        compiler_params=PARAMS,
        name="ffn",
    )(hid_index, rows, order, w_out, *pieces)
    quarters = lax.all_to_all(projected, "y", 0, 0, tiled=True)
    summed = pl.pallas_call(
        sum_kernel,
        out_shape=jax.ShapeDtypeStruct((slot_count, LANES), BF),
        in_specs=[VMEM],
        out_specs=VMEM,
        compiler_params=PARAMS,
        name="sum_quarters",
    )(quarters)
    returned = lax.all_to_all(summed.reshape(exchanged), "z", 0, 0, tiled=True)
    return pl.pallas_call(
        combine_kernel,
        out_shape=jax.ShapeDtypeStruct((block, width), BF),
        in_specs=[VMEM] * 4,
        out_specs=VMEM,
        compiler_params=PARAMS,
        name="combine",
    )(returned.reshape(slot_count, LANES), after, gates, select)


def solution(mesh):
    fine = Mesh(mesh.devices.reshape(16, 4, 4, 2), ("z", "y", "x", "c"))
    req = ("z", "y")
    hid = ("x", "c")
    in_specs = (
        P(req, None),
        P(),
        P(None, hid),
        P(None, hid),
        P(None, hid),
        P(hid, None),
        P(req, None, None, hid),
        P(req),
        P(req, None),
        P(),
        P(),
        P(req, None),
        P(None, None, req + hid),
        P(req, None),
    )
    out_specs = P(req + hid, None)
    return jax.shard_map(body, mesh=fine, in_specs=in_specs, out_specs=out_specs, check_vma=False)
```

```python
import functools

import jax
import jax.numpy as jnp
from jax import lax
from jax.experimental import pallas as pl
from jax.experimental.pallas import tpu as pltpu
from jax.sharding import Mesh
from jax.sharding import PartitionSpec as P

HDIM = 64
EPS = 1e-06
BF = jnp.bfloat16
F32 = jnp.float32
LANES = 128
CAPACITY = 3


def dot(a, b):
    return jnp.dot(a, b, preferred_element_type=F32)


def dot_nt(a, b):
    return lax.dot_general(a, b, (((1,), (1,)), ((), ())), preferred_element_type=F32)


def dot_tn(a, b):
    return lax.dot_general(a, b, (((0,), (0,)), ((), ())), preferred_element_type=F32)


def iota(shape, dim):
    return lax.broadcasted_iota(jnp.int32, shape, dim)


def to_column(row, size):
    diagonal = iota((size, size), 0) == iota((size, size), 1)
    return jnp.sum(jnp.where(diagonal, jnp.broadcast_to(row, (size, size)), 0), axis=1, keepdims=True)


def attention_kernel(
    index_ref, resid_hbm, gain_hbm, wq_hbm, wk_hbm, wv_hbm, wo_hbm, cache_hbm, lens_hbm, seg_hbm,
    ffn_gain_hbm, router_hbm, out_ref, own_ref, ffn_gain_ref, router_ref,
    resid_ref, gain_ref, wq_ref, wk_ref, wv_ref, wo_ref, cache_ref, lens_ref, seg_ref, seg_row, sems
):
    sources = (
        resid_hbm, gain_hbm, wq_hbm, wk_hbm, wv_hbm, seg_hbm, lens_hbm, cache_hbm, wo_hbm, ffn_gain_hbm, router_hbm
    )
    targets = (
        resid_ref, gain_ref, wq_ref, wk_ref, wv_ref, seg_ref, lens_ref, cache_ref, wo_ref, ffn_gain_ref, router_ref
    )
    copies = [pltpu.make_async_copy(a, b, sems.at[i]) for i, (a, b) in enumerate(zip(sources, targets))]
    for copy in copies:
        copy.start()
    total = resid_ref.shape[0]
    packed = seg_ref.shape[1]
    decoded, _, slots, width = cache_ref.shape
    heads = width // HDIM
    scale = HDIM ** (-0.5)
    copies[0].wait()
    copies[1].wait()
    x = resid_ref[...].astype(F32)
    inverse = lax.rsqrt(jnp.mean(x * x, axis=-1, keepdims=True) + EPS)
    normed = (x * inverse * gain_ref[...]).astype(BF)
    copies[2].wait()
    query = dot(normed, wq_ref[...]).astype(BF)
    copies[3].wait()
    keys = dot(normed, wk_ref[...]).astype(BF)
    copies[4].wait()
    values = dot(normed, wv_ref[...]).astype(BF)
    copies[5].wait()
    copies[6].wait()
    copies[7].wait()

    seg_row[...] = iota((1, total), 1) + (1 << 20)
    seg_row[:, :packed] = seg_ref[...]
    segments = seg_row[...]
    allowed = (iota((total, total), 1) <= iota((total, total), 0)) & (to_column(segments, total) == segments)
    lengths = to_column(lens_ref[...], decoded)
    slot_at = iota((decoded, decoded * slots), 1)
    own_cache = (slot_at // slots == iota((decoded, decoded * slots), 0)) & (slot_at % slots < lengths)

    cached_keys = cache_ref[:, 0].reshape(decoded * slots, width)
    cached_values = cache_ref[:, 1].reshape(decoded * slots, width)
    lane_head = iota((total, width), 1) // HDIM
    context = jnp.zeros((total, width), F32)
    for head in range(heads):
        mine = lane_head == head
        head_query = jnp.where(mine, query, jnp.zeros_like(query))
        scores = jnp.where(allowed, dot_nt(head_query, keys) * scale, -jnp.inf)
        highest = jnp.max(scores, axis=-1, keepdims=True)
        cached = jnp.where(own_cache, dot_nt(head_query[packed:], cached_keys) * scale, -jnp.inf)
        top_dec = jnp.maximum(highest[packed:], jnp.max(cached, axis=-1, keepdims=True))
        highest = jnp.concatenate([highest[:packed], top_dec], axis=0)
        weights = jnp.exp(scores - highest)
        weights_cache = jnp.exp(cached - top_dec)
        norm = jnp.sum(weights, axis=-1, keepdims=True)
        norm_dec = norm[packed:] + jnp.sum(weights_cache, axis=-1, keepdims=True)
        norm = jnp.concatenate([norm[:packed], norm_dec], axis=0)
        part = dot((weights / norm).astype(BF), values)
        part_cache = dot((weights_cache / norm_dec).astype(BF), cached_values)
        part = jnp.concatenate([part[:packed], part[packed:] + part_cache], axis=0)
        context = jnp.where(mine, part, context)
    copies[8].wait()
    out_ref[...] = dot(context.astype(BF), wo_ref[...]).astype(out_ref.dtype)

    block = own_ref.shape[0]
    index = index_ref[0]
    own_ref[...] = resid_ref[pl.ds(pl.multiple_of(index * block, block), block), :].astype(F32)
    copies[9].wait()
    copies[10].wait()


def own_routes(routes_ref, which, index, block):
    lane = iota((1, LANES), 1)
    row = pltpu.roll(routes_ref[pl.ds(which, 1), :], (LANES - index * block) % LANES, 1)
    size = block
    while size < LANES:
        row = jnp.where(lane < size, row, pltpu.roll(row, size, 1))
        size *= 2
    return row


def placement(row, columns, block, capacity):
    token = iota((block, LANES), 1) % block
    before = iota((block, LANES), 0) < token
    slot = jnp.zeros((1, LANES), jnp.int32)
    for column in columns:
        slot = slot + jnp.sum(((column == row) & before).astype(jnp.int32), axis=0, keepdims=True)
    return row * capacity + slot


def slot_rows(rows, capacity, chunks):
    at = iota((rows, LANES), 0)
    expert = at // (chunks * capacity)
    rest = at - expert * (chunks * capacity)
    chunk = rest // capacity
    return expert * capacity + rest - chunk * capacity, chunk


def route_columns(rows, block):
    size = (block, LANES)
    diagonal = iota(size, 0) == iota(size, 1)
    return [
        jnp.sum(jnp.where(diagonal, jnp.broadcast_to(row, size), 0), axis=1, keepdims=True) for row in rows
    ]


def routing_kernel(index_ref, routes_ref, gain_ref, chosen_ref, select_ref, column_ref):
    block = column_ref.shape[1]
    chunks = gain_ref.shape[1] // LANES
    rows = [own_routes(routes_ref, which, index_ref[0], block) for which in range(2)]
    columns = route_columns(rows, block)
    wanted, chunk = slot_rows(chosen_ref.shape[0], CAPACITY, chunks)
    same = chunk == iota(chunk.shape, 1) // block
    both = None
    for which in range(2):
        target = placement(rows[which], columns, block, CAPACITY)
        here = jnp.where(same & (wanted == target), 1.0, 0.0)
        select_ref[which] = here.astype(BF)
        both = here if both is None else both + here
        column_ref[which] = jnp.broadcast_to(columns[which], (block, LANES))
    chosen_ref[...] = both.astype(BF)


def mix_kernel(parts_ref, own_ref, gain_ref, after_ref, ffn_in_ref):
    mixed = parts_ref[0].astype(F32)
    for source in range(1, parts_ref.shape[0]):
        mixed = mixed + parts_ref[source].astype(F32)
    after = own_ref[...] + mixed
    after_ref[...] = after
    inverse = lax.rsqrt(jnp.mean(after * after, axis=-1, keepdims=True) + EPS)
    ffn_in_ref[...] = (after * inverse * gain_ref[...]).astype(BF)


def dispatch_kernel(ffn_in_ref, chosen_ref, out_ref):
    chunks = ffn_in_ref.shape[1] // LANES
    stacked = jnp.concatenate([ffn_in_ref[:, at * LANES : (at + 1) * LANES] for at in range(chunks)], axis=0)
    out_ref[...] = dot(chosen_ref[...], stacked).astype(BF)


def gates_kernel(ffn_in_ref, router_ref, column_ref, gates_ref):
    block = ffn_in_ref.shape[0]
    experts = router_ref.shape[0]
    logits = dot_nt(ffn_in_ref[...], router_ref[...])
    expert_at = iota((block, experts), 1)
    for which in range(2):
        mine = expert_at == column_ref[which][:, :experts]
        picked = jnp.sum(jnp.where(mine, logits, 0.0), axis=1, keepdims=True)
        gates_ref[which] = jnp.broadcast_to(jax.nn.sigmoid(picked), (block, LANES))


def order_kernel(chunks, tokens_ref, order_ref):
    chunk_rows = order_ref.shape[0]
    each = chunk_rows // chunks
    at = iota((chunk_rows, chunk_rows), 0)
    chunk = at // each
    rest = at - chunk * each
    source = rest // CAPACITY
    wanted = source * (chunks * CAPACITY) + chunk * CAPACITY + rest - source * CAPACITY
    order_ref[...] = jnp.where(wanted == iota((chunk_rows, chunk_rows), 1), 1.0, 0.0).astype(BF)


def stack_kernel(*refs):
    *pieces, out_ref = refs
    for at, piece in enumerate(pieces):
        out_ref[at] = piece[...]


def unpack_kernel(tokens_ref, order_ref, rows_ref):
    groups, chunk_rows, _ = tokens_ref.shape
    chunks = rows_ref.shape[1] // LANES
    each = chunk_rows // chunks
    for group in range(groups):
        unpacked = dot(order_ref[...], tokens_ref[group]).astype(BF)
        for at in range(chunks):
            rows_ref[group * each : (group + 1) * each, at * LANES : (at + 1) * LANES] = unpacked[
                at * each : (at + 1) * each
            ]


def ffn_kernel(index_ref, rows_ref, order_ref, down_ref, own_ref, other_ref, out_ref, total_ref):
    groups, chunk_rows, _ = out_ref.shape
    width = rows_ref.shape[1]
    chunks = width // LANES
    each = chunk_rows // chunks
    chips, both, _ = own_ref.shape
    columns = both // 2
    core = index_ref[0] % 2
    chip = index_ref[0] // 2

    def experts_part(first, second):
        total = None
        for shift in range(chips):
            came = (chip - shift + chips) % chips
            hidden = []
            for pieces in (first, second):
                projected = dot_nt(rows_ref[...], pieces[shift])
                gate_val, up_val = projected[:, :columns], projected[:, columns:]
                hidden.append(jax.nn.gelu(gate_val, approximate=True) * up_val)
            hidden = jnp.concatenate(hidden, axis=1).astype(BF)
            part = dot(hidden, down_ref[pl.ds(pl.multiple_of(came * both, 16), both), :])
            total = part if total is None else total + part
        total_ref[...] = total.astype(BF)

    @pl.when(core == 0)
    def _():
        experts_part(own_ref, other_ref)

    @pl.when(core != 0)
    def _():
        experts_part(other_ref, own_ref)

    for group in range(groups):
        mine = total_ref[group * each : (group + 1) * each]
        stacked = jnp.concatenate([mine[:, at * LANES : (at + 1) * LANES] for at in range(chunks)], axis=0)
        out_ref[group] = dot_tn(order_ref[...], stacked).astype(BF)


def sum_kernel(parts_ref, out_ref):
    total = parts_ref[0].astype(F32)
    for at in range(1, parts_ref.shape[0]):
        total = total + parts_ref[at].astype(F32)
    out_ref[...] = total.astype(BF)


def combine_kernel(experts_ref, after_ref, gates_ref, select_ref, out_ref):
    block, width = after_ref.shape
    chunks = width // LANES
    picked = [dot_tn(select_ref[which], experts_ref[...]) for which in range(2)]
    for at in range(chunks):
        lanes = slice(at * LANES, (at + 1) * LANES)
        mine = slice(at * block, (at + 1) * block)
        total = gates_ref[0] * picked[0][mine] + gates_ref[1] * picked[1][mine]
        out_ref[:, lanes] = (after_ref[:, lanes] + total).astype(BF)


VMEM = pl.BlockSpec(memory_space=pltpu.VMEM)
HBM = pl.BlockSpec(memory_space=pltpu.HBM)
SMEM = pl.BlockSpec(memory_space=pltpu.SMEM)


def in_hbm(array):
    return pltpu.with_memory_space_constraint(array, pltpu.HBM)


LONG = pl.CostEstimate(flops=10**10, transcendentals=0, bytes_accessed=1 << 21)
PARAMS = pltpu.CompilerParams(vmem_limit_bytes=16 * 1024 * 1024)


def body(
    resid, attn_gain, w_query, w_key, w_value, w_attn_out, cache, cache_lens, seg_ids, ffn_gain, router, routes, w_in, w_out
):
    hid = ("x", "c")
    hid_count = lax.axis_size(hid)
    hid_index = lax.axis_index(hid).astype(jnp.int32).reshape(1)
    group_rows, width = resid.shape
    experts = router.shape[1]
    block = group_rows // hid_count
    capacity = CAPACITY
    chunks = width // LANES
    slot_count = experts * chunks * capacity
    split = lax.axis_size("y")
    w_cols = jnp.transpose(w_in, (0, 2, 1))
    row = lax.axis_size("x")

    operands = (
        resid,
        attn_gain.reshape(1, width),
        w_query,
        w_key,
        w_value,
        w_attn_out,
        cache,
        cache_lens.reshape(1, -1),
        seg_ids,
        ffn_gain.reshape(1, width),
        router.T,
    )
    partial_mix, own, gain, router_rows = pl.pallas_call(
        attention_kernel,
        out_shape=(
            jax.ShapeDtypeStruct((group_rows, width), BF),
            jax.ShapeDtypeStruct((block, width), F32),
            jax.ShapeDtypeStruct((1, width), F32),
            jax.ShapeDtypeStruct((experts, width), BF),
        ),
        in_specs=[SMEM] + [HBM] * len(operands),
        out_specs=(VMEM,) * 4,
        scratch_shapes=[pltpu.VMEM(each.shape, each.dtype) for each in operands[:9]]
        + [pltpu.VMEM((1, group_rows), jnp.int32), pltpu.SemaphoreType.DMA((len(operands),))],
        compiler_params=PARAMS,
        name="attention",
    )(hid_index, *map(in_hbm, operands))
    chosen, select, column = pl.pallas_call(
        routing_kernel,
        out_shape=(
            jax.ShapeDtypeStruct((slot_count, LANES), BF),
            jax.ShapeDtypeStruct((2, slot_count, LANES), BF),
            jax.ShapeDtypeStruct((2, block, LANES), jnp.int32),
        ),
        in_specs=[SMEM, VMEM, VMEM],
        out_specs=(VMEM,) * 3,
        compiler_params=PARAMS,
        name="routing",
    )(hid_index, routes.T, gain)
    column, w_cols = lax.optimization_barrier((column, w_cols))
    own_core = [w_cols]
    for shift in range(1, row):
        own_core.append(lax.ppermute(w_cols, "x", [(at, (at + shift) % row) for at in range(row)]))
    parts = lax.all_to_all(partial_mix.reshape(hid_count, block, width), hid, 0, 0, tiled=True)
    after, ffn_in = pl.pallas_call(
        mix_kernel,
        out_shape=(jax.ShapeDtypeStruct((block, width), F32), jax.ShapeDtypeStruct((block, width), BF)),
        in_specs=[VMEM] * 3,
        out_specs=(VMEM,) * 2,
        compiler_params=PARAMS,
        cost_estimate=LONG,
        name="mix",
    )(parts, own, gain)
    outgoing = pl.pallas_call(
        dispatch_kernel,
        out_shape=jax.ShapeDtypeStruct((slot_count, LANES), BF),
        in_specs=[VMEM] * 2,
        out_specs=VMEM,
        compiler_params=PARAMS,
        cost_estimate=LONG,
        name="dispatch",
    )(ffn_in, chosen)
    gates = pl.pallas_call(
        gates_kernel,
        out_shape=jax.ShapeDtypeStruct((2, block, LANES), F32),
        in_specs=[VMEM] * 3,
        out_specs=VMEM,
        compiler_params=PARAMS,
        cost_estimate=LONG,
        name="gates",
    )(ffn_in, router_rows, column)
    exchanged = (experts, chunks * CAPACITY, LANES)
    arrived = lax.all_to_all(outgoing.reshape(exchanged), "z", 0, 0, tiled=True)
    order = pl.pallas_call(
        functools.partial(order_kernel, chunks),
        out_shape=jax.ShapeDtypeStruct((slot_count, slot_count), BF),
        in_specs=[VMEM],
        out_specs=VMEM,
        compiler_params=PARAMS,
        cost_estimate=LONG,
        name="order",
    )(gates)
    order, *own_core = lax.optimization_barrier((order, *own_core))
    own_core = [cols.reshape(-1, width) for cols in own_core]
    stacked = pl.pallas_call(
        stack_kernel,
        out_shape=jax.ShapeDtypeStruct((row,) + own_core[0].shape, BF),
        in_specs=[VMEM] * row,
        out_specs=VMEM,
        compiler_params=PARAMS,
        cost_estimate=LONG,
        name="stack",
    )(*own_core)
    other_core = lax.ppermute(stacked, "c", [(0, 1), (1, 0)])
    tokens = lax.all_gather(arrived.reshape(slot_count, LANES), "y", axis=0)
    rows = pl.pallas_call(
        unpack_kernel,
        out_shape=jax.ShapeDtypeStruct((split * experts * CAPACITY, width), BF),
        in_specs=[VMEM] * 2,
        out_specs=VMEM,
        compiler_params=PARAMS,
        cost_estimate=LONG,
        name="unpack",
    )(tokens, order)
    projected = pl.pallas_call(
        ffn_kernel,
        out_shape=jax.ShapeDtypeStruct((split, slot_count, LANES), BF),
        in_specs=[SMEM] + [VMEM] * 5,
        out_specs=VMEM,
        scratch_shapes=[pltpu.VMEM((split * experts * CAPACITY, width), BF)],
        compiler_params=PARAMS,
        name="ffn",
    )(hid_index, rows, order, w_out, stacked, other_core)
    quarters = lax.all_to_all(projected, "y", 0, 0, tiled=True)
    summed = pl.pallas_call(
        sum_kernel,
        out_shape=jax.ShapeDtypeStruct((slot_count, LANES), BF),
        in_specs=[VMEM],
        out_specs=VMEM,
        compiler_params=PARAMS,
        name="sum_quarters",
    )(quarters)
    returned = lax.all_to_all(summed.reshape(exchanged), "z", 0, 0, tiled=True)
    return pl.pallas_call(
        combine_kernel,
        out_shape=jax.ShapeDtypeStruct((block, width), BF),
        in_specs=[VMEM] * 4,
        out_specs=VMEM,
        compiler_params=PARAMS,
        name="combine",
    )(returned.reshape(slot_count, LANES), after, gates, select)


def solution(mesh):
    fine = Mesh(mesh.devices.reshape(16, 4, 4, 2), ("z", "y", "x", "c"))
    req = ("z", "y")
    hid = ("x", "c")
    in_specs = (
        P(req, None),
        P(),
        P(None, hid),
        P(None, hid),
        P(None, hid),
        P(hid, None),
        P(req, None, None, hid),
        P(req),
        P(req, None),
        P(),
        P(),
        P(req, None),
        P(None, None, req + hid),
        P(req, None),
    )
    out_specs = P(req + hid, None)
    return jax.shard_map(body, mesh=fine, in_specs=in_specs, out_specs=out_specs, check_vma=False)
```

```python
import functools

import jax
import jax.numpy as jnp
from jax import lax
from jax.experimental import pallas as pl
from jax.experimental.pallas import tpu as pltpu
from jax.sharding import Mesh
from jax.sharding import PartitionSpec as P

HDIM = 64
EPS = 1e-06
BF = jnp.bfloat16
F32 = jnp.float32
LANES = 128
CAPACITY = 3


def dot(a, b):
    return jnp.dot(a, b, preferred_element_type=F32)


def dot_nt(a, b):
    return lax.dot_general(a, b, (((1,), (1,)), ((), ())), preferred_element_type=F32)


def dot_tn(a, b):
    return lax.dot_general(a, b, (((0,), (0,)), ((), ())), preferred_element_type=F32)


def iota(shape, dim):
    return lax.broadcasted_iota(jnp.int32, shape, dim)


def to_column(row, size):
    diagonal = iota((size, size), 0) == iota((size, size), 1)
    return jnp.sum(jnp.where(diagonal, jnp.broadcast_to(row, (size, size)), 0), axis=1, keepdims=True)


def attention_kernel(
    index_ref, resid_hbm, gain_hbm, wq_hbm, wk_hbm, wv_hbm, wo_hbm, cache_hbm, lens_hbm, seg_hbm,
    ffn_gain_hbm, router_hbm, out_ref, own_ref, ffn_gain_ref, router_ref,
    resid_ref, gain_ref, wq_ref, wk_ref, wv_ref, wo_ref, cache_ref, lens_ref, seg_ref, seg_row, sems
):
    sources = (
        resid_hbm, gain_hbm, wq_hbm, wk_hbm, wv_hbm, seg_hbm, lens_hbm, cache_hbm, wo_hbm, ffn_gain_hbm, router_hbm
    )
    targets = (
        resid_ref, gain_ref, wq_ref, wk_ref, wv_ref, seg_ref, lens_ref, cache_ref, wo_ref, ffn_gain_ref, router_ref
    )
    copies = [pltpu.make_async_copy(a, b, sems.at[i]) for i, (a, b) in enumerate(zip(sources, targets))]
    for copy in copies:
        copy.start()
    total = resid_ref.shape[0]
    packed = seg_ref.shape[1]
    decoded, _, slots, width = cache_ref.shape
    heads = width // HDIM
    scale = HDIM ** (-0.5)
    copies[0].wait()
    copies[1].wait()
    x = resid_ref[...].astype(F32)
    inverse = lax.rsqrt(jnp.mean(x * x, axis=-1, keepdims=True) + EPS)
    normed = (x * inverse * gain_ref[...]).astype(BF)
    copies[2].wait()
    query = dot(normed, wq_ref[...]).astype(BF)
    copies[3].wait()
    keys = dot(normed, wk_ref[...]).astype(BF)
    copies[4].wait()
    values = dot(normed, wv_ref[...]).astype(BF)
    copies[5].wait()
    copies[6].wait()
    copies[7].wait()

    seg_row[...] = iota((1, total), 1) + (1 << 20)
    seg_row[:, :packed] = seg_ref[...]
    segments = seg_row[...]
    allowed = (iota((total, total), 1) <= iota((total, total), 0)) & (to_column(segments, total) == segments)
    lengths = to_column(lens_ref[...], decoded)
    slot_at = iota((decoded, decoded * slots), 1)
    own_cache = (slot_at // slots == iota((decoded, decoded * slots), 0)) & (slot_at % slots < lengths)

    cached_keys = cache_ref[:, 0].reshape(decoded * slots, width)
    cached_values = cache_ref[:, 1].reshape(decoded * slots, width)
    lane_head = iota((total, width), 1) // HDIM
    context = jnp.zeros((total, width), F32)
    for head in range(heads):
        mine = lane_head == head
        head_query = jnp.where(mine, query, jnp.zeros_like(query))
        scores = jnp.where(allowed, dot_nt(head_query, keys) * scale, -jnp.inf)
        highest = jnp.max(scores, axis=-1, keepdims=True)
        cached = jnp.where(own_cache, dot_nt(head_query[packed:], cached_keys) * scale, -jnp.inf)
        top_dec = jnp.maximum(highest[packed:], jnp.max(cached, axis=-1, keepdims=True))
        highest = jnp.concatenate([highest[:packed], top_dec], axis=0)
        weights = jnp.exp(scores - highest)
        weights_cache = jnp.exp(cached - top_dec)
        norm = jnp.sum(weights, axis=-1, keepdims=True)
        norm_dec = norm[packed:] + jnp.sum(weights_cache, axis=-1, keepdims=True)
        norm = jnp.concatenate([norm[:packed], norm_dec], axis=0)
        part = dot((weights / norm).astype(BF), values)
        part_cache = dot((weights_cache / norm_dec).astype(BF), cached_values)
        part = jnp.concatenate([part[:packed], part[packed:] + part_cache], axis=0)
        context = jnp.where(mine, part, context)
    copies[8].wait()
    out_ref[...] = dot(context.astype(BF), wo_ref[...]).astype(out_ref.dtype)

    block = own_ref.shape[0]
    index = index_ref[0]
    own_ref[...] = resid_ref[pl.ds(pl.multiple_of(index * block, block), block), :].astype(F32)
    copies[9].wait()
    copies[10].wait()


def own_routes(routes_ref, which, index, block):
    lane = iota((1, LANES), 1)
    row = pltpu.roll(routes_ref[pl.ds(which, 1), :], (LANES - index * block) % LANES, 1)
    size = block
    while size < LANES:
        row = jnp.where(lane < size, row, pltpu.roll(row, size, 1))
        size *= 2
    return row


def placement(row, columns, block, capacity):
    token = iota((block, LANES), 1) % block
    before = iota((block, LANES), 0) < token
    slot = jnp.zeros((1, LANES), jnp.int32)
    for column in columns:
        slot = slot + jnp.sum(((column == row) & before).astype(jnp.int32), axis=0, keepdims=True)
    return row * capacity + slot


def slot_rows(rows, capacity, chunks):
    at = iota((rows, LANES), 0)
    expert = at // (chunks * capacity)
    rest = at - expert * (chunks * capacity)
    chunk = rest // capacity
    return expert * capacity + rest - chunk * capacity, chunk


def route_columns(rows, block):
    size = (block, LANES)
    diagonal = iota(size, 0) == iota(size, 1)
    return [
        jnp.sum(jnp.where(diagonal, jnp.broadcast_to(row, size), 0), axis=1, keepdims=True) for row in rows
    ]


def routing_kernel(index_ref, routes_ref, gain_ref, chosen_ref, select_ref, column_ref):
    block = column_ref.shape[1]
    chunks = gain_ref.shape[1] // LANES
    rows = [own_routes(routes_ref, which, index_ref[0], block) for which in range(2)]
    columns = route_columns(rows, block)
    wanted, chunk = slot_rows(chosen_ref.shape[0], CAPACITY, chunks)
    same = chunk == iota(chunk.shape, 1) // block
    both = None
    for which in range(2):
        target = placement(rows[which], columns, block, CAPACITY)
        here = jnp.where(same & (wanted == target), 1.0, 0.0)
        select_ref[which] = here.astype(BF)
        both = here if both is None else both + here
        column_ref[which] = jnp.broadcast_to(columns[which], (block, LANES))
    chosen_ref[...] = both.astype(BF)


def mix_kernel(parts_ref, own_ref, gain_ref, after_ref, ffn_in_ref):
    mixed = parts_ref[0].astype(F32)
    for source in range(1, parts_ref.shape[0]):
        mixed = mixed + parts_ref[source].astype(F32)
    after = own_ref[...] + mixed
    after_ref[...] = after
    inverse = lax.rsqrt(jnp.mean(after * after, axis=-1, keepdims=True) + EPS)
    ffn_in_ref[...] = (after * inverse * gain_ref[...]).astype(BF)


def dispatch_kernel(ffn_in_ref, chosen_ref, out_ref):
    chunks = ffn_in_ref.shape[1] // LANES
    stacked = jnp.concatenate([ffn_in_ref[:, at * LANES : (at + 1) * LANES] for at in range(chunks)], axis=0)
    out_ref[...] = dot(chosen_ref[...], stacked).astype(BF)


def gates_kernel(ffn_in_ref, router_ref, column_ref, gates_ref):
    block = ffn_in_ref.shape[0]
    experts = router_ref.shape[0]
    logits = dot_nt(ffn_in_ref[...], router_ref[...])
    expert_at = iota((block, experts), 1)
    for which in range(2):
        mine = expert_at == column_ref[which][:, :experts]
        picked = jnp.sum(jnp.where(mine, logits, 0.0), axis=1, keepdims=True)
        gates_ref[which] = jnp.broadcast_to(jax.nn.sigmoid(picked), (block, LANES))


def order_kernel(chunks, tokens_ref, order_ref):
    chunk_rows = order_ref.shape[0]
    each = chunk_rows // chunks
    at = iota((chunk_rows, chunk_rows), 0)
    chunk = at // each
    rest = at - chunk * each
    source = rest // CAPACITY
    wanted = source * (chunks * CAPACITY) + chunk * CAPACITY + rest - source * CAPACITY
    order_ref[...] = jnp.where(wanted == iota((chunk_rows, chunk_rows), 1), 1.0, 0.0).astype(BF)


def spread_kernel(tokens_ref, out_ref):
    for at in range(out_ref.shape[0]):
        out_ref[at] = tokens_ref[...]


def stack_kernel(spread_ref, *refs):
    *pieces, out_ref = refs
    for at, piece in enumerate(pieces):
        out_ref[at] = piece[...]


def unpack_kernel(tokens_ref, order_ref, rows_ref):
    groups, chunk_rows, _ = tokens_ref.shape
    chunks = rows_ref.shape[1] // LANES
    each = chunk_rows // chunks
    for group in range(groups):
        unpacked = dot(order_ref[...], tokens_ref[group]).astype(BF)
        for at in range(chunks):
            rows_ref[group * each : (group + 1) * each, at * LANES : (at + 1) * LANES] = unpacked[
                at * each : (at + 1) * each
            ]


def ffn_kernel(index_ref, rows_ref, order_ref, down_ref, own_ref, other_ref, out_ref, total_ref):
    groups, chunk_rows, _ = out_ref.shape
    width = rows_ref.shape[1]
    chunks = width // LANES
    each = chunk_rows // chunks
    chips, both, _ = own_ref.shape
    columns = both // 2
    core = index_ref[0] % 2
    chip = index_ref[0] // 2

    def experts_part(first, second):
        total = None
        for shift in range(chips):
            came = (chip - shift + chips) % chips
            hidden = []
            for pieces in (first, second):
                projected = dot_nt(rows_ref[...], pieces[shift])
                gate_val, up_val = projected[:, :columns], projected[:, columns:]
                hidden.append(jax.nn.gelu(gate_val, approximate=True) * up_val)
            hidden = jnp.concatenate(hidden, axis=1).astype(BF)
            part = dot(hidden, down_ref[pl.ds(pl.multiple_of(came * both, 16), both), :])
            total = part if total is None else total + part
        total_ref[...] = total.astype(BF)

    @pl.when(core == 0)
    def _():
        experts_part(own_ref, other_ref)

    @pl.when(core != 0)
    def _():
        experts_part(other_ref, own_ref)

    for group in range(groups):
        mine = total_ref[group * each : (group + 1) * each]
        stacked = jnp.concatenate([mine[:, at * LANES : (at + 1) * LANES] for at in range(chunks)], axis=0)
        out_ref[group] = dot_tn(order_ref[...], stacked).astype(BF)


def sum_kernel(parts_ref, out_ref):
    total = parts_ref[0].astype(F32)
    for at in range(1, parts_ref.shape[0]):
        total = total + parts_ref[at].astype(F32)
    out_ref[...] = total.astype(BF)


def combine_kernel(experts_ref, after_ref, gates_ref, select_ref, out_ref):
    block, width = after_ref.shape
    chunks = width // LANES
    picked = [dot_tn(select_ref[which], experts_ref[...]) for which in range(2)]
    for at in range(chunks):
        lanes = slice(at * LANES, (at + 1) * LANES)
        mine = slice(at * block, (at + 1) * block)
        total = gates_ref[0] * picked[0][mine] + gates_ref[1] * picked[1][mine]
        out_ref[:, lanes] = (after_ref[:, lanes] + total).astype(BF)


VMEM = pl.BlockSpec(memory_space=pltpu.VMEM)
HBM = pl.BlockSpec(memory_space=pltpu.HBM)
SMEM = pl.BlockSpec(memory_space=pltpu.SMEM)


def in_hbm(array):
    return pltpu.with_memory_space_constraint(array, pltpu.HBM)


LONG = pl.CostEstimate(flops=10**10, transcendentals=0, bytes_accessed=1 << 21)
VERY_LONG = pl.CostEstimate(flops=2 * 10**10, transcendentals=0, bytes_accessed=1 << 21)
PARAMS = pltpu.CompilerParams(vmem_limit_bytes=16 * 1024 * 1024)


def body(
    resid, attn_gain, w_query, w_key, w_value, w_attn_out, cache, cache_lens, seg_ids, ffn_gain, router, routes, w_in, w_out
):
    hid = ("x", "c")
    hid_count = lax.axis_size(hid)
    hid_index = lax.axis_index(hid).astype(jnp.int32).reshape(1)
    group_rows, width = resid.shape
    experts = router.shape[1]
    block = group_rows // hid_count
    capacity = CAPACITY
    chunks = width // LANES
    slot_count = experts * chunks * capacity
    split = lax.axis_size("y")
    w_cols = jnp.transpose(w_in, (0, 2, 1))
    row = lax.axis_size("x")

    operands = (
        resid,
        attn_gain.reshape(1, width),
        w_query,
        w_key,
        w_value,
        w_attn_out,
        cache,
        cache_lens.reshape(1, -1),
        seg_ids,
        ffn_gain.reshape(1, width),
        router.T,
    )
    partial_mix, own, gain, router_rows = pl.pallas_call(
        attention_kernel,
        out_shape=(
            jax.ShapeDtypeStruct((group_rows, width), BF),
            jax.ShapeDtypeStruct((block, width), F32),
            jax.ShapeDtypeStruct((1, width), F32),
            jax.ShapeDtypeStruct((experts, width), BF),
        ),
        in_specs=[SMEM] + [HBM] * len(operands),
        out_specs=(VMEM,) * 4,
        scratch_shapes=[pltpu.VMEM(each.shape, each.dtype) for each in operands[:9]]
        + [pltpu.VMEM((1, group_rows), jnp.int32), pltpu.SemaphoreType.DMA((len(operands),))],
        compiler_params=PARAMS,
        name="attention",
    )(hid_index, *map(in_hbm, operands))
    chosen, select, column = pl.pallas_call(
        routing_kernel,
        out_shape=(
            jax.ShapeDtypeStruct((slot_count, LANES), BF),
            jax.ShapeDtypeStruct((2, slot_count, LANES), BF),
            jax.ShapeDtypeStruct((2, block, LANES), jnp.int32),
        ),
        in_specs=[SMEM, VMEM, VMEM],
        out_specs=(VMEM,) * 3,
        compiler_params=PARAMS,
        name="routing",
    )(hid_index, routes.T, gain)
    column, w_cols = lax.optimization_barrier((column, w_cols))
    moves = [[(at, (at + shift) % row) for at in range(row)] for shift in range(row)]
    own_core = [w_cols] + [lax.ppermute(w_cols, "x", move) for move in moves[1:-1]]
    parts = lax.all_to_all(partial_mix.reshape(hid_count, block, width), hid, 0, 0, tiled=True)
    after, ffn_in = pl.pallas_call(
        mix_kernel,
        out_shape=(jax.ShapeDtypeStruct((block, width), F32), jax.ShapeDtypeStruct((block, width), BF)),
        in_specs=[VMEM] * 3,
        out_specs=(VMEM,) * 2,
        compiler_params=PARAMS,
        cost_estimate=LONG,
        name="mix",
    )(parts, own, gain)
    outgoing = pl.pallas_call(
        dispatch_kernel,
        out_shape=jax.ShapeDtypeStruct((slot_count, LANES), BF),
        in_specs=[VMEM] * 2,
        out_specs=VMEM,
        compiler_params=PARAMS,
        cost_estimate=LONG,
        name="dispatch",
    )(ffn_in, chosen)
    gates = pl.pallas_call(
        gates_kernel,
        out_shape=jax.ShapeDtypeStruct((2, block, LANES), F32),
        in_specs=[VMEM] * 3,
        out_specs=VMEM,
        compiler_params=PARAMS,
        cost_estimate=LONG,
        name="gates",
    )(ffn_in, router_rows, column)
    exchanged = (experts, chunks * CAPACITY, LANES)
    arrived = lax.all_to_all(outgoing.reshape(exchanged), "z", 0, 0, tiled=True)
    order = pl.pallas_call(
        functools.partial(order_kernel, chunks),
        out_shape=jax.ShapeDtypeStruct((slot_count, slot_count), BF),
        in_specs=[VMEM],
        out_specs=VMEM,
        compiler_params=PARAMS,
        name="order",
    )(gates)
    order, *own_core = lax.optimization_barrier((order, *own_core))
    own_core.append(lax.ppermute(own_core[0], "x", moves[-1]))
    spread = pl.pallas_call(
        spread_kernel,
        out_shape=jax.ShapeDtypeStruct((split, slot_count, LANES), BF),
        in_specs=[VMEM],
        out_specs=VMEM,
        compiler_params=PARAMS,
        name="spread",
    )(arrived.reshape(slot_count, LANES))
    tokens = lax.all_to_all(spread, "y", 0, 0, tiled=True)
    own_core = [cols.reshape(-1, width) for cols in own_core]
    stacked = pl.pallas_call(
        stack_kernel,
        out_shape=jax.ShapeDtypeStruct((row,) + own_core[0].shape, BF),
        in_specs=[pl.BlockSpec(memory_space=pl.ANY)] + [VMEM] * row,
        out_specs=VMEM,
        compiler_params=PARAMS,
        name="stack",
    )(spread, *own_core)
    other_core = lax.ppermute(stacked, "c", [(0, 1), (1, 0)])
    rows = pl.pallas_call(
        unpack_kernel,
        out_shape=jax.ShapeDtypeStruct((split * experts * CAPACITY, width), BF),
        in_specs=[VMEM] * 2,
        out_specs=VMEM,
        compiler_params=PARAMS,
        cost_estimate=VERY_LONG,
        name="unpack",
    )(tokens, order)
    projected = pl.pallas_call(
        ffn_kernel,
        out_shape=jax.ShapeDtypeStruct((split, slot_count, LANES), BF),
        in_specs=[SMEM] + [VMEM] * 5,
        out_specs=VMEM,
        scratch_shapes=[pltpu.VMEM((split * experts * CAPACITY, width), BF)],
        compiler_params=PARAMS,
        name="ffn",
    )(hid_index, rows, order, w_out, stacked, other_core)
    quarters = lax.all_to_all(projected, "y", 0, 0, tiled=True)
    summed = pl.pallas_call(
        sum_kernel,
        out_shape=jax.ShapeDtypeStruct((slot_count, LANES), BF),
        in_specs=[VMEM],
        out_specs=VMEM,
        compiler_params=PARAMS,
        name="sum_quarters",
    )(quarters)
    returned = lax.all_to_all(summed.reshape(exchanged), "z", 0, 0, tiled=True)
    return pl.pallas_call(
        combine_kernel,
        out_shape=jax.ShapeDtypeStruct((block, width), BF),
        in_specs=[VMEM] * 4,
        out_specs=VMEM,
        compiler_params=PARAMS,
        name="combine",
    )(returned.reshape(slot_count, LANES), after, gates, select)


def solution(mesh):
    fine = Mesh(mesh.devices.reshape(16, 4, 4, 2), ("z", "y", "x", "c"))
    req = ("z", "y")
    hid = ("x", "c")
    in_specs = (
        P(req, None),
        P(),
        P(None, hid),
        P(None, hid),
        P(None, hid),
        P(hid, None),
        P(req, None, None, hid),
        P(req),
        P(req, None),
        P(),
        P(),
        P(req, None),
        P(None, None, req + hid),
        P(req, None),
    )
    out_specs = P(req + hid, None)
    return jax.shard_map(body, mesh=fine, in_specs=in_specs, out_specs=out_specs, check_vma=False)
```

```python
import functools

import jax
import jax.numpy as jnp
from jax import lax
from jax.experimental import pallas as pl
from jax.experimental.pallas import tpu as pltpu
from jax.sharding import Mesh
from jax.sharding import PartitionSpec as P

HDIM = 64
EPS = 1e-06
BF = jnp.bfloat16
F32 = jnp.float32
LANES = 128
CAPACITY = 3


def dot(a, b):
    return jnp.dot(a, b, preferred_element_type=F32)


def dot_nt(a, b):
    return lax.dot_general(a, b, (((1,), (1,)), ((), ())), preferred_element_type=F32)


def dot_tn(a, b):
    return lax.dot_general(a, b, (((0,), (0,)), ((), ())), preferred_element_type=F32)


def iota(shape, dim):
    return lax.broadcasted_iota(jnp.int32, shape, dim)


def to_column(row, size):
    diagonal = iota((size, size), 0) == iota((size, size), 1)
    return jnp.sum(jnp.where(diagonal, jnp.broadcast_to(row, (size, size)), 0), axis=1, keepdims=True)


def attention_kernel(
    index_ref, resid_hbm, gain_hbm, wq_hbm, wk_hbm, wv_hbm, wo_hbm, cache_hbm, lens_hbm, seg_hbm,
    ffn_gain_hbm, router_hbm, out_ref, own_ref, ffn_gain_ref, router_ref,
    resid_ref, gain_ref, wq_ref, wk_ref, wv_ref, wo_ref, cache_ref, lens_ref, seg_ref, seg_row, sems
):
    sources = (
        resid_hbm, gain_hbm, wq_hbm, wk_hbm, wv_hbm, seg_hbm, lens_hbm, cache_hbm, wo_hbm, ffn_gain_hbm, router_hbm
    )
    targets = (
        resid_ref, gain_ref, wq_ref, wk_ref, wv_ref, seg_ref, lens_ref, cache_ref, wo_ref, ffn_gain_ref, router_ref
    )
    copies = [pltpu.make_async_copy(a, b, sems.at[i]) for i, (a, b) in enumerate(zip(sources, targets))]
    for copy in copies:
        copy.start()
    total = resid_ref.shape[0]
    packed = seg_ref.shape[1]
    decoded, _, slots, width = cache_ref.shape
    heads = width // HDIM
    scale = HDIM ** (-0.5)
    copies[0].wait()
    copies[1].wait()
    x = resid_ref[...].astype(F32)
    inverse = lax.rsqrt(jnp.mean(x * x, axis=-1, keepdims=True) + EPS)
    normed = (x * inverse * gain_ref[...]).astype(BF)
    copies[2].wait()
    query = dot(normed, wq_ref[...]).astype(BF)
    copies[3].wait()
    keys = dot(normed, wk_ref[...]).astype(BF)
    copies[4].wait()
    values = dot(normed, wv_ref[...]).astype(BF)
    copies[5].wait()
    copies[6].wait()
    copies[7].wait()

    seg_row[...] = iota((1, total), 1) + (1 << 20)
    seg_row[:, :packed] = seg_ref[...]
    segments = seg_row[...]
    allowed = (iota((total, total), 1) <= iota((total, total), 0)) & (to_column(segments, total) == segments)
    lengths = to_column(lens_ref[...], decoded)
    slot_at = iota((decoded, decoded * slots), 1)
    own_cache = (slot_at // slots == iota((decoded, decoded * slots), 0)) & (slot_at % slots < lengths)

    cached_keys = cache_ref[:, 0].reshape(decoded * slots, width)
    cached_values = cache_ref[:, 1].reshape(decoded * slots, width)
    lane_head = iota((total, width), 1) // HDIM
    context = jnp.zeros((total, width), F32)
    for head in range(heads):
        mine = lane_head == head
        head_query = jnp.where(mine, query, jnp.zeros_like(query))
        scores = jnp.where(allowed, dot_nt(head_query, keys) * scale, -jnp.inf)
        highest = jnp.max(scores, axis=-1, keepdims=True)
        cached = jnp.where(own_cache, dot_nt(head_query[packed:], cached_keys) * scale, -jnp.inf)
        top_dec = jnp.maximum(highest[packed:], jnp.max(cached, axis=-1, keepdims=True))
        highest = jnp.concatenate([highest[:packed], top_dec], axis=0)
        weights = jnp.exp(scores - highest)
        weights_cache = jnp.exp(cached - top_dec)
        norm = jnp.sum(weights, axis=-1, keepdims=True)
        norm_dec = norm[packed:] + jnp.sum(weights_cache, axis=-1, keepdims=True)
        norm = jnp.concatenate([norm[:packed], norm_dec], axis=0)
        part = dot((weights / norm).astype(BF), values)
        part_cache = dot((weights_cache / norm_dec).astype(BF), cached_values)
        part = jnp.concatenate([part[:packed], part[packed:] + part_cache], axis=0)
        context = jnp.where(mine, part, context)
    copies[8].wait()
    out_ref[...] = dot(context.astype(BF), wo_ref[...]).astype(out_ref.dtype)

    block = own_ref.shape[0]
    index = index_ref[0]
    own_ref[...] = resid_ref[pl.ds(pl.multiple_of(index * block, block), block), :].astype(F32)
    copies[9].wait()
    copies[10].wait()


def own_routes(routes_ref, which, index, block):
    lane = iota((1, LANES), 1)
    row = pltpu.roll(routes_ref[pl.ds(which, 1), :], (LANES - index * block) % LANES, 1)
    size = block
    while size < LANES:
        row = jnp.where(lane < size, row, pltpu.roll(row, size, 1))
        size *= 2
    return row


def placement(row, columns, block, capacity):
    token = iota((block, LANES), 1) % block
    before = iota((block, LANES), 0) < token
    slot = jnp.zeros((1, LANES), jnp.int32)
    for column in columns:
        slot = slot + jnp.sum(((column == row) & before).astype(jnp.int32), axis=0, keepdims=True)
    return row * capacity + slot


def slot_rows(rows, capacity, chunks):
    at = iota((rows, LANES), 0)
    expert = at // (chunks * capacity)
    rest = at - expert * (chunks * capacity)
    chunk = rest // capacity
    return expert * capacity + rest - chunk * capacity, chunk


def route_columns(rows, block):
    size = (block, LANES)
    diagonal = iota(size, 0) == iota(size, 1)
    return [
        jnp.sum(jnp.where(diagonal, jnp.broadcast_to(row, size), 0), axis=1, keepdims=True) for row in rows
    ]


def routing_kernel(index_ref, routes_ref, gain_ref, chosen_ref, select_ref, column_ref):
    block = column_ref.shape[1]
    chunks = gain_ref.shape[1] // LANES
    rows = [own_routes(routes_ref, which, index_ref[0], block) for which in range(2)]
    columns = route_columns(rows, block)
    wanted, chunk = slot_rows(chosen_ref.shape[0], CAPACITY, chunks)
    same = chunk == iota(chunk.shape, 1) // block
    both = None
    for which in range(2):
        target = placement(rows[which], columns, block, CAPACITY)
        here = jnp.where(same & (wanted == target), 1.0, 0.0)
        select_ref[which] = here.astype(BF)
        both = here if both is None else both + here
        column_ref[which] = jnp.broadcast_to(columns[which], (block, LANES))
    chosen_ref[...] = both.astype(BF)


def mix_kernel(parts_ref, own_ref, gain_ref, after_ref, ffn_in_ref):
    mixed = parts_ref[0].astype(F32)
    for source in range(1, parts_ref.shape[0]):
        mixed = mixed + parts_ref[source].astype(F32)
    after = own_ref[...] + mixed
    after_ref[...] = after
    inverse = lax.rsqrt(jnp.mean(after * after, axis=-1, keepdims=True) + EPS)
    ffn_in_ref[...] = (after * inverse * gain_ref[...]).astype(BF)


def dispatch_kernel(ffn_in_ref, chosen_ref, out_ref):
    chunks = ffn_in_ref.shape[1] // LANES
    stacked = jnp.concatenate([ffn_in_ref[:, at * LANES : (at + 1) * LANES] for at in range(chunks)], axis=0)
    out_ref[...] = dot(chosen_ref[...], stacked).astype(BF)


def gates_kernel(ffn_in_ref, router_ref, column_ref, gates_ref):
    block = ffn_in_ref.shape[0]
    experts = router_ref.shape[0]
    logits = dot_nt(ffn_in_ref[...], router_ref[...])
    expert_at = iota((block, experts), 1)
    for which in range(2):
        mine = expert_at == column_ref[which][:, :experts]
        picked = jnp.sum(jnp.where(mine, logits, 0.0), axis=1, keepdims=True)
        gates_ref[which] = jnp.broadcast_to(jax.nn.sigmoid(picked), (block, LANES))


def order_kernel(chunks, tokens_ref, order_ref):
    chunk_rows = order_ref.shape[0]
    each = chunk_rows // chunks
    at = iota((chunk_rows, chunk_rows), 0)
    chunk = at // each
    rest = at - chunk * each
    source = rest // CAPACITY
    wanted = source * (chunks * CAPACITY) + chunk * CAPACITY + rest - source * CAPACITY
    order_ref[...] = jnp.where(wanted == iota((chunk_rows, chunk_rows), 1), 1.0, 0.0).astype(BF)


def spread_kernel(tokens_ref, out_ref):
    for at in range(out_ref.shape[0]):
        out_ref[at] = tokens_ref[...]


def stack_kernel(spread_ref, *refs):
    *pieces, out_ref = refs
    for at, piece in enumerate(pieces):
        out_ref[at] = piece[...]


def hidden_of(rows, piece):
    columns = piece.shape[0] // 2
    projected = dot_nt(rows, piece)
    gate_val, up_val = projected[:, :columns], projected[:, columns:]
    return (jax.nn.gelu(gate_val, approximate=True) * up_val).astype(BF)


def own_kernel(tokens_hbm, order_ref, own_ref, rows_ref, hidden_ref, tokens_ref, sems):
    groups, chunk_rows, _ = tokens_ref.shape
    copies = [pltpu.make_async_copy(tokens_hbm.at[at], tokens_ref.at[at], sems.at[at]) for at in range(groups)]
    for copy in copies:
        copy.start()
    chunks = rows_ref.shape[1] // LANES
    each = chunk_rows // chunks
    for group in range(groups):
        copies[group].wait()
        unpacked = dot(order_ref[...], tokens_ref[group]).astype(BF)
        for at in range(chunks):
            rows_ref[group * each : (group + 1) * each, at * LANES : (at + 1) * LANES] = unpacked[
                at * each : (at + 1) * each
            ]
    for shift in range(own_ref.shape[0]):
        hidden_ref[shift] = hidden_of(rows_ref[...], own_ref[shift])


def ffn_kernel(index_ref, rows_ref, order_ref, down_ref, own_hidden_ref, other_hbm, out_ref, total_ref, other_ref, sems):
    chips, both, _ = other_ref.shape
    copies = [pltpu.make_async_copy(other_hbm.at[at], other_ref.at[at], sems.at[at]) for at in range(chips)]
    for copy in copies:
        copy.start()
    groups, chunk_rows, _ = out_ref.shape
    width = rows_ref.shape[1]
    chunks = width // LANES
    each = chunk_rows // chunks
    core = index_ref[0] % 2
    chip = index_ref[0] // 2

    def experts_part(own_first):
        total = None
        for shift in range(chips):
            came = (chip - shift + chips) % chips
            copies[shift].wait()
            pair = [own_hidden_ref[shift], hidden_of(rows_ref[...], other_ref[shift])]
            hidden = jnp.concatenate(pair if own_first else pair[::-1], axis=1)
            part = dot(hidden, down_ref[pl.ds(pl.multiple_of(came * both, 16), both), :])
            total = part if total is None else total + part
        total_ref[...] = total.astype(BF)

    @pl.when(core == 0)
    def _():
        experts_part(True)

    @pl.when(core != 0)
    def _():
        experts_part(False)

    for group in range(groups):
        mine = total_ref[group * each : (group + 1) * each]
        stacked = jnp.concatenate([mine[:, at * LANES : (at + 1) * LANES] for at in range(chunks)], axis=0)
        out_ref[group] = dot_tn(order_ref[...], stacked).astype(BF)


def sum_kernel(parts_ref, out_ref):
    total = parts_ref[0].astype(F32)
    for at in range(1, parts_ref.shape[0]):
        total = total + parts_ref[at].astype(F32)
    out_ref[...] = total.astype(BF)


def combine_kernel(experts_ref, after_ref, gates_ref, select_ref, out_ref):
    block, width = after_ref.shape
    chunks = width // LANES
    picked = [dot_tn(select_ref[which], experts_ref[...]) for which in range(2)]
    for at in range(chunks):
        lanes = slice(at * LANES, (at + 1) * LANES)
        mine = slice(at * block, (at + 1) * block)
        total = gates_ref[0] * picked[0][mine] + gates_ref[1] * picked[1][mine]
        out_ref[:, lanes] = (after_ref[:, lanes] + total).astype(BF)


VMEM = pl.BlockSpec(memory_space=pltpu.VMEM)
HBM = pl.BlockSpec(memory_space=pltpu.HBM)
SMEM = pl.BlockSpec(memory_space=pltpu.SMEM)


def in_hbm(array):
    return pltpu.with_memory_space_constraint(array, pltpu.HBM)


LONG = pl.CostEstimate(flops=10**10, transcendentals=0, bytes_accessed=1 << 21)
VERY_LONG = pl.CostEstimate(flops=2 * 10**10, transcendentals=0, bytes_accessed=1 << 21)
PARAMS = pltpu.CompilerParams(vmem_limit_bytes=16 * 1024 * 1024)


def body(
    resid, attn_gain, w_query, w_key, w_value, w_attn_out, cache, cache_lens, seg_ids, ffn_gain, router, routes, w_in, w_out
):
    hid = ("x", "c")
    hid_count = lax.axis_size(hid)
    hid_index = lax.axis_index(hid).astype(jnp.int32).reshape(1)
    group_rows, width = resid.shape
    experts = router.shape[1]
    block = group_rows // hid_count
    capacity = CAPACITY
    chunks = width // LANES
    slot_count = experts * chunks * capacity
    split = lax.axis_size("y")
    w_cols = jnp.transpose(w_in, (0, 2, 1))
    row = lax.axis_size("x")

    operands = (
        resid,
        attn_gain.reshape(1, width),
        w_query,
        w_key,
        w_value,
        w_attn_out,
        cache,
        cache_lens.reshape(1, -1),
        seg_ids,
        ffn_gain.reshape(1, width),
        router.T,
    )
    partial_mix, own, gain, router_rows = pl.pallas_call(
        attention_kernel,
        out_shape=(
            jax.ShapeDtypeStruct((group_rows, width), BF),
            jax.ShapeDtypeStruct((block, width), F32),
            jax.ShapeDtypeStruct((1, width), F32),
            jax.ShapeDtypeStruct((experts, width), BF),
        ),
        in_specs=[SMEM] + [HBM] * len(operands),
        out_specs=(VMEM,) * 4,
        scratch_shapes=[pltpu.VMEM(each.shape, each.dtype) for each in operands[:9]]
        + [pltpu.VMEM((1, group_rows), jnp.int32), pltpu.SemaphoreType.DMA((len(operands),))],
        compiler_params=PARAMS,
        name="attention",
    )(hid_index, *map(in_hbm, operands))
    chosen, select, column = pl.pallas_call(
        routing_kernel,
        out_shape=(
            jax.ShapeDtypeStruct((slot_count, LANES), BF),
            jax.ShapeDtypeStruct((2, slot_count, LANES), BF),
            jax.ShapeDtypeStruct((2, block, LANES), jnp.int32),
        ),
        in_specs=[SMEM, VMEM, VMEM],
        out_specs=(VMEM,) * 3,
        compiler_params=PARAMS,
        name="routing",
    )(hid_index, routes.T, gain)
    column, w_cols = lax.optimization_barrier((column, w_cols))
    moves = [[(at, (at + shift) % row) for at in range(row)] for shift in range(row)]
    own_core = [w_cols] + [lax.ppermute(w_cols, "x", move) for move in moves[1:-1]]
    parts = lax.all_to_all(partial_mix.reshape(hid_count, block, width), hid, 0, 0, tiled=True)
    after, ffn_in = pl.pallas_call(
        mix_kernel,
        out_shape=(jax.ShapeDtypeStruct((block, width), F32), jax.ShapeDtypeStruct((block, width), BF)),
        in_specs=[VMEM] * 3,
        out_specs=(VMEM,) * 2,
        compiler_params=PARAMS,
        cost_estimate=LONG,
        name="mix",
    )(parts, own, gain)
    outgoing = pl.pallas_call(
        dispatch_kernel,
        out_shape=jax.ShapeDtypeStruct((slot_count, LANES), BF),
        in_specs=[VMEM] * 2,
        out_specs=VMEM,
        compiler_params=PARAMS,
        cost_estimate=LONG,
        name="dispatch",
    )(ffn_in, chosen)
    gates = pl.pallas_call(
        gates_kernel,
        out_shape=jax.ShapeDtypeStruct((2, block, LANES), F32),
        in_specs=[VMEM] * 3,
        out_specs=VMEM,
        compiler_params=PARAMS,
        cost_estimate=LONG,
        name="gates",
    )(ffn_in, router_rows, column)
    exchanged = (experts, chunks * CAPACITY, LANES)
    arrived = lax.all_to_all(outgoing.reshape(exchanged), "z", 0, 0, tiled=True)
    order = pl.pallas_call(
        functools.partial(order_kernel, chunks),
        out_shape=jax.ShapeDtypeStruct((slot_count, slot_count), BF),
        in_specs=[VMEM],
        out_specs=VMEM,
        compiler_params=PARAMS,
        name="order",
    )(gates)
    order, *own_core = lax.optimization_barrier((order, *own_core))
    own_core.append(lax.ppermute(own_core[0], "x", moves[-1]))
    spread = pl.pallas_call(
        spread_kernel,
        out_shape=jax.ShapeDtypeStruct((split, slot_count, LANES), BF),
        in_specs=[VMEM],
        out_specs=VMEM,
        compiler_params=PARAMS,
        name="spread",
    )(arrived.reshape(slot_count, LANES))
    tokens = lax.all_to_all(spread, "y", 0, 0, tiled=True)
    own_core = [cols.reshape(-1, width) for cols in own_core]
    stacked = pl.pallas_call(
        stack_kernel,
        out_shape=jax.ShapeDtypeStruct((row,) + own_core[0].shape, BF),
        in_specs=[pl.BlockSpec(memory_space=pl.ANY)] + [VMEM] * row,
        out_specs=VMEM,
        compiler_params=PARAMS,
        name="stack",
    )(spread, *own_core)
    other_core = lax.ppermute(stacked, "c", [(0, 1), (1, 0)])
    rows, own_hidden = pl.pallas_call(
        own_kernel,
        out_shape=(
            jax.ShapeDtypeStruct((split * experts * CAPACITY, width), BF),
            jax.ShapeDtypeStruct((row, split * experts * CAPACITY, w_in.shape[2]), BF),
        ),
        in_specs=[HBM, VMEM, VMEM],
        out_specs=(VMEM,) * 2,
        scratch_shapes=[pltpu.VMEM(spread.shape, BF), pltpu.SemaphoreType.DMA((split,))],
        compiler_params=PARAMS,
        cost_estimate=VERY_LONG,
        name="own",
    )(in_hbm(tokens), order, stacked)
    projected = pl.pallas_call(
        ffn_kernel,
        out_shape=jax.ShapeDtypeStruct((split, slot_count, LANES), BF),
        in_specs=[SMEM] + [VMEM] * 4 + [HBM],
        out_specs=VMEM,
        scratch_shapes=[
            pltpu.VMEM((split * experts * CAPACITY, width), BF),
            pltpu.VMEM(stacked.shape, BF),
            pltpu.SemaphoreType.DMA((row,)),
        ],
        compiler_params=PARAMS,
        name="ffn",
    )(hid_index, rows, order, w_out, own_hidden, in_hbm(other_core))
    quarters = lax.all_to_all(projected, "y", 0, 0, tiled=True)
    summed = pl.pallas_call(
        sum_kernel,
        out_shape=jax.ShapeDtypeStruct((slot_count, LANES), BF),
        in_specs=[VMEM],
        out_specs=VMEM,
        compiler_params=PARAMS,
        name="sum_quarters",
    )(quarters)
    returned = lax.all_to_all(summed.reshape(exchanged), "z", 0, 0, tiled=True)
    return pl.pallas_call(
        combine_kernel,
        out_shape=jax.ShapeDtypeStruct((block, width), BF),
        in_specs=[VMEM] * 4,
        out_specs=VMEM,
        compiler_params=PARAMS,
        name="combine",
    )(returned.reshape(slot_count, LANES), after, gates, select)


def solution(mesh):
    fine = Mesh(mesh.devices.reshape(16, 4, 4, 2), ("z", "y", "x", "c"))
    req = ("z", "y")
    hid = ("x", "c")
    in_specs = (
        P(req, None),
        P(),
        P(None, hid),
        P(None, hid),
        P(None, hid),
        P(hid, None),
        P(req, None, None, hid),
        P(req),
        P(req, None),
        P(),
        P(),
        P(req, None),
        P(None, None, req + hid),
        P(req, None),
    )
    out_specs = P(req + hid, None)
    return jax.shard_map(body, mesh=fine, in_specs=in_specs, out_specs=out_specs, check_vma=False)
```

```python
import functools

import jax
import jax.numpy as jnp
from jax import lax
from jax.experimental import pallas as pl
from jax.experimental.pallas import tpu as pltpu
from jax.sharding import Mesh
from jax.sharding import PartitionSpec as P

HDIM = 64
EPS = 1e-06
BF = jnp.bfloat16
F32 = jnp.float32
LANES = 128
CAPACITY = 3


def dot(a, b):
    return jnp.dot(a, b, preferred_element_type=F32)


def dot_nt(a, b):
    return lax.dot_general(a, b, (((1,), (1,)), ((), ())), preferred_element_type=F32)


def dot_tn(a, b):
    return lax.dot_general(a, b, (((0,), (0,)), ((), ())), preferred_element_type=F32)


def iota(shape, dim):
    return lax.broadcasted_iota(jnp.int32, shape, dim)


def to_column(row, size):
    diagonal = iota((size, size), 0) == iota((size, size), 1)
    return jnp.sum(jnp.where(diagonal, jnp.broadcast_to(row, (size, size)), 0), axis=1, keepdims=True)


def attention_kernel(
    index_ref, resid_hbm, gain_hbm, wq_hbm, wk_hbm, wv_hbm, wo_hbm, cache_hbm, lens_hbm, seg_hbm,
    ffn_gain_hbm, router_hbm, out_ref, own_ref, ffn_gain_ref, router_ref,
    resid_ref, gain_ref, wq_ref, wk_ref, wv_ref, wo_ref, cache_ref, lens_ref, seg_ref, seg_row, sems
):
    sources = (
        resid_hbm, gain_hbm, wq_hbm, wk_hbm, wv_hbm, seg_hbm, lens_hbm, cache_hbm, wo_hbm, ffn_gain_hbm, router_hbm
    )
    targets = (
        resid_ref, gain_ref, wq_ref, wk_ref, wv_ref, seg_ref, lens_ref, cache_ref, wo_ref, ffn_gain_ref, router_ref
    )
    copies = [pltpu.make_async_copy(a, b, sems.at[i]) for i, (a, b) in enumerate(zip(sources, targets))]
    for copy in copies:
        copy.start()
    total = resid_ref.shape[0]
    packed = seg_ref.shape[1]
    decoded, _, slots, width = cache_ref.shape
    heads = width // HDIM
    scale = HDIM ** (-0.5)
    copies[0].wait()
    copies[1].wait()
    x = resid_ref[...].astype(F32)
    inverse = lax.rsqrt(jnp.mean(x * x, axis=-1, keepdims=True) + EPS)
    normed = (x * inverse * gain_ref[...]).astype(BF)
    copies[2].wait()
    query = dot(normed, wq_ref[...]).astype(BF)
    copies[3].wait()
    keys = dot(normed, wk_ref[...]).astype(BF)
    copies[4].wait()
    values = dot(normed, wv_ref[...]).astype(BF)
    copies[5].wait()
    copies[6].wait()
    copies[7].wait()

    seg_row[...] = iota((1, total), 1) + (1 << 20)
    seg_row[:, :packed] = seg_ref[...]
    segments = seg_row[...]
    allowed = (iota((total, total), 1) <= iota((total, total), 0)) & (to_column(segments, total) == segments)
    lengths = to_column(lens_ref[...], decoded)
    slot_at = iota((decoded, decoded * slots), 1)
    own_cache = (slot_at // slots == iota((decoded, decoded * slots), 0)) & (slot_at % slots < lengths)

    cached_keys = cache_ref[:, 0].reshape(decoded * slots, width)
    cached_values = cache_ref[:, 1].reshape(decoded * slots, width)
    lane_head = iota((total, width), 1) // HDIM
    context = jnp.zeros((total, width), F32)
    for head in range(heads):
        mine = lane_head == head
        head_query = jnp.where(mine, query, jnp.zeros_like(query))
        scores = jnp.where(allowed, dot_nt(head_query, keys) * scale, -jnp.inf)
        highest = jnp.max(scores, axis=-1, keepdims=True)
        cached = jnp.where(own_cache, dot_nt(head_query[packed:], cached_keys) * scale, -jnp.inf)
        top_dec = jnp.maximum(highest[packed:], jnp.max(cached, axis=-1, keepdims=True))
        highest = jnp.concatenate([highest[:packed], top_dec], axis=0)
        weights = jnp.exp(scores - highest)
        weights_cache = jnp.exp(cached - top_dec)
        norm = jnp.sum(weights, axis=-1, keepdims=True)
        norm_dec = norm[packed:] + jnp.sum(weights_cache, axis=-1, keepdims=True)
        norm = jnp.concatenate([norm[:packed], norm_dec], axis=0)
        part = dot((weights / norm).astype(BF), values)
        part_cache = dot((weights_cache / norm_dec).astype(BF), cached_values)
        part = jnp.concatenate([part[:packed], part[packed:] + part_cache], axis=0)
        context = jnp.where(mine, part, context)
    copies[8].wait()
    out_ref[...] = dot(context.astype(BF), wo_ref[...]).astype(out_ref.dtype)

    block = own_ref.shape[0]
    index = index_ref[0]
    own_ref[...] = resid_ref[pl.ds(pl.multiple_of(index * block, block), block), :].astype(F32)
    copies[9].wait()
    copies[10].wait()


def own_routes(routes_ref, which, index, block):
    lane = iota((1, LANES), 1)
    row = pltpu.roll(routes_ref[pl.ds(which, 1), :], (LANES - index * block) % LANES, 1)
    size = block
    while size < LANES:
        row = jnp.where(lane < size, row, pltpu.roll(row, size, 1))
        size *= 2
    return row


def placement(row, columns, block, capacity):
    token = iota((block, LANES), 1) % block
    before = iota((block, LANES), 0) < token
    slot = jnp.zeros((1, LANES), jnp.int32)
    for column in columns:
        slot = slot + jnp.sum(((column == row) & before).astype(jnp.int32), axis=0, keepdims=True)
    return row * capacity + slot


def slot_rows(rows, capacity, chunks):
    at = iota((rows, LANES), 0)
    expert = at // (chunks * capacity)
    rest = at - expert * (chunks * capacity)
    chunk = rest // capacity
    return expert * capacity + rest - chunk * capacity, chunk


def route_columns(rows, block):
    size = (block, LANES)
    diagonal = iota(size, 0) == iota(size, 1)
    return [
        jnp.sum(jnp.where(diagonal, jnp.broadcast_to(row, size), 0), axis=1, keepdims=True) for row in rows
    ]


def routing_kernel(index_ref, routes_ref, gain_ref, chosen_ref, target_ref, column_ref):
    block = column_ref.shape[1]
    chunks = gain_ref.shape[1] // LANES
    rows = [own_routes(routes_ref, which, index_ref[0], block) for which in range(2)]
    columns = route_columns(rows, block)
    wanted, chunk = slot_rows(chosen_ref.shape[0], CAPACITY, chunks)
    same = chunk == iota(chunk.shape, 1) // block
    both = None
    for which in range(2):
        target = placement(rows[which], columns, block, CAPACITY)
        here = jnp.where(same & (wanted == target), 1.0, 0.0)
        target_ref[pl.ds(which, 1), :] = target
        both = here if both is None else both + here
        column_ref[which] = jnp.broadcast_to(columns[which], (block, LANES))
    chosen_ref[...] = both.astype(BF)


def residual(parts_ref, own_ref):
    mixed = parts_ref[0].astype(F32)
    for source in range(1, parts_ref.shape[0]):
        mixed = mixed + parts_ref[source].astype(F32)
    return own_ref[...] + mixed


def mix_kernel(parts_ref, own_ref, gain_ref, ffn_in_ref):
    after = residual(parts_ref, own_ref)
    inverse = lax.rsqrt(jnp.mean(after * after, axis=-1, keepdims=True) + EPS)
    ffn_in_ref[...] = (after * inverse * gain_ref[...]).astype(BF)


def dispatch_kernel(ffn_in_ref, chosen_ref, out_ref):
    chunks = ffn_in_ref.shape[1] // LANES
    stacked = jnp.concatenate([ffn_in_ref[:, at * LANES : (at + 1) * LANES] for at in range(chunks)], axis=0)
    out_ref[...] = dot(chosen_ref[...], stacked).astype(BF)


def gates_kernel(ffn_in_ref, router_ref, column_ref, parts_ref, own_ref, gates_ref, after_ref):
    after_ref[...] = residual(parts_ref, own_ref)
    block = ffn_in_ref.shape[0]
    experts = router_ref.shape[0]
    logits = dot_nt(ffn_in_ref[...], router_ref[...])
    expert_at = iota((block, experts), 1)
    for which in range(2):
        mine = expert_at == column_ref[which][:, :experts]
        picked = jnp.sum(jnp.where(mine, logits, 0.0), axis=1, keepdims=True)
        gates_ref[which] = jnp.broadcast_to(jax.nn.sigmoid(picked), (block, LANES))


def order_kernel(chunks, tokens_ref, order_ref):
    chunk_rows = order_ref.shape[0]
    each = chunk_rows // chunks
    at = iota((chunk_rows, chunk_rows), 0)
    chunk = at // each
    rest = at - chunk * each
    source = rest // CAPACITY
    wanted = source * (chunks * CAPACITY) + chunk * CAPACITY + rest - source * CAPACITY
    order_ref[...] = jnp.where(wanted == iota((chunk_rows, chunk_rows), 1), 1.0, 0.0).astype(BF)


def spread_kernel(tokens_ref, out_ref):
    for at in range(out_ref.shape[0]):
        out_ref[at] = tokens_ref[...]


def stack_kernel(spread_ref, *refs):
    *pieces, out_ref = refs
    for at, piece in enumerate(pieces):
        out_ref[at] = piece[...]


def hidden_of(rows, piece):
    columns = piece.shape[0] // 2
    projected = dot_nt(rows, piece)
    gate_val, up_val = projected[:, :columns], projected[:, columns:]
    return (jax.nn.gelu(gate_val, approximate=True) * up_val).astype(BF)


def own_kernel(tokens_hbm, order_ref, own_ref, down_hbm, rows_ref, hidden_ref, down_ref, tokens_ref, sems, sem):
    copies = [pltpu.make_async_copy(tokens_hbm.at[at], tokens_ref.at[at], sems.at[at]) for at in range(tokens_ref.shape[0])]
    for copy in copies:
        copy.start()
    fetch = pltpu.make_async_copy(down_hbm, down_ref, sem)
    fetch.start()
    groups, chunk_rows, _ = tokens_ref.shape
    chunks = rows_ref.shape[1] // LANES
    each = chunk_rows // chunks
    for group in range(groups):
        copies[group].wait()
        unpacked = dot(order_ref[...], tokens_ref[group]).astype(BF)
        for at in range(chunks):
            rows_ref[group * each : (group + 1) * each, at * LANES : (at + 1) * LANES] = unpacked[
                at * each : (at + 1) * each
            ]
    for shift in range(own_ref.shape[0]):
        hidden_ref[shift] = hidden_of(rows_ref[...], own_ref[shift])
    fetch.wait()


def ffn_kernel(index_ref, rows_ref, order_ref, down_ref, own_hidden_ref, other_ref, out_ref, total_ref):
    chips, both, _ = other_ref.shape
    groups, chunk_rows, _ = out_ref.shape
    width = rows_ref.shape[1]
    chunks = width // LANES
    each = chunk_rows // chunks
    core = index_ref[0] % 2
    chip = index_ref[0] // 2

    def experts_part(own_first):
        total = None
        for shift in range(chips):
            came = (chip - shift + chips) % chips
            pair = [own_hidden_ref[shift], hidden_of(rows_ref[...], other_ref[shift])]
            hidden = jnp.concatenate(pair if own_first else pair[::-1], axis=1)
            part = dot(hidden, down_ref[pl.ds(pl.multiple_of(came * both, 16), both), :])
            total = part if total is None else total + part
        total_ref[...] = total.astype(BF)

    @pl.when(core == 0)
    def _():
        experts_part(True)

    @pl.when(core != 0)
    def _():
        experts_part(False)

    for group in range(groups):
        mine = total_ref[group * each : (group + 1) * each]
        stacked = jnp.concatenate([mine[:, at * LANES : (at + 1) * LANES] for at in range(chunks)], axis=0)
        out_ref[group] = dot_tn(order_ref[...], stacked).astype(BF)


def sum_kernel(parts_ref, out_ref):
    total = parts_ref[0].astype(F32)
    for at in range(1, parts_ref.shape[0]):
        total = total + parts_ref[at].astype(F32)
    out_ref[...] = total.astype(BF)


def combine_kernel(experts_ref, after_ref, gates_ref, target_ref, out_ref):
    block, width = after_ref.shape
    chunks = width // LANES
    wanted, chunk = slot_rows(experts_ref.shape[0], CAPACITY, chunks)
    same = chunk == iota(chunk.shape, 1) // block
    picked = []
    for which in range(2):
        chosen = same & (wanted == target_ref[pl.ds(which, 1), :])
        picked.append(dot_tn(jnp.where(chosen, 1.0, 0.0).astype(BF), experts_ref[...]))
    for at in range(chunks):
        lanes = slice(at * LANES, (at + 1) * LANES)
        mine = slice(at * block, (at + 1) * block)
        total = gates_ref[0] * picked[0][mine] + gates_ref[1] * picked[1][mine]
        out_ref[:, lanes] = (after_ref[:, lanes] + total).astype(BF)


VMEM = pl.BlockSpec(memory_space=pltpu.VMEM)
HBM = pl.BlockSpec(memory_space=pltpu.HBM)
SMEM = pl.BlockSpec(memory_space=pltpu.SMEM)


def in_hbm(array):
    return pltpu.with_memory_space_constraint(array, pltpu.HBM)


LONG = pl.CostEstimate(flops=10**10, transcendentals=0, bytes_accessed=1 << 21)
VERY_LONG = pl.CostEstimate(flops=2 * 10**10, transcendentals=0, bytes_accessed=1 << 21)
PARAMS = pltpu.CompilerParams(vmem_limit_bytes=16 * 1024 * 1024)


def body(
    resid, attn_gain, w_query, w_key, w_value, w_attn_out, cache, cache_lens, seg_ids, ffn_gain, router, routes, w_in, w_out
):
    hid = ("x", "c")
    hid_count = lax.axis_size(hid)
    hid_index = lax.axis_index(hid).astype(jnp.int32).reshape(1)
    group_rows, width = resid.shape
    experts = router.shape[1]
    block = group_rows // hid_count
    capacity = CAPACITY
    chunks = width // LANES
    slot_count = experts * chunks * capacity
    split = lax.axis_size("y")
    w_cols = jnp.transpose(w_in, (0, 2, 1))
    row = lax.axis_size("x")

    operands = (
        resid,
        attn_gain.reshape(1, width),
        w_query,
        w_key,
        w_value,
        w_attn_out,
        cache,
        cache_lens.reshape(1, -1),
        seg_ids,
        ffn_gain.reshape(1, width),
        router.T,
    )
    partial_mix, own, gain, router_rows = pl.pallas_call(
        attention_kernel,
        out_shape=(
            jax.ShapeDtypeStruct((group_rows, width), BF),
            jax.ShapeDtypeStruct((block, width), F32),
            jax.ShapeDtypeStruct((1, width), F32),
            jax.ShapeDtypeStruct((experts, width), BF),
        ),
        in_specs=[SMEM] + [HBM] * len(operands),
        out_specs=(VMEM,) * 4,
        scratch_shapes=[pltpu.VMEM(each.shape, each.dtype) for each in operands[:9]]
        + [pltpu.VMEM((1, group_rows), jnp.int32), pltpu.SemaphoreType.DMA((len(operands),))],
        compiler_params=PARAMS,
        name="attention",
    )(hid_index, *map(in_hbm, operands))
    chosen, target, column = pl.pallas_call(
        routing_kernel,
        out_shape=(
            jax.ShapeDtypeStruct((slot_count, LANES), BF),
            jax.ShapeDtypeStruct((2, LANES), jnp.int32),
            jax.ShapeDtypeStruct((2, block, LANES), jnp.int32),
        ),
        in_specs=[SMEM, VMEM, VMEM],
        out_specs=(VMEM,) * 3,
        compiler_params=PARAMS,
        name="routing",
    )(hid_index, routes.T, gain)
    column, w_cols = lax.optimization_barrier((column, w_cols))
    moves = [[(at, (at + shift) % row) for at in range(row)] for shift in range(row)]
    own_core = [w_cols] + [lax.ppermute(w_cols, "x", move) for move in moves[1:-1]]
    parts = lax.all_to_all(partial_mix.reshape(hid_count, block, width), hid, 0, 0, tiled=True)
    ffn_in = pl.pallas_call(
        mix_kernel,
        out_shape=jax.ShapeDtypeStruct((block, width), BF),
        in_specs=[VMEM] * 3,
        out_specs=VMEM,
        compiler_params=PARAMS,
        cost_estimate=LONG,
        name="mix",
    )(parts, own, gain)
    outgoing = pl.pallas_call(
        dispatch_kernel,
        out_shape=jax.ShapeDtypeStruct((slot_count, LANES), BF),
        in_specs=[VMEM] * 2,
        out_specs=VMEM,
        compiler_params=PARAMS,
        cost_estimate=LONG,
        name="dispatch",
    )(ffn_in, chosen)
    gates, after = pl.pallas_call(
        gates_kernel,
        out_shape=(jax.ShapeDtypeStruct((2, block, LANES), F32), jax.ShapeDtypeStruct((block, width), F32)),
        in_specs=[VMEM] * 5,
        out_specs=(VMEM,) * 2,
        compiler_params=PARAMS,
        cost_estimate=LONG,
        name="gates",
    )(ffn_in, router_rows, column, parts, own)
    exchanged = (experts, chunks * CAPACITY, LANES)
    arrived = lax.all_to_all(outgoing.reshape(exchanged), "z", 0, 0, tiled=True)
    order = pl.pallas_call(
        functools.partial(order_kernel, chunks),
        out_shape=jax.ShapeDtypeStruct((slot_count, slot_count), BF),
        in_specs=[VMEM],
        out_specs=VMEM,
        compiler_params=PARAMS,
        name="order",
    )(gates)
    order, *own_core = lax.optimization_barrier((order, *own_core))
    own_core.append(lax.ppermute(own_core[0], "x", moves[-1]))
    spread = pl.pallas_call(
        spread_kernel,
        out_shape=jax.ShapeDtypeStruct((split, slot_count, LANES), BF),
        in_specs=[VMEM],
        out_specs=VMEM,
        compiler_params=PARAMS,
        name="spread",
    )(arrived.reshape(slot_count, LANES))
    tokens = lax.all_to_all(spread, "y", 0, 0, tiled=True)
    own_core = [cols.reshape(-1, width) for cols in own_core]
    stacked = pl.pallas_call(
        stack_kernel,
        out_shape=jax.ShapeDtypeStruct((row,) + own_core[0].shape, BF),
        in_specs=[pl.BlockSpec(memory_space=pl.ANY)] + [VMEM] * row,
        out_specs=VMEM,
        compiler_params=PARAMS,
        name="stack",
    )(spread, *own_core)
    other_core = lax.ppermute(stacked, "c", [(0, 1), (1, 0)])
    rows, own_hidden, down = pl.pallas_call(
        own_kernel,
        out_shape=(
            jax.ShapeDtypeStruct((split * experts * CAPACITY, width), BF),
            jax.ShapeDtypeStruct((row, split * experts * CAPACITY, w_in.shape[2]), BF),
            jax.ShapeDtypeStruct(w_out.shape, BF),
        ),
        in_specs=[HBM, VMEM, VMEM, HBM],
        out_specs=(VMEM,) * 3,
        scratch_shapes=[pltpu.VMEM(spread.shape, BF), pltpu.SemaphoreType.DMA((split,)), pltpu.SemaphoreType.DMA],
        compiler_params=PARAMS,
        cost_estimate=VERY_LONG,
        name="own",
    )(in_hbm(tokens), order, stacked, in_hbm(w_out))
    projected = pl.pallas_call(
        ffn_kernel,
        out_shape=jax.ShapeDtypeStruct((split, slot_count, LANES), BF),
        in_specs=[SMEM] + [VMEM] * 5,
        out_specs=VMEM,
        scratch_shapes=[
            pltpu.VMEM((split * experts * CAPACITY, width), BF),
        ],
        compiler_params=PARAMS,
        name="ffn",
    )(hid_index, rows, order, down, own_hidden, other_core)
    quarters = lax.all_to_all(projected, "y", 0, 0, tiled=True)
    summed = pl.pallas_call(
        sum_kernel,
        out_shape=jax.ShapeDtypeStruct((slot_count, LANES), BF),
        in_specs=[VMEM],
        out_specs=VMEM,
        compiler_params=PARAMS,
        name="sum_quarters",
    )(quarters)
    returned = lax.all_to_all(summed.reshape(exchanged), "z", 0, 0, tiled=True)
    return pl.pallas_call(
        combine_kernel,
        out_shape=jax.ShapeDtypeStruct((block, width), BF),
        in_specs=[VMEM] * 4,
        out_specs=VMEM,
        compiler_params=PARAMS,
        name="combine",
    )(returned.reshape(slot_count, LANES), after, gates, target)


def solution(mesh):
    fine = Mesh(mesh.devices.reshape(16, 4, 4, 2), ("z", "y", "x", "c"))
    req = ("z", "y")
    hid = ("x", "c")
    in_specs = (
        P(req, None),
        P(),
        P(None, hid),
        P(None, hid),
        P(None, hid),
        P(hid, None),
        P(req, None, None, hid),
        P(req),
        P(req, None),
        P(),
        P(),
        P(req, None),
        P(None, None, req + hid),
        P(req, None),
    )
    out_specs = P(req + hid, None)
    return jax.shard_map(body, mesh=fine, in_specs=in_specs, out_specs=out_specs, check_vma=False)
```

```python
import functools

import jax
import jax.numpy as jnp
from jax import lax
from jax.experimental import pallas as pl
from jax.experimental.pallas import tpu as pltpu
from jax.sharding import Mesh
from jax.sharding import PartitionSpec as P

HDIM = 64
EPS = 1e-06
BF = jnp.bfloat16
F32 = jnp.float32
LANES = 128
CAPACITY = 3


def dot(a, b):
    return jnp.dot(a, b, preferred_element_type=F32)


def dot_nt(a, b):
    return lax.dot_general(a, b, (((1,), (1,)), ((), ())), preferred_element_type=F32)


def dot_tn(a, b):
    return lax.dot_general(a, b, (((0,), (0,)), ((), ())), preferred_element_type=F32)


def iota(shape, dim):
    return lax.broadcasted_iota(jnp.int32, shape, dim)


def to_column(row, size):
    diagonal = iota((size, size), 0) == iota((size, size), 1)
    return jnp.sum(jnp.where(diagonal, jnp.broadcast_to(row, (size, size)), 0), axis=1, keepdims=True)


def attention_kernel(
    index_ref, resid_hbm, gain_hbm, wq_hbm, wk_hbm, wv_hbm, wo_hbm, cache_hbm, lens_hbm, seg_hbm,
    ffn_gain_hbm, router_hbm, cols_hbm, out_ref, own_ref, ffn_gain_ref, router_ref, cols_ref,
    resid_ref, gain_ref, wq_ref, wk_ref, wv_ref, wo_ref, cache_ref, lens_ref, seg_ref, seg_row, sems
):
    sources = (
        resid_hbm, gain_hbm, wq_hbm, wk_hbm, wv_hbm, seg_hbm, lens_hbm, cache_hbm, wo_hbm, ffn_gain_hbm, router_hbm, cols_hbm
    )
    targets = (
        resid_ref, gain_ref, wq_ref, wk_ref, wv_ref, seg_ref, lens_ref, cache_ref, wo_ref, ffn_gain_ref, router_ref, cols_ref
    )
    copies = [pltpu.make_async_copy(a, b, sems.at[i]) for i, (a, b) in enumerate(zip(sources, targets))]
    for copy in copies:
        copy.start()
    total = resid_ref.shape[0]
    packed = seg_ref.shape[1]
    decoded, _, slots, width = cache_ref.shape
    heads = width // HDIM
    scale = HDIM ** (-0.5)
    copies[0].wait()
    copies[1].wait()
    x = resid_ref[...].astype(F32)
    inverse = lax.rsqrt(jnp.mean(x * x, axis=-1, keepdims=True) + EPS)
    normed = (x * inverse * gain_ref[...]).astype(BF)
    copies[2].wait()
    query = dot(normed, wq_ref[...]).astype(BF)
    copies[3].wait()
    keys = dot(normed, wk_ref[...]).astype(BF)
    copies[4].wait()
    values = dot(normed, wv_ref[...]).astype(BF)
    copies[5].wait()
    copies[6].wait()

    seg_row[...] = iota((1, total), 1) + (1 << 20)
    seg_row[:, :packed] = seg_ref[...]
    segments = seg_row[...]
    allowed = (iota((total, total), 1) <= iota((total, total), 0)) & (to_column(segments, total) == segments)
    lengths = to_column(lens_ref[...], decoded)
    slot_at = iota((decoded, decoded * slots), 1)
    own_cache = (slot_at // slots == iota((decoded, decoded * slots), 0)) & (slot_at % slots < lengths)

    lane_head = iota((total, width), 1) // HDIM
    queries = [jnp.where(lane_head == head, query, jnp.zeros_like(query)) for head in range(heads)]
    packed_scores = [jnp.where(allowed, dot_nt(head_query, keys) * scale, -jnp.inf) for head_query in queries]
    packed_highest = [jnp.max(scores, axis=-1, keepdims=True) for scores in packed_scores]
    copies[7].wait()
    cached_keys = cache_ref[:, 0].reshape(decoded * slots, width)
    cached_values = cache_ref[:, 1].reshape(decoded * slots, width)
    context = jnp.zeros((total, width), F32)
    for head in range(heads):
        mine = lane_head == head
        scores, highest = packed_scores[head], packed_highest[head]
        cached = jnp.where(own_cache, dot_nt(queries[head][packed:], cached_keys) * scale, -jnp.inf)
        top_dec = jnp.maximum(highest[packed:], jnp.max(cached, axis=-1, keepdims=True))
        highest = jnp.concatenate([highest[:packed], top_dec], axis=0)
        weights = jnp.exp(scores - highest)
        weights_cache = jnp.exp(cached - top_dec)
        norm = jnp.sum(weights, axis=-1, keepdims=True)
        norm_dec = norm[packed:] + jnp.sum(weights_cache, axis=-1, keepdims=True)
        norm = jnp.concatenate([norm[:packed], norm_dec], axis=0)
        part = dot((weights / norm).astype(BF), values)
        part_cache = dot((weights_cache / norm_dec).astype(BF), cached_values)
        part = jnp.concatenate([part[:packed], part[packed:] + part_cache], axis=0)
        context = jnp.where(mine, part, context)
    copies[8].wait()
    out_ref[...] = dot(context.astype(BF), wo_ref[...]).astype(out_ref.dtype)

    block = own_ref.shape[0]
    index = index_ref[0]
    own_ref[...] = resid_ref[pl.ds(pl.multiple_of(index * block, block), block), :].astype(F32)
    copies[9].wait()
    copies[10].wait()
    copies[11].wait()


def own_routes(routes_ref, which, index, block):
    lane = iota((1, LANES), 1)
    row = pltpu.roll(routes_ref[pl.ds(which, 1), :], (LANES - index * block) % LANES, 1)
    size = block
    while size < LANES:
        row = jnp.where(lane < size, row, pltpu.roll(row, size, 1))
        size *= 2
    return row


def placement(row, columns, block, capacity):
    token = iota((block, LANES), 1) % block
    before = iota((block, LANES), 0) < token
    slot = jnp.zeros((1, LANES), jnp.int32)
    for column in columns:
        slot = slot + jnp.sum(((column == row) & before).astype(jnp.int32), axis=0, keepdims=True)
    return row * capacity + slot


def slot_rows(rows, capacity, chunks):
    at = iota((rows, LANES), 0)
    expert = at // (chunks * capacity)
    rest = at - expert * (chunks * capacity)
    chunk = rest // capacity
    return expert * capacity + rest - chunk * capacity, chunk


def route_columns(rows, block):
    size = (block, LANES)
    diagonal = iota(size, 0) == iota(size, 1)
    return [
        jnp.sum(jnp.where(diagonal, jnp.broadcast_to(row, size), 0), axis=1, keepdims=True) for row in rows
    ]


def routing_kernel(index_ref, routes_ref, gain_ref, chosen_ref, target_ref, column_ref):
    block = column_ref.shape[1]
    chunks = gain_ref.shape[1] // LANES
    rows = [own_routes(routes_ref, which, index_ref[0], block) for which in range(2)]
    columns = route_columns(rows, block)
    wanted, chunk = slot_rows(chosen_ref.shape[0], CAPACITY, chunks)
    same = chunk == iota(chunk.shape, 1) // block
    both = None
    for which in range(2):
        target = placement(rows[which], columns, block, CAPACITY)
        here = jnp.where(same & (wanted == target), 1.0, 0.0)
        target_ref[pl.ds(which, 1), :] = target
        both = here if both is None else both + here
        column_ref[which] = jnp.broadcast_to(columns[which], (block, LANES))
    chosen_ref[...] = both.astype(BF)


def residual(parts_ref, own_ref):
    mixed = parts_ref[0].astype(F32)
    for source in range(1, parts_ref.shape[0]):
        mixed = mixed + parts_ref[source].astype(F32)
    return own_ref[...] + mixed


def dispatch_kernel(parts_ref, own_ref, gain_ref, chosen_ref, out_ref, ffn_in_ref):
    after = residual(parts_ref, own_ref)
    inverse = lax.rsqrt(jnp.mean(after * after, axis=-1, keepdims=True) + EPS)
    ffn_in = (after * inverse * gain_ref[...]).astype(BF)
    ffn_in_ref[...] = ffn_in
    chunks = ffn_in.shape[1] // LANES
    stacked = jnp.concatenate([ffn_in[:, at * LANES : (at + 1) * LANES] for at in range(chunks)], axis=0)
    out_ref[...] = dot(chosen_ref[...], stacked).astype(BF)


def gates_kernel(ffn_in_ref, router_ref, column_ref, parts_ref, own_ref, gates_ref, after_ref):
    after_ref[...] = residual(parts_ref, own_ref)
    block = ffn_in_ref.shape[0]
    experts = router_ref.shape[0]
    logits = dot_nt(ffn_in_ref[...], router_ref[...])
    expert_at = iota((block, experts), 1)
    for which in range(2):
        mine = expert_at == column_ref[which][:, :experts]
        picked = jnp.sum(jnp.where(mine, logits, 0.0), axis=1, keepdims=True)
        gates_ref[which] = jnp.broadcast_to(jax.nn.sigmoid(picked), (block, LANES))


def order_kernel(chunks, tokens_ref, order_ref):
    chunk_rows = order_ref.shape[0]
    each = chunk_rows // chunks
    at = iota((chunk_rows, chunk_rows), 0)
    chunk = at // each
    rest = at - chunk * each
    source = rest // CAPACITY
    wanted = source * (chunks * CAPACITY) + chunk * CAPACITY + rest - source * CAPACITY
    order_ref[...] = jnp.where(wanted == iota((chunk_rows, chunk_rows), 1), 1.0, 0.0).astype(BF)


def spread_kernel(tokens_ref, out_hbm, sems):
    copies = [pltpu.make_async_copy(tokens_ref, out_hbm.at[at], sems.at[at]) for at in range(out_hbm.shape[0])]
    for copy in copies:
        copy.start()
    for copy in copies:
        copy.wait()


def stack_kernel(spread_ref, *refs):
    *pieces, out_ref = refs
    for at, piece in enumerate(pieces):
        out_ref[at] = piece[...]


def hidden_of(rows, piece):
    columns = piece.shape[0] // 2
    projected = dot_nt(rows, piece)
    gate_val, up_val = projected[:, :columns], projected[:, columns:]
    return (jax.nn.gelu(gate_val, approximate=True) * up_val).astype(BF)


def own_kernel(tokens_hbm, order_ref, own_ref, down_hbm, rows_ref, hidden_ref, down_ref, tokens_ref, sems, sem):
    copies = [pltpu.make_async_copy(tokens_hbm.at[at], tokens_ref.at[at], sems.at[at]) for at in range(tokens_ref.shape[0])]
    for copy in copies:
        copy.start()
    fetch = pltpu.make_async_copy(down_hbm, down_ref, sem)
    fetch.start()
    groups, chunk_rows, _ = tokens_ref.shape
    chunks = rows_ref.shape[1] // LANES
    each = chunk_rows // chunks
    for group in range(groups):
        copies[group].wait()
        unpacked = dot(order_ref[...], tokens_ref[group]).astype(BF)
        for at in range(chunks):
            rows_ref[group * each : (group + 1) * each, at * LANES : (at + 1) * LANES] = unpacked[
                at * each : (at + 1) * each
            ]
    for shift in range(own_ref.shape[0]):
        hidden_ref[shift] = hidden_of(rows_ref[...], own_ref[shift])
    fetch.wait()


def ffn_kernel(index_ref, rows_ref, order_ref, down_ref, own_hidden_ref, other_ref, out_ref, total_ref):
    chips, both, _ = other_ref.shape
    groups, chunk_rows, _ = out_ref.shape
    width = rows_ref.shape[1]
    chunks = width // LANES
    each = chunk_rows // chunks
    core = index_ref[0] % 2
    chip = index_ref[0] // 2

    def experts_part(own_first):
        total = None
        for shift in range(chips):
            came = (chip - shift + chips) % chips
            pair = [own_hidden_ref[shift], hidden_of(rows_ref[...], other_ref[shift])]
            hidden = jnp.concatenate(pair if own_first else pair[::-1], axis=1)
            part = dot(hidden, down_ref[pl.ds(pl.multiple_of(came * both, 16), both), :])
            total = part if total is None else total + part
        total_ref[...] = total.astype(BF)

    @pl.when(core == 0)
    def _():
        experts_part(True)

    @pl.when(core != 0)
    def _():
        experts_part(False)

    for group in range(groups):
        mine = total_ref[group * each : (group + 1) * each]
        stacked = jnp.concatenate([mine[:, at * LANES : (at + 1) * LANES] for at in range(chunks)], axis=0)
        out_ref[group] = dot_tn(order_ref[...], stacked).astype(BF)


def sum_kernel(parts_ref, out_ref):
    total = parts_ref[0].astype(F32)
    for at in range(1, parts_ref.shape[0]):
        total = total + parts_ref[at].astype(F32)
    out_ref[...] = total.astype(BF)


def combine_kernel(experts_ref, after_ref, gates_ref, target_ref, out_ref):
    block, width = after_ref.shape
    chunks = width // LANES
    wanted, chunk = slot_rows(experts_ref.shape[0], CAPACITY, chunks)
    same = chunk == iota(chunk.shape, 1) // block
    picked = []
    for which in range(2):
        chosen = same & (wanted == target_ref[pl.ds(which, 1), :])
        picked.append(dot_tn(jnp.where(chosen, 1.0, 0.0).astype(BF), experts_ref[...]))
    for at in range(chunks):
        lanes = slice(at * LANES, (at + 1) * LANES)
        mine = slice(at * block, (at + 1) * block)
        total = gates_ref[0] * picked[0][mine] + gates_ref[1] * picked[1][mine]
        out_ref[:, lanes] = (after_ref[:, lanes] + total).astype(BF)


VMEM = pl.BlockSpec(memory_space=pltpu.VMEM)
HBM = pl.BlockSpec(memory_space=pltpu.HBM)
SMEM = pl.BlockSpec(memory_space=pltpu.SMEM)


def in_hbm(array):
    return pltpu.with_memory_space_constraint(array, pltpu.HBM)


LONG = pl.CostEstimate(flops=10**10, transcendentals=0, bytes_accessed=1 << 21)
VERY_LONG = pl.CostEstimate(flops=2 * 10**10, transcendentals=0, bytes_accessed=1 << 21)
PARAMS = pltpu.CompilerParams(vmem_limit_bytes=16 * 1024 * 1024)


def body(
    resid, attn_gain, w_query, w_key, w_value, w_attn_out, cache, cache_lens, seg_ids, ffn_gain, router, routes, w_in, w_out
):
    hid = ("x", "c")
    hid_count = lax.axis_size(hid)
    hid_index = lax.axis_index(hid).astype(jnp.int32).reshape(1)
    group_rows, width = resid.shape
    experts = router.shape[1]
    block = group_rows // hid_count
    capacity = CAPACITY
    chunks = width // LANES
    slot_count = experts * chunks * capacity
    split = lax.axis_size("y")
    w_cols = jnp.transpose(w_in, (0, 2, 1))
    row = lax.axis_size("x")

    operands = (
        resid,
        attn_gain.reshape(1, width),
        w_query,
        w_key,
        w_value,
        w_attn_out,
        cache,
        cache_lens.reshape(1, -1),
        seg_ids,
        ffn_gain.reshape(1, width),
        router.T,
        w_cols,
    )
    partial_mix, own, gain, router_rows, w_cols = pl.pallas_call(
        attention_kernel,
        out_shape=(
            jax.ShapeDtypeStruct((group_rows, width), BF),
            jax.ShapeDtypeStruct((block, width), F32),
            jax.ShapeDtypeStruct((1, width), F32),
            jax.ShapeDtypeStruct((experts, width), BF),
            jax.ShapeDtypeStruct(w_cols.shape, BF),
        ),
        in_specs=[SMEM] + [HBM] * len(operands),
        out_specs=(VMEM,) * 5,
        scratch_shapes=[pltpu.VMEM(each.shape, each.dtype) for each in operands[:9]]
        + [pltpu.VMEM((1, group_rows), jnp.int32), pltpu.SemaphoreType.DMA((len(operands),))],
        compiler_params=PARAMS,
        name="attention",
    )(hid_index, *map(in_hbm, operands))
    chosen, target, column = pl.pallas_call(
        routing_kernel,
        out_shape=(
            jax.ShapeDtypeStruct((slot_count, LANES), BF),
            jax.ShapeDtypeStruct((2, LANES), jnp.int32),
            jax.ShapeDtypeStruct((2, block, LANES), jnp.int32),
        ),
        in_specs=[SMEM, VMEM, VMEM],
        out_specs=(VMEM,) * 3,
        compiler_params=PARAMS,
        name="routing",
    )(hid_index, routes.T, gain)
    column, w_cols = lax.optimization_barrier((column, w_cols))
    moves = [[(at, (at + shift) % row) for at in range(row)] for shift in range(row)]
    own_core = [w_cols] + [lax.ppermute(w_cols, "x", move) for move in moves[1:-1]]
    parts = lax.all_to_all(partial_mix.reshape(hid_count, block, width), hid, 0, 0, tiled=True)
    outgoing, ffn_in = pl.pallas_call(
        dispatch_kernel,
        out_shape=(jax.ShapeDtypeStruct((slot_count, LANES), BF), jax.ShapeDtypeStruct((block, width), BF)),
        in_specs=[VMEM] * 4,
        out_specs=(VMEM,) * 2,
        compiler_params=PARAMS,
        cost_estimate=VERY_LONG,
        name="dispatch",
    )(parts, own, gain, chosen)
    gates, after = pl.pallas_call(
        gates_kernel,
        out_shape=(jax.ShapeDtypeStruct((2, block, LANES), F32), jax.ShapeDtypeStruct((block, width), F32)),
        in_specs=[VMEM] * 5,
        out_specs=(VMEM,) * 2,
        compiler_params=PARAMS,
        cost_estimate=LONG,
        name="gates",
    )(ffn_in, router_rows, column, parts, own)
    exchanged = (experts, chunks * CAPACITY, LANES)
    arrived = lax.all_to_all(outgoing.reshape(exchanged), "z", 0, 0, tiled=True)
    order = pl.pallas_call(
        functools.partial(order_kernel, chunks),
        out_shape=jax.ShapeDtypeStruct((slot_count, slot_count), BF),
        in_specs=[VMEM],
        out_specs=VMEM,
        compiler_params=PARAMS,
        name="order",
    )(gates)
    order, *own_core = lax.optimization_barrier((order, *own_core))
    own_core.append(lax.ppermute(own_core[0], "x", moves[-1]))
    spread = pl.pallas_call(
        spread_kernel,
        out_shape=pltpu.HBM((split, slot_count, LANES), BF),
        in_specs=[VMEM],
        out_specs=HBM,
        scratch_shapes=[pltpu.SemaphoreType.DMA((split,))],
        compiler_params=PARAMS,
        name="spread",
    )(arrived.reshape(slot_count, LANES))
    tokens = lax.all_to_all(spread, "y", 0, 0, tiled=True)
    own_core = [cols.reshape(-1, width) for cols in own_core]
    stacked = pl.pallas_call(
        stack_kernel,
        out_shape=jax.ShapeDtypeStruct((row,) + own_core[0].shape, BF),
        in_specs=[HBM] + [VMEM] * row,
        out_specs=VMEM,
        compiler_params=PARAMS,
        name="stack",
    )(in_hbm(spread), *own_core)
    other_core = lax.ppermute(stacked, "c", [(0, 1), (1, 0)])
    rows, own_hidden, down = pl.pallas_call(
        own_kernel,
        out_shape=(
            jax.ShapeDtypeStruct((split * experts * CAPACITY, width), BF),
            jax.ShapeDtypeStruct((row, split * experts * CAPACITY, w_in.shape[2]), BF),
            jax.ShapeDtypeStruct(w_out.shape, BF),
        ),
        in_specs=[HBM, VMEM, VMEM, HBM],
        out_specs=(VMEM,) * 3,
        scratch_shapes=[pltpu.VMEM((split, slot_count, LANES), BF), pltpu.SemaphoreType.DMA((split,)), pltpu.SemaphoreType.DMA],
        compiler_params=PARAMS,
        cost_estimate=VERY_LONG,
        name="own",
    )(in_hbm(tokens), order, stacked, in_hbm(w_out))
    projected = pl.pallas_call(
        ffn_kernel,
        out_shape=jax.ShapeDtypeStruct((split, slot_count, LANES), BF),
        in_specs=[SMEM] + [VMEM] * 5,
        out_specs=VMEM,
        scratch_shapes=[
            pltpu.VMEM((split * experts * CAPACITY, width), BF),
        ],
        compiler_params=PARAMS,
        name="ffn",
    )(hid_index, rows, order, down, own_hidden, other_core)
    quarters = lax.all_to_all(projected, "y", 0, 0, tiled=True)
    summed = pl.pallas_call(
        sum_kernel,
        out_shape=jax.ShapeDtypeStruct((slot_count, LANES), BF),
        in_specs=[VMEM],
        out_specs=VMEM,
        compiler_params=PARAMS,
        name="sum_quarters",
    )(quarters)
    returned = lax.all_to_all(summed.reshape(exchanged), "z", 0, 0, tiled=True)
    return pl.pallas_call(
        combine_kernel,
        out_shape=jax.ShapeDtypeStruct((block, width), BF),
        in_specs=[VMEM] * 4,
        out_specs=VMEM,
        compiler_params=PARAMS,
        name="combine",
    )(returned.reshape(slot_count, LANES), after, gates, target)


def solution(mesh):
    fine = Mesh(mesh.devices.reshape(16, 4, 4, 2), ("z", "y", "x", "c"))
    req = ("z", "y")
    hid = ("x", "c")
    in_specs = (
        P(req, None),
        P(),
        P(None, hid),
        P(None, hid),
        P(None, hid),
        P(hid, None),
        P(req, None, None, hid),
        P(req),
        P(req, None),
        P(),
        P(),
        P(req, None),
        P(None, None, req + hid),
        P(req, None),
    )
    out_specs = P(req + hid, None)
    return jax.shard_map(body, mesh=fine, in_specs=in_specs, out_specs=out_specs, check_vma=False)
```

```python
import functools

import jax
import jax.numpy as jnp
from jax import lax
from jax.experimental import pallas as pl
from jax.experimental.pallas import tpu as pltpu
from jax.sharding import Mesh
from jax.sharding import PartitionSpec as P

HDIM = 64
EPS = 1e-06
BF = jnp.bfloat16
F32 = jnp.float32
LANES = 128
CAPACITY = 3


def dot(a, b):
    return jnp.dot(a, b, preferred_element_type=F32)


def dot_nt(a, b):
    return lax.dot_general(a, b, (((1,), (1,)), ((), ())), preferred_element_type=F32)


def dot_tn(a, b):
    return lax.dot_general(a, b, (((0,), (0,)), ((), ())), preferred_element_type=F32)


def iota(shape, dim):
    return lax.broadcasted_iota(jnp.int32, shape, dim)


def quotient(number, by):
    shift = (by & -by).bit_length() - 1
    odd = by >> shift
    if odd == 1:
        return number >> shift
    if odd == 3:
        return ((number >> shift) * 21846) >> 16
    return number // by


def to_column(row, size):
    diagonal = iota((size, size), 0) == iota((size, size), 1)
    return jnp.sum(jnp.where(diagonal, jnp.broadcast_to(row, (size, size)), 0), axis=1, keepdims=True)


def attention_kernel(
    index_ref, resid_hbm, gain_hbm, wq_hbm, wk_hbm, wv_hbm, wo_hbm, cache_hbm, lens_hbm, seg_hbm,
    ffn_gain_hbm, router_hbm, out_ref, own_ref, ffn_gain_ref, router_ref,
    resid_ref, gain_ref, wq_ref, wk_ref, wv_ref, wo_ref, cache_ref, lens_ref, seg_ref, seg_row, sems
):
    sources = (
        resid_hbm, gain_hbm, wq_hbm, wk_hbm, wv_hbm, seg_hbm, lens_hbm, cache_hbm, wo_hbm, ffn_gain_hbm, router_hbm
    )
    targets = (
        resid_ref, gain_ref, wq_ref, wk_ref, wv_ref, seg_ref, lens_ref, cache_ref, wo_ref, ffn_gain_ref, router_ref
    )
    copies = [pltpu.make_async_copy(a, b, sems.at[i]) for i, (a, b) in enumerate(zip(sources, targets))]
    for copy in copies:
        copy.start()
    total = resid_ref.shape[0]
    packed = seg_ref.shape[1]
    decoded, _, slots, width = cache_ref.shape
    heads = width // HDIM
    scale = HDIM ** (-0.5)
    causal = iota((total, total), 1) <= iota((total, total), 0)
    seg_row[...] = iota((1, total), 1) + (1 << 20)
    slot_at = iota((decoded, decoded * slots), 1)
    request = quotient(slot_at, slots)
    own_request = request == iota((decoded, decoded * slots), 0)
    slot_at = slot_at - request * slots
    lane_head = quotient(iota((total, width), 1), HDIM)
    copies[0].wait()
    copies[1].wait()
    x = resid_ref[...].astype(F32)
    inverse = lax.rsqrt(jnp.mean(x * x, axis=-1, keepdims=True) + EPS)
    normed = (x * inverse * gain_ref[...]).astype(BF)
    copies[2].wait()
    query = dot(normed, wq_ref[...]).astype(BF)
    copies[3].wait()
    keys = dot(normed, wk_ref[...]).astype(BF)
    copies[4].wait()
    values = dot(normed, wv_ref[...]).astype(BF)
    copies[5].wait()
    copies[6].wait()
    copies[7].wait()

    seg_row[:, :packed] = seg_ref[...]
    segments = seg_row[...]
    allowed = causal & (to_column(segments, total) == segments)
    lengths = to_column(lens_ref[...], decoded)
    own_cache = own_request & (slot_at < lengths)

    cached_keys = cache_ref[:, 0].reshape(decoded * slots, width)
    cached_values = cache_ref[:, 1].reshape(decoded * slots, width)
    context = jnp.zeros((total, width), F32)
    for head in range(heads):
        mine = lane_head == head
        head_query = jnp.where(mine, query, jnp.zeros_like(query))
        scores = jnp.where(allowed, dot_nt(head_query, keys) * scale, -jnp.inf)
        highest = jnp.max(scores, axis=-1, keepdims=True)
        cached = jnp.where(own_cache, dot_nt(head_query[packed:], cached_keys) * scale, -jnp.inf)
        top_dec = jnp.maximum(highest[packed:], jnp.max(cached, axis=-1, keepdims=True))
        highest = jnp.concatenate([highest[:packed], top_dec], axis=0)
        weights = jnp.exp(scores - highest)
        weights_cache = jnp.exp(cached - top_dec)
        norm = jnp.sum(weights, axis=-1, keepdims=True)
        norm_dec = norm[packed:] + jnp.sum(weights_cache, axis=-1, keepdims=True)
        norm = jnp.concatenate([norm[:packed], norm_dec], axis=0)
        part = dot((weights / norm).astype(BF), values)
        part_cache = dot((weights_cache / norm_dec).astype(BF), cached_values)
        part = jnp.concatenate([part[:packed], part[packed:] + part_cache], axis=0)
        context = jnp.where(mine, part, context)
    copies[8].wait()
    out_ref[...] = dot(context.astype(BF), wo_ref[...]).astype(out_ref.dtype)

    block = own_ref.shape[0]
    index = index_ref[0]
    own_ref[...] = resid_ref[pl.ds(pl.multiple_of(index * block, block), block), :].astype(F32)
    copies[9].wait()
    copies[10].wait()


def own_routes(routes_ref, which, index, block):
    lane = iota((1, LANES), 1)
    row = pltpu.roll(routes_ref[pl.ds(which, 1), :], (LANES - index * block) % LANES, 1)
    size = block
    while size < LANES:
        row = jnp.where(lane < size, row, pltpu.roll(row, size, 1))
        size *= 2
    return row


def placement(row, columns, block, capacity):
    token = iota((block, LANES), 1)
    token = token - quotient(token, block) * block
    before = iota((block, LANES), 0) < token
    slot = jnp.zeros((1, LANES), jnp.int32)
    for column in columns:
        slot = slot + jnp.sum(((column == row) & before).astype(jnp.int32), axis=0, keepdims=True)
    return row * capacity + slot


def slot_rows(rows, capacity, chunks):
    at = iota((rows, LANES), 0)
    expert = quotient(at, chunks * capacity)
    rest = at - expert * (chunks * capacity)
    chunk = quotient(rest, capacity)
    return expert * capacity + rest - chunk * capacity, chunk


def route_columns(rows, block):
    size = (block, LANES)
    diagonal = iota(size, 0) == iota(size, 1)
    return [
        jnp.sum(jnp.where(diagonal, jnp.broadcast_to(row, size), 0), axis=1, keepdims=True) for row in rows
    ]


def routing_kernel(index_ref, routes_ref, gain_ref, chosen_ref, target_ref, column_ref):
    block = column_ref.shape[1]
    chunks = gain_ref.shape[1] // LANES
    rows = [own_routes(routes_ref, which, index_ref[0], block) for which in range(2)]
    columns = route_columns(rows, block)
    wanted, chunk = slot_rows(chosen_ref.shape[0], CAPACITY, chunks)
    same = chunk == quotient(iota(chunk.shape, 1), block)
    both = None
    for which in range(2):
        target = placement(rows[which], columns, block, CAPACITY)
        here = jnp.where(same & (wanted == target), 1.0, 0.0)
        target_ref[pl.ds(which, 1), :] = target
        both = here if both is None else both + here
        column_ref[which] = jnp.broadcast_to(columns[which], (block, LANES))
    chosen_ref[...] = both.astype(BF)


def residual(parts_ref, own_ref):
    mixed = parts_ref[0].astype(F32)
    for source in range(1, parts_ref.shape[0]):
        mixed = mixed + parts_ref[source].astype(F32)
    return own_ref[...] + mixed


def mix_kernel(parts_ref, own_ref, gain_ref, ffn_in_ref):
    after = residual(parts_ref, own_ref)
    inverse = lax.rsqrt(jnp.mean(after * after, axis=-1, keepdims=True) + EPS)
    ffn_in_ref[...] = (after * inverse * gain_ref[...]).astype(BF)


def dispatch_kernel(ffn_in_ref, chosen_ref, out_ref):
    chunks = ffn_in_ref.shape[1] // LANES
    stacked = jnp.concatenate([ffn_in_ref[:, at * LANES : (at + 1) * LANES] for at in range(chunks)], axis=0)
    out_ref[...] = dot(chosen_ref[...], stacked).astype(BF)


def gates_kernel(ffn_in_ref, router_ref, column_ref, parts_ref, own_ref, gates_ref, after_ref):
    after_ref[...] = residual(parts_ref, own_ref)
    block = ffn_in_ref.shape[0]
    experts = router_ref.shape[0]
    logits = dot_nt(ffn_in_ref[...], router_ref[...])
    expert_at = iota((block, experts), 1)
    for which in range(2):
        mine = expert_at == column_ref[which][:, :experts]
        picked = jnp.sum(jnp.where(mine, logits, 0.0), axis=1, keepdims=True)
        gates_ref[which] = jnp.broadcast_to(jax.nn.sigmoid(picked), (block, LANES))


def order_kernel(chunks, tokens_ref, order_ref):
    chunk_rows = order_ref.shape[0]
    each = chunk_rows // chunks
    at = iota((chunk_rows, chunk_rows), 0)
    chunk = quotient(at, each)
    rest = at - chunk * each
    source = quotient(rest, CAPACITY)
    wanted = source * (chunks * CAPACITY) + chunk * CAPACITY + rest - source * CAPACITY
    order_ref[...] = jnp.where(wanted == iota((chunk_rows, chunk_rows), 1), 1.0, 0.0).astype(BF)


def spread_kernel(tokens_ref, out_ref):
    for at in range(out_ref.shape[0]):
        out_ref[at] = tokens_ref[...]


def stack_kernel(spread_ref, *refs):
    *pieces, out_ref = refs
    for at, piece in enumerate(pieces):
        out_ref[at] = piece[...]


def hidden_of(rows, piece):
    columns = piece.shape[0] // 2
    projected = dot_nt(rows, piece)
    gate_val, up_val = projected[:, :columns], projected[:, columns:]
    return (jax.nn.gelu(gate_val, approximate=True) * up_val).astype(BF)


def own_kernel(tokens_hbm, order_ref, own_ref, down_hbm, rows_ref, hidden_ref, down_ref, tokens_ref, sems, sem):
    copies = [pltpu.make_async_copy(tokens_hbm.at[at], tokens_ref.at[at], sems.at[at]) for at in range(tokens_ref.shape[0])]
    for copy in copies:
        copy.start()
    fetch = pltpu.make_async_copy(down_hbm, down_ref, sem)
    fetch.start()
    groups, chunk_rows, _ = tokens_ref.shape
    chunks = rows_ref.shape[1] // LANES
    each = chunk_rows // chunks
    for group in range(groups):
        copies[group].wait()
        unpacked = dot(order_ref[...], tokens_ref[group]).astype(BF)
        for at in range(chunks):
            rows_ref[group * each : (group + 1) * each, at * LANES : (at + 1) * LANES] = unpacked[
                at * each : (at + 1) * each
            ]
    for shift in range(own_ref.shape[0]):
        hidden_ref[shift] = hidden_of(rows_ref[...], own_ref[shift])
    fetch.wait()


def ffn_kernel(index_ref, rows_ref, order_ref, down_ref, own_hidden_ref, other_ref, out_ref, total_ref):
    chips, both, _ = other_ref.shape
    groups, chunk_rows, _ = out_ref.shape
    width = rows_ref.shape[1]
    chunks = width // LANES
    each = chunk_rows // chunks
    core = index_ref[0] % 2
    chip = index_ref[0] // 2

    def experts_part(own_first):
        total = None
        for shift in range(chips):
            came = (chip - shift + chips) % chips
            pair = [own_hidden_ref[shift], hidden_of(rows_ref[...], other_ref[shift])]
            hidden = jnp.concatenate(pair if own_first else pair[::-1], axis=1)
            part = dot(hidden, down_ref[pl.ds(pl.multiple_of(came * both, 16), both), :])
            total = part if total is None else total + part
        total_ref[...] = total.astype(BF)

    @pl.when(core == 0)
    def _():
        experts_part(True)

    @pl.when(core != 0)
    def _():
        experts_part(False)

    for group in range(groups):
        mine = total_ref[group * each : (group + 1) * each]
        stacked = jnp.concatenate([mine[:, at * LANES : (at + 1) * LANES] for at in range(chunks)], axis=0)
        out_ref[group] = dot_tn(order_ref[...], stacked).astype(BF)


def sum_kernel(parts_ref, out_ref):
    total = parts_ref[0].astype(F32)
    for at in range(1, parts_ref.shape[0]):
        total = total + parts_ref[at].astype(F32)
    out_ref[...] = total.astype(BF)


def combine_kernel(experts_ref, after_ref, gates_ref, target_ref, out_ref):
    block, width = after_ref.shape
    chunks = width // LANES
    wanted, chunk = slot_rows(experts_ref.shape[0], CAPACITY, chunks)
    same = chunk == quotient(iota(chunk.shape, 1), block)
    picked = []
    for which in range(2):
        chosen = same & (wanted == target_ref[pl.ds(which, 1), :])
        picked.append(dot_tn(jnp.where(chosen, 1.0, 0.0).astype(BF), experts_ref[...]))
    for at in range(chunks):
        lanes = slice(at * LANES, (at + 1) * LANES)
        mine = slice(at * block, (at + 1) * block)
        total = gates_ref[0] * picked[0][mine] + gates_ref[1] * picked[1][mine]
        out_ref[:, lanes] = (after_ref[:, lanes] + total).astype(BF)


VMEM = pl.BlockSpec(memory_space=pltpu.VMEM)
HBM = pl.BlockSpec(memory_space=pltpu.HBM)
SMEM = pl.BlockSpec(memory_space=pltpu.SMEM)


def in_hbm(array):
    return pltpu.with_memory_space_constraint(array, pltpu.HBM)


LONG = pl.CostEstimate(flops=10**10, transcendentals=0, bytes_accessed=1 << 21)
VERY_LONG = pl.CostEstimate(flops=2 * 10**10, transcendentals=0, bytes_accessed=1 << 21)
PARAMS = pltpu.CompilerParams(vmem_limit_bytes=16 * 1024 * 1024)


def body(
    resid, attn_gain, w_query, w_key, w_value, w_attn_out, cache, cache_lens, seg_ids, ffn_gain, router, routes, w_in, w_out
):
    hid = ("x", "c")
    hid_count = lax.axis_size(hid)
    hid_index = lax.axis_index(hid).astype(jnp.int32).reshape(1)
    group_rows, width = resid.shape
    experts = router.shape[1]
    block = group_rows // hid_count
    capacity = CAPACITY
    chunks = width // LANES
    slot_count = experts * chunks * capacity
    split = lax.axis_size("y")
    w_cols = jnp.transpose(w_in, (0, 2, 1))
    row = lax.axis_size("x")

    operands = (
        resid,
        attn_gain.reshape(1, width),
        w_query,
        w_key,
        w_value,
        w_attn_out,
        cache,
        cache_lens.reshape(1, -1),
        seg_ids,
        ffn_gain.reshape(1, width),
        router.T,
    )
    partial_mix, own, gain, router_rows = pl.pallas_call(
        attention_kernel,
        out_shape=(
            jax.ShapeDtypeStruct((group_rows, width), BF),
            jax.ShapeDtypeStruct((block, width), F32),
            jax.ShapeDtypeStruct((1, width), F32),
            jax.ShapeDtypeStruct((experts, width), BF),
        ),
        in_specs=[SMEM] + [HBM] * len(operands),
        out_specs=(VMEM,) * 4,
        scratch_shapes=[pltpu.VMEM(each.shape, each.dtype) for each in operands[:9]]
        + [pltpu.VMEM((1, group_rows), jnp.int32), pltpu.SemaphoreType.DMA((len(operands),))],
        compiler_params=PARAMS,
        name="attention",
    )(hid_index, *map(in_hbm, operands))
    chosen, target, column = pl.pallas_call(
        routing_kernel,
        out_shape=(
            jax.ShapeDtypeStruct((slot_count, LANES), BF),
            jax.ShapeDtypeStruct((2, LANES), jnp.int32),
            jax.ShapeDtypeStruct((2, block, LANES), jnp.int32),
        ),
        in_specs=[SMEM, VMEM, VMEM],
        out_specs=(VMEM,) * 3,
        compiler_params=PARAMS,
        name="routing",
    )(hid_index, routes.T, gain)
    column, w_cols = lax.optimization_barrier((column, w_cols))
    moves = [[(at, (at + shift) % row) for at in range(row)] for shift in range(row)]
    own_core = [w_cols] + [lax.ppermute(w_cols, "x", move) for move in moves[1:-1]]
    parts = lax.all_to_all(partial_mix.reshape(hid_count, block, width), hid, 0, 0, tiled=True)
    ffn_in = pl.pallas_call(
        mix_kernel,
        out_shape=jax.ShapeDtypeStruct((block, width), BF),
        in_specs=[VMEM] * 3,
        out_specs=VMEM,
        compiler_params=PARAMS,
        cost_estimate=LONG,
        name="mix",
    )(parts, own, gain)
    outgoing = pl.pallas_call(
        dispatch_kernel,
        out_shape=jax.ShapeDtypeStruct((slot_count, LANES), BF),
        in_specs=[VMEM] * 2,
        out_specs=VMEM,
        compiler_params=PARAMS,
        cost_estimate=LONG,
        name="dispatch",
    )(ffn_in, chosen)
    gates, after = pl.pallas_call(
        gates_kernel,
        out_shape=(jax.ShapeDtypeStruct((2, block, LANES), F32), jax.ShapeDtypeStruct((block, width), F32)),
        in_specs=[VMEM] * 5,
        out_specs=(VMEM,) * 2,
        compiler_params=PARAMS,
        cost_estimate=LONG,
        name="gates",
    )(ffn_in, router_rows, column, parts, own)
    exchanged = (experts, chunks * CAPACITY, LANES)
    arrived = lax.all_to_all(outgoing.reshape(exchanged), "z", 0, 0, tiled=True)
    order = pl.pallas_call(
        functools.partial(order_kernel, chunks),
        out_shape=jax.ShapeDtypeStruct((slot_count, slot_count), BF),
        in_specs=[VMEM],
        out_specs=VMEM,
        compiler_params=PARAMS,
        name="order",
    )(gates)
    order, *own_core = lax.optimization_barrier((order, *own_core))
    own_core.append(lax.ppermute(own_core[0], "x", moves[-1]))
    spread = pl.pallas_call(
        spread_kernel,
        out_shape=jax.ShapeDtypeStruct((split, slot_count, LANES), BF),
        in_specs=[VMEM],
        out_specs=VMEM,
        compiler_params=PARAMS,
        name="spread",
    )(arrived.reshape(slot_count, LANES))
    tokens = lax.all_to_all(spread, "y", 0, 0, tiled=True)
    own_core = [cols.reshape(-1, width) for cols in own_core]
    stacked = pl.pallas_call(
        stack_kernel,
        out_shape=jax.ShapeDtypeStruct((row,) + own_core[0].shape, BF),
        in_specs=[pl.BlockSpec(memory_space=pl.ANY)] + [VMEM] * row,
        out_specs=VMEM,
        compiler_params=PARAMS,
        name="stack",
    )(spread, *own_core)
    other_core = lax.ppermute(stacked, "c", [(0, 1), (1, 0)])
    rows, own_hidden, down = pl.pallas_call(
        own_kernel,
        out_shape=(
            jax.ShapeDtypeStruct((split * experts * CAPACITY, width), BF),
            jax.ShapeDtypeStruct((row, split * experts * CAPACITY, w_in.shape[2]), BF),
            jax.ShapeDtypeStruct(w_out.shape, BF),
        ),
        in_specs=[HBM, VMEM, VMEM, HBM],
        out_specs=(VMEM,) * 3,
        scratch_shapes=[pltpu.VMEM(spread.shape, BF), pltpu.SemaphoreType.DMA((split,)), pltpu.SemaphoreType.DMA],
        compiler_params=PARAMS,
        cost_estimate=VERY_LONG,
        name="own",
    )(in_hbm(tokens), order, stacked, in_hbm(w_out))
    projected = pl.pallas_call(
        ffn_kernel,
        out_shape=jax.ShapeDtypeStruct((split, slot_count, LANES), BF),
        in_specs=[SMEM] + [VMEM] * 5,
        out_specs=VMEM,
        scratch_shapes=[
            pltpu.VMEM((split * experts * CAPACITY, width), BF),
        ],
        compiler_params=PARAMS,
        name="ffn",
    )(hid_index, rows, order, down, own_hidden, other_core)
    quarters = lax.all_to_all(projected, "y", 0, 0, tiled=True)
    summed = pl.pallas_call(
        sum_kernel,
        out_shape=jax.ShapeDtypeStruct((slot_count, LANES), BF),
        in_specs=[VMEM],
        out_specs=VMEM,
        compiler_params=PARAMS,
        name="sum_quarters",
    )(quarters)
    returned = lax.all_to_all(summed.reshape(exchanged), "z", 0, 0, tiled=True)
    return pl.pallas_call(
        combine_kernel,
        out_shape=jax.ShapeDtypeStruct((block, width), BF),
        in_specs=[VMEM] * 4,
        out_specs=VMEM,
        compiler_params=PARAMS,
        name="combine",
    )(returned.reshape(slot_count, LANES), after, gates, target)


def solution(mesh):
    fine = Mesh(mesh.devices.reshape(16, 4, 4, 2), ("z", "y", "x", "c"))
    req = ("z", "y")
    hid = ("x", "c")
    in_specs = (
        P(req, None),
        P(),
        P(None, hid),
        P(None, hid),
        P(None, hid),
        P(hid, None),
        P(req, None, None, hid),
        P(req),
        P(req, None),
        P(),
        P(),
        P(req, None),
        P(None, None, req + hid),
        P(req, None),
    )
    out_specs = P(req + hid, None)
    return jax.shard_map(body, mesh=fine, in_specs=in_specs, out_specs=out_specs, check_vma=False)
```

```python
import functools

import jax
import jax.numpy as jnp
from jax import lax
from jax.experimental import pallas as pl
from jax.experimental.pallas import tpu as pltpu
from jax.sharding import Mesh
from jax.sharding import PartitionSpec as P

HDIM = 64
EPS = 1e-06
BF = jnp.bfloat16
F32 = jnp.float32
LANES = 128
CAPACITY = 3


def dot(a, b):
    return jnp.dot(a, b, preferred_element_type=F32)


def dot_nt(a, b):
    return lax.dot_general(a, b, (((1,), (1,)), ((), ())), preferred_element_type=F32)


def dot_tn(a, b):
    return lax.dot_general(a, b, (((0,), (0,)), ((), ())), preferred_element_type=F32)


def iota(shape, dim):
    return lax.broadcasted_iota(jnp.int32, shape, dim)


def quotient(number, by):
    shift = (by & -by).bit_length() - 1
    odd = by >> shift
    if odd == 1:
        return number >> shift
    if odd == 3:
        return ((number >> shift) * 21846) >> 16
    return number // by


def to_column(row, size):
    diagonal = iota((size, size), 0) == iota((size, size), 1)
    return jnp.sum(jnp.where(diagonal, jnp.broadcast_to(row, (size, size)), 0), axis=1, keepdims=True)


def attention_kernel(
    index_ref, resid_hbm, gain_hbm, wq_hbm, wk_hbm, wv_hbm, wo_hbm, cache_hbm, lens_hbm, seg_hbm,
    ffn_gain_hbm, router_hbm, out_ref, own_ref, ffn_gain_ref, router_ref,
    resid_ref, gain_ref, wq_ref, wk_ref, wv_ref, wo_ref, cache_ref, lens_ref, seg_ref, seg_row, sems
):
    sources = (
        resid_hbm, gain_hbm, wq_hbm, wk_hbm, wv_hbm, seg_hbm, lens_hbm, cache_hbm, wo_hbm, ffn_gain_hbm, router_hbm
    )
    targets = (
        resid_ref, gain_ref, wq_ref, wk_ref, wv_ref, seg_ref, lens_ref, cache_ref, wo_ref, ffn_gain_ref, router_ref
    )
    copies = [pltpu.make_async_copy(a, b, sems.at[i]) for i, (a, b) in enumerate(zip(sources, targets))]
    for copy in copies:
        copy.start()
    total = resid_ref.shape[0]
    packed = seg_ref.shape[1]
    decoded, _, slots, width = cache_ref.shape
    heads = width // HDIM
    scale = HDIM ** (-0.5)
    causal = iota((total, total), 1) <= iota((total, total), 0)
    seg_row[...] = iota((1, total), 1) + (1 << 20)
    slot_at = iota((decoded, decoded * slots), 1)
    request = quotient(slot_at, slots)
    own_request = request == iota((decoded, decoded * slots), 0)
    slot_at = slot_at - request * slots
    lane_head = quotient(iota((total, width), 1), HDIM)
    copies[0].wait()
    copies[1].wait()
    x = resid_ref[...].astype(F32)
    inverse = lax.rsqrt(jnp.mean(x * x, axis=-1, keepdims=True) + EPS)
    normed = (x * inverse * gain_ref[...]).astype(BF)
    copies[2].wait()
    query = dot(normed, wq_ref[...]).astype(BF)
    copies[3].wait()
    keys = dot(normed, wk_ref[...]).astype(BF)
    copies[4].wait()
    values = dot(normed, wv_ref[...]).astype(BF)
    copies[5].wait()
    copies[6].wait()
    copies[7].wait()

    seg_row[:, :packed] = seg_ref[...]
    segments = seg_row[...]
    allowed = causal & (to_column(segments, total) == segments)
    lengths = to_column(lens_ref[...], decoded)
    own_cache = own_request & (slot_at < lengths)

    cached_keys = cache_ref[:, 0].reshape(decoded * slots, width)
    cached_values = cache_ref[:, 1].reshape(decoded * slots, width)
    context = jnp.zeros((total, width), F32)
    for head in range(heads):
        mine = lane_head == head
        head_query = jnp.where(mine, query, jnp.zeros_like(query))
        scores = jnp.where(allowed, dot_nt(head_query, keys) * scale, -jnp.inf)
        highest = jnp.max(scores, axis=-1, keepdims=True)
        cached = jnp.where(own_cache, dot_nt(head_query[packed:], cached_keys) * scale, -jnp.inf)
        top_dec = jnp.maximum(highest[packed:], jnp.max(cached, axis=-1, keepdims=True))
        highest = jnp.concatenate([highest[:packed], top_dec], axis=0)
        weights = jnp.exp(scores - highest)
        weights_cache = jnp.exp(cached - top_dec)
        norm = jnp.sum(weights, axis=-1, keepdims=True)
        norm_dec = norm[packed:] + jnp.sum(weights_cache, axis=-1, keepdims=True)
        norm = jnp.concatenate([norm[:packed], norm_dec], axis=0)
        part = dot((weights / norm).astype(BF), values)
        part_cache = dot((weights_cache / norm_dec).astype(BF), cached_values)
        part = jnp.concatenate([part[:packed], part[packed:] + part_cache], axis=0)
        context = jnp.where(mine, part, context)
    copies[8].wait()
    out_ref[...] = dot(context.astype(BF), wo_ref[...]).astype(out_ref.dtype)

    block = own_ref.shape[0]
    index = index_ref[0]
    own_ref[...] = resid_ref[pl.ds(pl.multiple_of(index * block, block), block), :].astype(F32)
    copies[9].wait()
    copies[10].wait()


def own_routes(routes_ref, which, index, block):
    lane = iota((1, LANES), 1)
    row = pltpu.roll(routes_ref[pl.ds(which, 1), :], (LANES - index * block) % LANES, 1)
    size = block
    while size < LANES:
        row = jnp.where(lane < size, row, pltpu.roll(row, size, 1))
        size *= 2
    return row


def placement(row, columns, block, capacity):
    token = iota((block, LANES), 1)
    token = token - quotient(token, block) * block
    before = iota((block, LANES), 0) < token
    slot = jnp.zeros((1, LANES), jnp.int32)
    for column in columns:
        slot = slot + jnp.sum(((column == row) & before).astype(jnp.int32), axis=0, keepdims=True)
    return row * capacity + slot


def slot_rows(rows, capacity, chunks):
    at = iota((rows, LANES), 0)
    expert = quotient(at, chunks * capacity)
    rest = at - expert * (chunks * capacity)
    chunk = quotient(rest, capacity)
    return expert * capacity + rest - chunk * capacity, chunk


def route_columns(rows, block):
    size = (block, LANES)
    diagonal = iota(size, 0) == iota(size, 1)
    return [
        jnp.sum(jnp.where(diagonal, jnp.broadcast_to(row, size), 0), axis=1, keepdims=True) for row in rows
    ]


def routing_kernel(index_ref, routes_ref, gain_ref, chosen_ref, target_ref, column_ref):
    block = column_ref.shape[1]
    chunks = gain_ref.shape[1] // LANES
    rows = [own_routes(routes_ref, which, index_ref[0], block) for which in range(2)]
    columns = route_columns(rows, block)
    wanted, chunk = slot_rows(chosen_ref.shape[0], CAPACITY, chunks)
    same = chunk == quotient(iota(chunk.shape, 1), block)
    both = None
    for which in range(2):
        target = placement(rows[which], columns, block, CAPACITY)
        here = jnp.where(same & (wanted == target), 1.0, 0.0)
        target_ref[pl.ds(which, 1), :] = target
        both = here if both is None else both + here
        column_ref[which] = jnp.broadcast_to(columns[which], (block, LANES))
    chosen_ref[...] = both.astype(BF)


def residual(parts_ref, own_ref):
    mixed = parts_ref[0].astype(F32)
    for source in range(1, parts_ref.shape[0]):
        mixed = mixed + parts_ref[source].astype(F32)
    return own_ref[...] + mixed


def mix_kernel(parts_ref, own_ref, gain_ref, ffn_in_ref):
    after = residual(parts_ref, own_ref)
    inverse = lax.rsqrt(jnp.mean(after * after, axis=-1, keepdims=True) + EPS)
    ffn_in_ref[...] = (after * inverse * gain_ref[...]).astype(BF)


def dispatch_kernel(ffn_in_ref, chosen_ref, out_ref):
    chunks = ffn_in_ref.shape[1] // LANES
    stacked = jnp.concatenate([ffn_in_ref[:, at * LANES : (at + 1) * LANES] for at in range(chunks)], axis=0)
    out_ref[...] = dot(chosen_ref[...], stacked).astype(BF)


def gates_kernel(ffn_in_ref, router_ref, column_ref, parts_ref, own_ref, gates_ref, after_ref):
    after_ref[...] = residual(parts_ref, own_ref)
    block = ffn_in_ref.shape[0]
    experts = router_ref.shape[0]
    logits = dot_nt(ffn_in_ref[...], router_ref[...])
    expert_at = iota((block, experts), 1)
    for which in range(2):
        mine = expert_at == column_ref[which][:, :experts]
        picked = jnp.sum(jnp.where(mine, logits, 0.0), axis=1, keepdims=True)
        gates_ref[which] = jnp.broadcast_to(jax.nn.sigmoid(picked), (block, LANES))


def order_kernel(chunks, tokens_ref, order_ref):
    chunk_rows = order_ref.shape[0]
    each = chunk_rows // chunks
    at = iota((chunk_rows, chunk_rows), 0)
    chunk = quotient(at, each)
    rest = at - chunk * each
    source = quotient(rest, CAPACITY)
    wanted = source * (chunks * CAPACITY) + chunk * CAPACITY + rest - source * CAPACITY
    order_ref[...] = jnp.where(wanted == iota((chunk_rows, chunk_rows), 1), 1.0, 0.0).astype(BF)


def spread_kernel(tokens_ref, out_ref):
    for at in range(out_ref.shape[0]):
        out_ref[at] = tokens_ref[...]


def stack_kernel(spread_ref, *refs):
    *pieces, out_ref = refs
    for at, piece in enumerate(pieces):
        out_ref[at] = piece[...]


def hidden_of(rows, piece):
    columns = piece.shape[0] // 2
    projected = dot_nt(rows, piece)
    gate_val, up_val = projected[:, :columns], projected[:, columns:]
    return (jax.nn.gelu(gate_val, approximate=True) * up_val).astype(BF)


def own_kernel(tokens_hbm, order_ref, own_ref, down_hbm, rows_ref, hidden_ref, down_ref, tokens_ref, sems, sem):
    copies = [pltpu.make_async_copy(tokens_hbm.at[at], tokens_ref.at[at], sems.at[at]) for at in range(tokens_ref.shape[0])]
    for copy in copies:
        copy.start()
    fetch = pltpu.make_async_copy(down_hbm.at[pl.ds(0, down_ref.shape[0])], down_ref, sem)
    fetch.start()
    groups, chunk_rows, _ = tokens_ref.shape
    chunks = rows_ref.shape[1] // LANES
    each = chunk_rows // chunks
    for group in range(groups):
        copies[group].wait()
        unpacked = dot(order_ref[...], tokens_ref[group]).astype(BF)
        for at in range(chunks):
            rows_ref[group * each : (group + 1) * each, at * LANES : (at + 1) * LANES] = unpacked[
                at * each : (at + 1) * each
            ]
    for shift in range(own_ref.shape[0]):
        hidden_ref[shift] = hidden_of(rows_ref[...], own_ref[shift])
    fetch.wait()


def ffn_kernel(
    index_ref, rows_ref, order_ref, first_ref, own_hidden_ref, other_ref, down_hbm, out_ref, total_ref, other_hidden_ref,
    second_ref, sem
):
    half = second_ref.shape[0]
    fetch = pltpu.make_async_copy(down_hbm.at[pl.ds(half, half)], second_ref, sem)
    fetch.start()
    chips, both, _ = other_ref.shape
    groups, chunk_rows, _ = out_ref.shape
    width = rows_ref.shape[1]
    chunks = width // LANES
    each = chunk_rows // chunks
    core = index_ref[0] % 2
    chip = index_ref[0] // 2

    for shift in range(chips):
        other_hidden_ref[shift] = hidden_of(rows_ref[...], other_ref[shift])

    def experts_part(own_first):
        total = None
        for source in range(chips):
            shift = (chip - source + chips) % chips
            pair = [own_hidden_ref[shift], other_hidden_ref[shift]]
            hidden = jnp.concatenate(pair if own_first else pair[::-1], axis=1)
            down_ref = first_ref if source * both < half else second_ref
            start = source * both % half
            part = dot(hidden, down_ref[start : start + both, :])
            total = part if total is None else total + part
        total_ref[...] = total.astype(BF)

    fetch.wait()

    @pl.when(core == 0)
    def _():
        experts_part(True)

    @pl.when(core != 0)
    def _():
        experts_part(False)

    for group in range(groups):
        mine = total_ref[group * each : (group + 1) * each]
        stacked = jnp.concatenate([mine[:, at * LANES : (at + 1) * LANES] for at in range(chunks)], axis=0)
        out_ref[group] = dot_tn(order_ref[...], stacked).astype(BF)


def sum_kernel(parts_ref, out_ref):
    total = parts_ref[0].astype(F32)
    for at in range(1, parts_ref.shape[0]):
        total = total + parts_ref[at].astype(F32)
    out_ref[...] = total.astype(BF)


def combine_kernel(experts_ref, after_ref, gates_ref, target_ref, out_ref):
    block, width = after_ref.shape
    chunks = width // LANES
    wanted, chunk = slot_rows(experts_ref.shape[0], CAPACITY, chunks)
    same = chunk == quotient(iota(chunk.shape, 1), block)
    picked = []
    for which in range(2):
        chosen = same & (wanted == target_ref[pl.ds(which, 1), :])
        picked.append(dot_tn(jnp.where(chosen, 1.0, 0.0).astype(BF), experts_ref[...]))
    for at in range(chunks):
        lanes = slice(at * LANES, (at + 1) * LANES)
        mine = slice(at * block, (at + 1) * block)
        total = gates_ref[0] * picked[0][mine] + gates_ref[1] * picked[1][mine]
        out_ref[:, lanes] = (after_ref[:, lanes] + total).astype(BF)


VMEM = pl.BlockSpec(memory_space=pltpu.VMEM)
HBM = pl.BlockSpec(memory_space=pltpu.HBM)
SMEM = pl.BlockSpec(memory_space=pltpu.SMEM)


def in_hbm(array):
    return pltpu.with_memory_space_constraint(array, pltpu.HBM)


LONG = pl.CostEstimate(flops=10**10, transcendentals=0, bytes_accessed=1 << 21)
VERY_LONG = pl.CostEstimate(flops=2 * 10**10, transcendentals=0, bytes_accessed=1 << 21)
PARAMS = pltpu.CompilerParams(vmem_limit_bytes=16 * 1024 * 1024)


def body(
    resid, attn_gain, w_query, w_key, w_value, w_attn_out, cache, cache_lens, seg_ids, ffn_gain, router, routes, w_in, w_out
):
    hid = ("x", "c")
    hid_count = lax.axis_size(hid)
    hid_index = lax.axis_index(hid).astype(jnp.int32).reshape(1)
    group_rows, width = resid.shape
    experts = router.shape[1]
    block = group_rows // hid_count
    capacity = CAPACITY
    chunks = width // LANES
    slot_count = experts * chunks * capacity
    split = lax.axis_size("y")
    w_cols = jnp.transpose(w_in, (0, 2, 1))
    row = lax.axis_size("x")

    operands = (
        resid,
        attn_gain.reshape(1, width),
        w_query,
        w_key,
        w_value,
        w_attn_out,
        cache,
        cache_lens.reshape(1, -1),
        seg_ids,
        ffn_gain.reshape(1, width),
        router.T,
    )
    partial_mix, own, gain, router_rows = pl.pallas_call(
        attention_kernel,
        out_shape=(
            jax.ShapeDtypeStruct((group_rows, width), BF),
            jax.ShapeDtypeStruct((block, width), F32),
            jax.ShapeDtypeStruct((1, width), F32),
            jax.ShapeDtypeStruct((experts, width), BF),
        ),
        in_specs=[SMEM] + [HBM] * len(operands),
        out_specs=(VMEM,) * 4,
        scratch_shapes=[pltpu.VMEM(each.shape, each.dtype) for each in operands[:9]]
        + [pltpu.VMEM((1, group_rows), jnp.int32), pltpu.SemaphoreType.DMA((len(operands),))],
        compiler_params=PARAMS,
        name="attention",
    )(hid_index, *map(in_hbm, operands))
    chosen, target, column = pl.pallas_call(
        routing_kernel,
        out_shape=(
            jax.ShapeDtypeStruct((slot_count, LANES), BF),
            jax.ShapeDtypeStruct((2, LANES), jnp.int32),
            jax.ShapeDtypeStruct((2, block, LANES), jnp.int32),
        ),
        in_specs=[SMEM, VMEM, VMEM],
        out_specs=(VMEM,) * 3,
        compiler_params=PARAMS,
        name="routing",
    )(hid_index, routes.T, gain)
    column, w_cols = lax.optimization_barrier((column, w_cols))
    moves = [[(at, (at + shift) % row) for at in range(row)] for shift in range(row)]
    own_core = [w_cols] + [lax.ppermute(w_cols, "x", move) for move in moves[1:-1]]
    parts = lax.all_to_all(partial_mix.reshape(hid_count, block, width), hid, 0, 0, tiled=True)
    ffn_in = pl.pallas_call(
        mix_kernel,
        out_shape=jax.ShapeDtypeStruct((block, width), BF),
        in_specs=[VMEM] * 3,
        out_specs=VMEM,
        compiler_params=PARAMS,
        cost_estimate=LONG,
        name="mix",
    )(parts, own, gain)
    outgoing = pl.pallas_call(
        dispatch_kernel,
        out_shape=jax.ShapeDtypeStruct((slot_count, LANES), BF),
        in_specs=[VMEM] * 2,
        out_specs=VMEM,
        compiler_params=PARAMS,
        cost_estimate=LONG,
        name="dispatch",
    )(ffn_in, chosen)
    gates, after = pl.pallas_call(
        gates_kernel,
        out_shape=(jax.ShapeDtypeStruct((2, block, LANES), F32), jax.ShapeDtypeStruct((block, width), F32)),
        in_specs=[VMEM] * 5,
        out_specs=(VMEM,) * 2,
        compiler_params=PARAMS,
        cost_estimate=LONG,
        name="gates",
    )(ffn_in, router_rows, column, parts, own)
    exchanged = (experts, chunks * CAPACITY, LANES)
    arrived = lax.all_to_all(outgoing.reshape(exchanged), "z", 0, 0, tiled=True)
    order = pl.pallas_call(
        functools.partial(order_kernel, chunks),
        out_shape=jax.ShapeDtypeStruct((slot_count, slot_count), BF),
        in_specs=[VMEM],
        out_specs=VMEM,
        compiler_params=PARAMS,
        name="order",
    )(gates)
    order, *own_core = lax.optimization_barrier((order, *own_core))
    own_core.append(lax.ppermute(own_core[0], "x", moves[-1]))
    spread = pl.pallas_call(
        spread_kernel,
        out_shape=jax.ShapeDtypeStruct((split, slot_count, LANES), BF),
        in_specs=[VMEM],
        out_specs=VMEM,
        compiler_params=PARAMS,
        name="spread",
    )(arrived.reshape(slot_count, LANES))
    tokens = lax.all_to_all(spread, "y", 0, 0, tiled=True)
    own_core = [cols.reshape(-1, width) for cols in own_core]
    stacked = pl.pallas_call(
        stack_kernel,
        out_shape=jax.ShapeDtypeStruct((row,) + own_core[0].shape, BF),
        in_specs=[pl.BlockSpec(memory_space=pl.ANY)] + [VMEM] * row,
        out_specs=VMEM,
        compiler_params=PARAMS,
        name="stack",
    )(spread, *own_core)
    other_core = lax.ppermute(stacked, "c", [(0, 1), (1, 0)])
    rows, own_hidden, down = pl.pallas_call(
        own_kernel,
        out_shape=(
            jax.ShapeDtypeStruct((split * experts * CAPACITY, width), BF),
            jax.ShapeDtypeStruct((row, split * experts * CAPACITY, w_in.shape[2]), BF),
            jax.ShapeDtypeStruct((w_out.shape[0] // 2, width), BF),
        ),
        in_specs=[HBM, VMEM, VMEM, HBM],
        out_specs=(VMEM,) * 3,
        scratch_shapes=[pltpu.VMEM(spread.shape, BF), pltpu.SemaphoreType.DMA((split,)), pltpu.SemaphoreType.DMA],
        compiler_params=PARAMS,
        cost_estimate=VERY_LONG,
        name="own",
    )(in_hbm(tokens), order, stacked, in_hbm(w_out))
    projected = pl.pallas_call(
        ffn_kernel,
        out_shape=jax.ShapeDtypeStruct((split, slot_count, LANES), BF),
        in_specs=[SMEM] + [VMEM] * 5 + [HBM],
        out_specs=VMEM,
        scratch_shapes=[
            pltpu.VMEM((split * experts * CAPACITY, width), BF),
            pltpu.VMEM(own_hidden.shape, BF),
            pltpu.VMEM(down.shape, BF),
            pltpu.SemaphoreType.DMA,
        ],
        compiler_params=PARAMS,
        name="ffn",
    )(hid_index, rows, order, down, own_hidden, other_core, in_hbm(w_out))
    quarters = lax.all_to_all(projected, "y", 0, 0, tiled=True)
    summed = pl.pallas_call(
        sum_kernel,
        out_shape=jax.ShapeDtypeStruct((slot_count, LANES), BF),
        in_specs=[VMEM],
        out_specs=VMEM,
        compiler_params=PARAMS,
        name="sum_quarters",
    )(quarters)
    returned = lax.all_to_all(summed.reshape(exchanged), "z", 0, 0, tiled=True)
    return pl.pallas_call(
        combine_kernel,
        out_shape=jax.ShapeDtypeStruct((block, width), BF),
        in_specs=[VMEM] * 4,
        out_specs=VMEM,
        compiler_params=PARAMS,
        name="combine",
    )(returned.reshape(slot_count, LANES), after, gates, target)


def solution(mesh):
    fine = Mesh(mesh.devices.reshape(16, 4, 4, 2), ("z", "y", "x", "c"))
    req = ("z", "y")
    hid = ("x", "c")
    in_specs = (
        P(req, None),
        P(),
        P(None, hid),
        P(None, hid),
        P(None, hid),
        P(hid, None),
        P(req, None, None, hid),
        P(req),
        P(req, None),
        P(),
        P(),
        P(req, None),
        P(None, None, req + hid),
        P(req, None),
    )
    out_specs = P(req + hid, None)
    return jax.shard_map(body, mesh=fine, in_specs=in_specs, out_specs=out_specs, check_vma=False)
```

```python
import functools

import jax
import jax.numpy as jnp
from jax import lax
from jax.experimental import pallas as pl
from jax.experimental.pallas import tpu as pltpu
from jax.sharding import Mesh
from jax.sharding import PartitionSpec as P

HDIM = 64
EPS = 1e-06
BF = jnp.bfloat16
F32 = jnp.float32
LANES = 128
CAPACITY = 3


def dot(a, b):
    return jnp.dot(a, b, preferred_element_type=F32)


def dot_nt(a, b):
    return lax.dot_general(a, b, (((1,), (1,)), ((), ())), preferred_element_type=F32)


def dot_tn(a, b):
    return lax.dot_general(a, b, (((0,), (0,)), ((), ())), preferred_element_type=F32)


def iota(shape, dim):
    return lax.broadcasted_iota(jnp.int32, shape, dim)


def quotient(number, by):
    shift = (by & -by).bit_length() - 1
    odd = by >> shift
    if odd == 1:
        return number >> shift
    if odd == 3:
        return ((number >> shift) * 21846) >> 16
    return number // by


def to_column(row, size):
    diagonal = iota((size, size), 0) == iota((size, size), 1)
    return jnp.sum(jnp.where(diagonal, jnp.broadcast_to(row, (size, size)), 0), axis=1, keepdims=True)


def attention_kernel(
    index_ref, resid_hbm, gain_hbm, wq_hbm, wk_hbm, wv_hbm, wo_hbm, cache_hbm, lens_hbm, seg_hbm,
    ffn_gain_hbm, router_hbm, out_ref, own_ref, ffn_gain_ref, router_ref,
    resid_ref, gain_ref, wq_ref, wk_ref, wv_ref, wo_ref, cache_ref, lens_ref, seg_ref, seg_row, sems
):
    sources = (
        resid_hbm, gain_hbm, wq_hbm, wk_hbm, wv_hbm, seg_hbm, lens_hbm, cache_hbm, wo_hbm, ffn_gain_hbm, router_hbm
    )
    targets = (
        resid_ref, gain_ref, wq_ref, wk_ref, wv_ref, seg_ref, lens_ref, cache_ref, wo_ref, ffn_gain_ref, router_ref
    )
    copies = [pltpu.make_async_copy(a, b, sems.at[i]) for i, (a, b) in enumerate(zip(sources, targets))]
    for copy in copies:
        copy.start()
    total = resid_ref.shape[0]
    packed = seg_ref.shape[1]
    decoded, _, slots, width = cache_ref.shape
    heads = width // HDIM
    scale = HDIM ** (-0.5)
    causal = iota((total, total), 1) <= iota((total, total), 0)
    seg_row[...] = iota((1, total), 1) + (1 << 20)
    slot_at = iota((decoded, decoded * slots), 1)
    request = quotient(slot_at, slots)
    own_request = request == iota((decoded, decoded * slots), 0)
    slot_at = slot_at - request * slots
    lane_head = quotient(iota((total, width), 1), HDIM)
    copies[0].wait()
    copies[1].wait()
    x = resid_ref[...].astype(F32)
    inverse = lax.rsqrt(jnp.mean(x * x, axis=-1, keepdims=True) + EPS)
    normed = (x * inverse * gain_ref[...]).astype(BF)
    copies[2].wait()
    query = dot(normed, wq_ref[...]).astype(BF)
    copies[3].wait()
    keys = dot(normed, wk_ref[...]).astype(BF)
    copies[4].wait()
    values = dot(normed, wv_ref[...]).astype(BF)
    copies[5].wait()
    copies[6].wait()
    copies[7].wait()

    seg_row[:, :packed] = seg_ref[...]
    segments = seg_row[...]
    allowed = causal & (to_column(segments, total) == segments)
    lengths = to_column(lens_ref[...], decoded)
    own_cache = own_request & (slot_at < lengths)

    cached_keys = cache_ref[:, 0].reshape(decoded * slots, width)
    cached_values = cache_ref[:, 1].reshape(decoded * slots, width)
    context = jnp.zeros((total, width), F32)
    for head in range(heads):
        mine = lane_head == head
        head_query = jnp.where(mine, query, jnp.zeros_like(query))
        scores = jnp.where(allowed, dot_nt(head_query, keys) * scale, -jnp.inf)
        highest = jnp.max(scores, axis=-1, keepdims=True)
        cached = jnp.where(own_cache, dot_nt(head_query[packed:], cached_keys) * scale, -jnp.inf)
        top_dec = jnp.maximum(highest[packed:], jnp.max(cached, axis=-1, keepdims=True))
        highest = jnp.concatenate([highest[:packed], top_dec], axis=0)
        weights = jnp.exp(scores - highest)
        weights_cache = jnp.exp(cached - top_dec)
        norm = jnp.sum(weights, axis=-1, keepdims=True)
        norm_dec = norm[packed:] + jnp.sum(weights_cache, axis=-1, keepdims=True)
        norm = jnp.concatenate([norm[:packed], norm_dec], axis=0)
        part = dot((weights / norm).astype(BF), values)
        part_cache = dot((weights_cache / norm_dec).astype(BF), cached_values)
        part = jnp.concatenate([part[:packed], part[packed:] + part_cache], axis=0)
        context = jnp.where(mine, part, context)
    copies[8].wait()
    out_ref[...] = dot(context.astype(BF), wo_ref[...]).astype(out_ref.dtype)

    block = own_ref.shape[0]
    index = index_ref[0]
    own_ref[...] = resid_ref[pl.ds(pl.multiple_of(index * block, block), block), :].astype(F32)
    copies[9].wait()
    copies[10].wait()


def own_routes(routes_ref, which, index, block):
    lane = iota((1, LANES), 1)
    row = pltpu.roll(routes_ref[pl.ds(which, 1), :], (LANES - index * block) % LANES, 1)
    size = block
    while size < LANES:
        row = jnp.where(lane < size, row, pltpu.roll(row, size, 1))
        size *= 2
    return row


def placement(row, columns, block, capacity):
    token = iota((block, LANES), 1)
    token = token - quotient(token, block) * block
    before = iota((block, LANES), 0) < token
    slot = jnp.zeros((1, LANES), jnp.int32)
    for column in columns:
        slot = slot + jnp.sum(((column == row) & before).astype(jnp.int32), axis=0, keepdims=True)
    return row * capacity + slot


def slot_rows(rows, capacity, chunks):
    at = iota((rows, LANES), 0)
    expert = quotient(at, chunks * capacity)
    rest = at - expert * (chunks * capacity)
    chunk = quotient(rest, capacity)
    return expert * capacity + rest - chunk * capacity, chunk


def route_columns(rows, block):
    size = (block, LANES)
    diagonal = iota(size, 0) == iota(size, 1)
    return [
        jnp.sum(jnp.where(diagonal, jnp.broadcast_to(row, size), 0), axis=1, keepdims=True) for row in rows
    ]


def routing_kernel(index_ref, routes_ref, gain_ref, chosen_ref, target_ref, column_ref):
    block = column_ref.shape[1]
    chunks = gain_ref.shape[1] // LANES
    rows = [own_routes(routes_ref, which, index_ref[0], block) for which in range(2)]
    columns = route_columns(rows, block)
    wanted, chunk = slot_rows(chosen_ref.shape[0], CAPACITY, chunks)
    same = chunk == quotient(iota(chunk.shape, 1), block)
    both = None
    for which in range(2):
        target = placement(rows[which], columns, block, CAPACITY)
        here = jnp.where(same & (wanted == target), 1.0, 0.0)
        target_ref[pl.ds(which, 1), :] = target
        both = here if both is None else both + here
        column_ref[which] = jnp.broadcast_to(columns[which], (block, LANES))
    chosen_ref[...] = both.astype(BF)


def residual(parts_ref, own_ref):
    mixed = parts_ref[0].astype(F32)
    for source in range(1, parts_ref.shape[0]):
        mixed = mixed + parts_ref[source].astype(F32)
    return own_ref[...] + mixed


def mix_kernel(parts_ref, own_ref, gain_ref, ffn_in_ref):
    after = residual(parts_ref, own_ref)
    inverse = lax.rsqrt(jnp.mean(after * after, axis=-1, keepdims=True) + EPS)
    ffn_in_ref[...] = (after * inverse * gain_ref[...]).astype(BF)


def dispatch_kernel(ffn_in_ref, chosen_ref, out_ref):
    chunks = ffn_in_ref.shape[1] // LANES
    stacked = jnp.concatenate([ffn_in_ref[:, at * LANES : (at + 1) * LANES] for at in range(chunks)], axis=0)
    out_ref[...] = dot(chosen_ref[...], stacked).astype(BF)


def gates_kernel(ffn_in_ref, router_ref, column_ref, parts_ref, own_ref, gates_ref, after_ref):
    after_ref[...] = residual(parts_ref, own_ref)
    block = ffn_in_ref.shape[0]
    experts = router_ref.shape[0]
    logits = dot_nt(ffn_in_ref[...], router_ref[...])
    expert_at = iota((block, experts), 1)
    for which in range(2):
        mine = expert_at == column_ref[which][:, :experts]
        picked = jnp.sum(jnp.where(mine, logits, 0.0), axis=1, keepdims=True)
        gates_ref[which] = jnp.broadcast_to(jax.nn.sigmoid(picked), (block, LANES))


def order_kernel(chunks, tokens_ref, order_ref):
    chunk_rows = order_ref.shape[0]
    each = chunk_rows // chunks
    at = iota((chunk_rows, chunk_rows), 0)
    chunk = quotient(at, each)
    rest = at - chunk * each
    source = quotient(rest, CAPACITY)
    wanted = source * (chunks * CAPACITY) + chunk * CAPACITY + rest - source * CAPACITY
    order_ref[...] = jnp.where(wanted == iota((chunk_rows, chunk_rows), 1), 1.0, 0.0).astype(BF)


def spread_kernel(tokens_ref, out_ref):
    for at in range(out_ref.shape[0]):
        out_ref[at] = tokens_ref[...]


def stack_kernel(spread_ref, *refs):
    *pieces, out_ref = refs
    for at, piece in enumerate(pieces):
        out_ref[at] = piece[...]


def hidden_of(rows, piece):
    columns = piece.shape[0] // 2
    projected = dot_nt(rows, piece)
    gate_val, up_val = projected[:, :columns], projected[:, columns:]
    return (jax.nn.gelu(gate_val, approximate=True) * up_val).astype(BF)


def own_kernel(tokens_hbm, order_ref, own_ref, down_hbm, rows_ref, hidden_ref, down_ref, tokens_ref, sems, sem):
    copies = [pltpu.make_async_copy(tokens_hbm.at[at], tokens_ref.at[at], sems.at[at]) for at in range(tokens_ref.shape[0])]
    for copy in copies:
        copy.start()
    fetch = pltpu.make_async_copy(down_hbm.at[pl.ds(0, down_ref.shape[0])], down_ref, sem)
    fetch.start()
    groups, chunk_rows, _ = tokens_ref.shape
    chunks = rows_ref.shape[1] // LANES
    each = chunk_rows // chunks
    for group in range(groups):
        copies[group].wait()
        unpacked = dot(order_ref[...], tokens_ref[group]).astype(BF)
        for at in range(chunks):
            rows_ref[group * each : (group + 1) * each, at * LANES : (at + 1) * LANES] = unpacked[
                at * each : (at + 1) * each
            ]
    for shift in range(own_ref.shape[0]):
        hidden_ref[shift] = hidden_of(rows_ref[...], own_ref[shift])
    fetch.wait()


def ffn_kernel(
    index_ref, rows_ref, order_ref, first_ref, own_hidden_ref, other_ref, down_hbm, out_ref, total_ref, other_hidden_ref,
    second_ref, sem
):
    half = second_ref.shape[0]
    fetch = pltpu.make_async_copy(down_hbm.at[pl.ds(half, half)], second_ref, sem)
    fetch.start()
    chips, both, _ = other_ref.shape
    groups, chunk_rows, _ = out_ref.shape
    width = rows_ref.shape[1]
    chunks = width // LANES
    each = chunk_rows // chunks
    core = index_ref[0] % 2
    chip = index_ref[0] // 2

    for shift in range(chips):
        other_hidden_ref[shift] = hidden_of(rows_ref[...], other_ref[shift])

    def experts_part(own_first):
        total = None
        for source in range(chips):
            shift = (chip - source + chips) % chips
            pair = [own_hidden_ref[shift], other_hidden_ref[shift]]
            hidden = jnp.concatenate(pair if own_first else pair[::-1], axis=1)
            down_ref = first_ref if source * both < half else second_ref
            start = source * both % half
            part = dot(hidden, down_ref[start : start + both, :])
            total = part if total is None else total + part
        total_ref[...] = total.astype(BF)

    fetch.wait()

    @pl.when(core == 0)
    def _():
        experts_part(True)

    @pl.when(core != 0)
    def _():
        experts_part(False)

    for group in range(groups):
        mine = total_ref[group * each : (group + 1) * each]
        stacked = jnp.concatenate([mine[:, at * LANES : (at + 1) * LANES] for at in range(chunks)], axis=0)
        out_ref[group] = dot_tn(order_ref[...], stacked).astype(BF)


def sum_kernel(parts_ref, out_ref):
    total = parts_ref[0].astype(F32)
    for at in range(1, parts_ref.shape[0]):
        total = total + parts_ref[at].astype(F32)
    out_ref[...] = total.astype(BF)


def combine_kernel(experts_ref, after_ref, gates_ref, target_ref, out_ref):
    block, width = after_ref.shape
    chunks = width // LANES
    wanted, chunk = slot_rows(experts_ref.shape[0], CAPACITY, chunks)
    same = chunk == quotient(iota(chunk.shape, 1), block)
    picked = []
    for which in range(2):
        chosen = same & (wanted == target_ref[pl.ds(which, 1), :])
        picked.append(dot_tn(jnp.where(chosen, 1.0, 0.0).astype(BF), experts_ref[...]))
    for at in range(chunks):
        lanes = slice(at * LANES, (at + 1) * LANES)
        mine = slice(at * block, (at + 1) * block)
        total = gates_ref[0] * picked[0][mine] + gates_ref[1] * picked[1][mine]
        out_ref[:, lanes] = (after_ref[:, lanes] + total).astype(BF)


VMEM = pl.BlockSpec(memory_space=pltpu.VMEM)
HBM = pl.BlockSpec(memory_space=pltpu.HBM)
SMEM = pl.BlockSpec(memory_space=pltpu.SMEM)


def in_hbm(array):
    return pltpu.with_memory_space_constraint(array, pltpu.HBM)


LONG = pl.CostEstimate(flops=10**10, transcendentals=0, bytes_accessed=1 << 21)
VERY_LONG = pl.CostEstimate(flops=2 * 10**10, transcendentals=0, bytes_accessed=1 << 21)
PARAMS = pltpu.CompilerParams(vmem_limit_bytes=16 * 1024 * 1024)


def body(
    resid, attn_gain, w_query, w_key, w_value, w_attn_out, cache, cache_lens, seg_ids, ffn_gain, router, routes, w_in, w_out
):
    hid = ("x", "c")
    hid_count = lax.axis_size(hid)
    hid_index = lax.axis_index(hid).astype(jnp.int32).reshape(1)
    group_rows, width = resid.shape
    experts = router.shape[1]
    block = group_rows // hid_count
    capacity = CAPACITY
    chunks = width // LANES
    slot_count = experts * chunks * capacity
    split = lax.axis_size("y")
    w_cols = jnp.transpose(w_in, (0, 2, 1))
    row = lax.axis_size("x")

    operands = (
        resid,
        attn_gain.reshape(1, width),
        w_query,
        w_key,
        w_value,
        w_attn_out,
        cache,
        cache_lens.reshape(1, -1),
        seg_ids,
        ffn_gain.reshape(1, width),
        router.T,
    )
    partial_mix, own, gain, router_rows = pl.pallas_call(
        attention_kernel,
        out_shape=(
            jax.ShapeDtypeStruct((group_rows, width), BF),
            jax.ShapeDtypeStruct((block, width), F32),
            jax.ShapeDtypeStruct((1, width), F32),
            jax.ShapeDtypeStruct((experts, width), BF),
        ),
        in_specs=[SMEM] + [HBM] * len(operands),
        out_specs=(VMEM,) * 4,
        scratch_shapes=[pltpu.VMEM(each.shape, each.dtype) for each in operands[:9]]
        + [pltpu.VMEM((1, group_rows), jnp.int32), pltpu.SemaphoreType.DMA((len(operands),))],
        compiler_params=PARAMS,
        name="attention",
    )(hid_index, *map(in_hbm, operands))
    chosen, target, column = pl.pallas_call(
        routing_kernel,
        out_shape=(
            jax.ShapeDtypeStruct((slot_count, LANES), BF),
            jax.ShapeDtypeStruct((2, LANES), jnp.int32),
            jax.ShapeDtypeStruct((2, block, LANES), jnp.int32),
        ),
        in_specs=[SMEM, VMEM, VMEM],
        out_specs=(VMEM,) * 3,
        compiler_params=PARAMS,
        name="routing",
    )(hid_index, routes.T, gain)
    column, w_cols = lax.optimization_barrier((column, w_cols))
    moves = [[(at, (at + shift) % row) for at in range(row)] for shift in range(row)]
    own_core = [w_cols] + [lax.ppermute(w_cols, "x", move) for move in moves[1:-1]]
    parts = lax.all_to_all(partial_mix.reshape(hid_count, block, width), hid, 0, 0, tiled=True)
    ffn_in = pl.pallas_call(
        mix_kernel,
        out_shape=jax.ShapeDtypeStruct((block, width), BF),
        in_specs=[VMEM] * 3,
        out_specs=VMEM,
        compiler_params=PARAMS,
        cost_estimate=LONG,
        name="mix",
    )(parts, own, gain)
    outgoing = pl.pallas_call(
        dispatch_kernel,
        out_shape=jax.ShapeDtypeStruct((slot_count, LANES), BF),
        in_specs=[VMEM] * 2,
        out_specs=VMEM,
        compiler_params=PARAMS,
        cost_estimate=LONG,
        name="dispatch",
    )(ffn_in, chosen)
    gates, after = pl.pallas_call(
        gates_kernel,
        out_shape=(jax.ShapeDtypeStruct((2, block, LANES), F32), jax.ShapeDtypeStruct((block, width), F32)),
        in_specs=[VMEM] * 5,
        out_specs=(VMEM,) * 2,
        compiler_params=PARAMS,
        cost_estimate=LONG,
        name="gates",
    )(ffn_in, router_rows, column, parts, own)
    exchanged = (experts, chunks * CAPACITY, LANES)
    arrived = lax.all_to_all(outgoing.reshape(exchanged), "z", 0, 0, tiled=True)
    order = pl.pallas_call(
        functools.partial(order_kernel, chunks),
        out_shape=jax.ShapeDtypeStruct((slot_count, slot_count), BF),
        in_specs=[VMEM],
        out_specs=VMEM,
        compiler_params=PARAMS,
        name="order",
    )(gates)
    order, across, beside, w_cols = lax.optimization_barrier((order, own_core[2], own_core[1], own_core[0]))
    own_core = [w_cols, beside, across]
    own_core.append(lax.ppermute(own_core[0], "x", moves[-1]))
    spread = pl.pallas_call(
        spread_kernel,
        out_shape=jax.ShapeDtypeStruct((split, slot_count, LANES), BF),
        in_specs=[VMEM],
        out_specs=VMEM,
        compiler_params=PARAMS,
        name="spread",
    )(arrived.reshape(slot_count, LANES))
    tokens = lax.all_to_all(spread, "y", 0, 0, tiled=True)
    own_core = [cols.reshape(-1, width) for cols in own_core]
    stacked = pl.pallas_call(
        stack_kernel,
        out_shape=jax.ShapeDtypeStruct((row,) + own_core[0].shape, BF),
        in_specs=[pl.BlockSpec(memory_space=pl.ANY)] + [VMEM] * row,
        out_specs=VMEM,
        compiler_params=PARAMS,
        name="stack",
    )(spread, *own_core)
    other_core = lax.ppermute(stacked, "c", [(0, 1), (1, 0)])
    rows, own_hidden, down = pl.pallas_call(
        own_kernel,
        out_shape=(
            jax.ShapeDtypeStruct((split * experts * CAPACITY, width), BF),
            jax.ShapeDtypeStruct((row, split * experts * CAPACITY, w_in.shape[2]), BF),
            jax.ShapeDtypeStruct((w_out.shape[0] // 2, width), BF),
        ),
        in_specs=[HBM, VMEM, VMEM, HBM],
        out_specs=(VMEM,) * 3,
        scratch_shapes=[pltpu.VMEM(spread.shape, BF), pltpu.SemaphoreType.DMA((split,)), pltpu.SemaphoreType.DMA],
        compiler_params=PARAMS,
        cost_estimate=VERY_LONG,
        name="own",
    )(in_hbm(tokens), order, stacked, in_hbm(w_out))
    projected = pl.pallas_call(
        ffn_kernel,
        out_shape=jax.ShapeDtypeStruct((split, slot_count, LANES), BF),
        in_specs=[SMEM] + [VMEM] * 5 + [HBM],
        out_specs=VMEM,
        scratch_shapes=[
            pltpu.VMEM((split * experts * CAPACITY, width), BF),
            pltpu.VMEM(own_hidden.shape, BF),
            pltpu.VMEM(down.shape, BF),
            pltpu.SemaphoreType.DMA,
        ],
        compiler_params=PARAMS,
        name="ffn",
    )(hid_index, rows, order, down, own_hidden, other_core, in_hbm(w_out))
    quarters = lax.all_to_all(projected, "y", 0, 0, tiled=True)
    summed = pl.pallas_call(
        sum_kernel,
        out_shape=jax.ShapeDtypeStruct((slot_count, LANES), BF),
        in_specs=[VMEM],
        out_specs=VMEM,
        compiler_params=PARAMS,
        name="sum_quarters",
    )(quarters)
    returned = lax.all_to_all(summed.reshape(exchanged), "z", 0, 0, tiled=True)
    return pl.pallas_call(
        combine_kernel,
        out_shape=jax.ShapeDtypeStruct((block, width), BF),
        in_specs=[VMEM] * 4,
        out_specs=VMEM,
        compiler_params=PARAMS,
        name="combine",
    )(returned.reshape(slot_count, LANES), after, gates, target)


def solution(mesh):
    fine = Mesh(mesh.devices.reshape(16, 4, 4, 2), ("z", "y", "x", "c"))
    req = ("z", "y")
    hid = ("x", "c")
    in_specs = (
        P(req, None),
        P(),
        P(None, hid),
        P(None, hid),
        P(None, hid),
        P(hid, None),
        P(req, None, None, hid),
        P(req),
        P(req, None),
        P(),
        P(),
        P(req, None),
        P(None, None, req + hid),
        P(req, None),
    )
    out_specs = P(req + hid, None)
    return jax.shard_map(body, mesh=fine, in_specs=in_specs, out_specs=out_specs, check_vma=False)
```
